32 devices in a mesh: groups: 2 (over x), slab: 16 (over z, y, core).
Axes of the slice: x: 2, y: 2, z: 4, core: 2. Of those that a mesh axis runs over, the one named last changes fastest.
Arguments:
- adjoint_now: float32 [128, 320, 320], P(('groups', 'slab')), parts along dimension 0, may hold values from -6 to 6
- adjoint_prior: float32 [128, 320, 320], P(('groups', 'slab')), parts along dimension 0, may hold values from -6 to 6
- velocity_term: float32 [128, 320, 320], P(('groups', 'slab')), parts along dimension 0, may hold values from 0.04 to 0.2
- forward_field: float32 [2, 128, 320, 320], P(None, ('groups', 'slab')), parts along dimension 1, may hold values from -6 to 6
- traces: bfloat16 [2048, 2048], P(('groups', 'slab')), parts along dimension 0, may hold values from -6 to 6
- time_filter: bfloat16 [2, 2048], replicated, may hold values from -0.125 to 0.125
- slab_of_trace: int32 [2048, 1], P(('groups', 'slab')), parts along dimension 0, may hold values from 0 to 15; in each aligned block of 64 rows (0 to 63, 64 to 127, ...) at most 4 rows name the same one
- cell_index: int32 [2048], P(('groups', 'slab')), parts along dimension 0, may hold values from 0 to 409599
Outputs:
- gradient_image: float32 [128, 320, 320], P(('groups', 'slab')), parts along dimension 0
- adjoint_last: float32 [128, 320, 320], P(('groups', 'slab')), parts along dimension 0
- adjoint_before: float32 [128, 320, 320], P(('groups', 'slab')), parts along dimension 0
The draws below stay inside these ranges and needn't reach their ends.
There are 2 independent parts, one for each index of `groups`. The reference program is written for one: setup_inputs(seed, part) draws one part's arguments, and reference() takes and returns one part's arrays. A program takes and returns all parts, laid end to end along the dimension named above; an argument that names none is the same for every part. Nothing has to cross between parts.
Inputs may be any that keep to these rules, and one draw needn't show every extreme that they name: `slab_of_trace`: of one device's 64 rows at most 4 name the same slab, and in every draw some device sends exactly 4 rows to one slab.
All inputs are finite; a program needn't handle non-finite values.
Results may differ from the reference program's by a relative error of at most 0.0003.
Values may be sent and summed in bfloat16 or wider, within the bound.
No kernel may reach another device: no remote copies, remote signals or barrier semaphores. Data moves between devices by JAX's collectives and lax.ppermute only.
A program may use at most 128 MiB of HBM per device.

```python
import math
import jax
import jax.numpy as jnp
import numpy as np

CZ = 4
NX = 320
NY = 320
SAMP = 2048
TR_DEV = 64
CAP = 4
STEPS = 2
NZ = 64
REC = 1024
N_SLAB = 16


def touch_ends(values, own_key, least, largest):
    dims = values.shape
    place = [jax.random.randint(jax.random.fold_in(own_key, axis), (), 0, dims[axis]) for axis in range(len(dims))]
    values = values.at[tuple(place)].set(least)
    longest = dims.index(max(dims))
    place[longest] = (place[longest] + 1) % dims[longest]
    return values.at[tuple(place)].set(largest)


def shard_levels(key, dims, pieces, smallest, top_value):
    factor_of = 1.0
    for position, parts in pieces:
        steps = jax.random.uniform(jax.random.fold_in(jax.random.fold_in(key, 6), position), (parts,), jnp.float32, smallest / len(pieces), top_value / len(pieces))
        factor_of = factor_of * jnp.repeat(jnp.exp(steps), dims[position] // parts).reshape((-1,) + (1,) * (len(dims) - 1 - position))
    return factor_of


def deal_out(stream_key, own, number, rows, number_of, top, bound, skew):
    ranking = jax.random.permutation(stream_key, number_of)
    crowded, common = shares(number_of, rows * top, bound, skew, True), shares(number_of, rows * top, bound, skew, False)
    places = jnp.arange(number_of)

    def named(tallies, offset_by):
        used = int((tallies > 0).sum())
        fixed = max(1, used // 4)
        shifted = fixed + (places - fixed + offset_by * (used - fixed)) % max(1, number_of - fixed)
        return jnp.zeros((number_of,), jnp.int32).at[ranking[jnp.where(places < fixed, places, shifted)]].set(jnp.asarray(tallies, jnp.int32))

    tallies = jnp.where(number % 4 == 0, named(crowded, number // 4), named(common, number - number // 4 - 1))
    mixed = jax.random.permutation(jax.random.fold_in(own, 3), number_of)
    source_of, taker = mixed[0:number_of // 2 * 2:2], mixed[1:number_of // 2 * 2:2]
    margin = jnp.minimum(tallies[source_of] - 1, bound - tallies[taker]) // 2
    margin = jnp.where((source_of == ranking[0]) | (taker == ranking[0]) | (tallies[taker] == 0), 0, jnp.maximum(margin, 0))
    shifted = jax.random.randint(jax.random.fold_in(own, 4), (number_of // 2,), 0, 1 << 20) % (margin + 1)
    tallies = tallies.at[source_of].add(-shifted).at[taker].add(shifted)
    items = jnp.searchsorted(jnp.cumsum(tallies), jnp.arange(rows * top), side="right").astype(jnp.int32)
    listing = items.reshape(top, rows).T
    listing = listing[jax.random.permutation(jax.random.fold_in(own, 1), rows)]
    offset_by = jax.random.randint(jax.random.fold_in(own, 2), (rows, 1), 0, top)
    return jnp.take_along_axis(listing, (jnp.arange(top)[None, :] + offset_by) % top, axis=1)


def shares(count, total, most, slope, full):
    weights = [(1 << 20) // math.isqrt(rank ** slope) + 1 for rank in range(1, count + 1)]
    largest = most if full else min(most, max(-(-total // count), total * weights[0] // sum(weights)))
    least = 1 if total - largest >= count - 1 else 0
    holding, rest = [largest] + [least] * (count - 1), total - largest - least * (count - 1)
    while rest > 0:
        movable = [i for i in range(1, count) if holding[i] < largest] or [i for i in range(1, count) if holding[i] < most]
        whole, remaining = sum([weights[i] for i in movable]), rest
        for i in movable:
            addition = min(most - holding[i], max(1, remaining * weights[i] // whole), rest)
            holding[i] = holding[i] + addition
            rest = rest - addition
    return np.array(holding)


def normal_values(own_key, dims, spread, limit, cuts=(), kind=jnp.bfloat16):
    factor_of = shard_levels(own_key, dims, cuts, -0.22, 0.18) if cuts else 1.0
    drawn = jax.random.normal(own_key, dims, jnp.float32) * spread * factor_of
    return jnp.minimum(jnp.maximum(drawn, -limit), limit).astype(kind)


def setup_inputs(seed: int = 0, part: int = 0) -> dict:
    arg_keys = jax.random.split(jax.random.key(seed), 9)
    own_keys = jax.random.split(jax.random.fold_in(arg_keys[8], part), 9)
    adjoint_now = normal_values(own_keys[0], (NZ, NX, NY), 1.0, 6.0, ((0, 16),), jnp.float32)
    adjoint_prior = normal_values(own_keys[1], (NZ, NX, NY), 1.0, 6.0, ((0, 16),), jnp.float32)
    velocity_term = jnp.clip(0.04 + 0.16 * jax.random.uniform(own_keys[2], (NZ, NX, NY), jnp.float32) ** shard_levels(own_keys[2], (NZ, NX, NY), ((0, 16),), -0.2, 0.2), 0.04, 0.2)
    forward_field = normal_values(own_keys[3], (STEPS, NZ, NX, NY), 1.0, 6.0, ((1, 16),), jnp.float32)
    traces = normal_values(own_keys[4], (REC, SAMP), 1.0, 6.0, ((0, 16),))
    time_filter = normal_values(arg_keys[5], (STEPS, SAMP), SAMP ** -0.5, 0.125)
    slab_of_trace_keys = jax.random.split(jax.random.fold_in(own_keys[6], 1), REC // TR_DEV)
    slab_of_trace_turns = jax.random.permutation(jax.random.fold_in(own_keys[6], 3), REC // TR_DEV)
    slab_of_trace = jax.vmap(lambda own, number: deal_out(jax.random.fold_in(own_keys[6], 2), own, number, TR_DEV, N_SLAB, 1, CAP, 2))(slab_of_trace_keys, slab_of_trace_turns).reshape((REC, 1))
    cell_index = touch_ends(jax.random.randint(own_keys[7], (REC,), 0, CZ * NX * NY), jax.random.fold_in(own_keys[7], 1), 0, (CZ * NX * NY) - 1).astype(jnp.int32)
    return dict(adjoint_now=adjoint_now, adjoint_prior=adjoint_prior, velocity_term=velocity_term, forward_field=forward_field, traces=traces, time_filter=time_filter, slab_of_trace=slab_of_trace, cell_index=cell_index)


STENCIL_WEIGHTS = (-205.0 / 72.0, 8.0 / 5.0, -1.0 / 5.0, 8.0 / 315.0, -1.0 / 560.0)


def laplace(extended):
    widened = jnp.pad(extended, ((0, 0), (4, 4), (4, 4)))
    inner = extended.shape[0] - 8
    width_x = extended.shape[1]
    width_y = extended.shape[2]
    centre = widened[4:4 + inner, 4:4 + width_x, 4:4 + width_y]
    summed = 3.0 * STENCIL_WEIGHTS[0] * centre
    for offset in range(1, 5):
        pair = widened[4 + offset:4 + offset + inner, 4:4 + width_x, 4:4 + width_y]
        pair = pair + widened[4 - offset:4 - offset + inner, 4:4 + width_x, 4:4 + width_y]
        pair = pair + widened[4:4 + inner, 4 + offset:4 + offset + width_x, 4:4 + width_y]
        pair = pair + widened[4:4 + inner, 4 - offset:4 - offset + width_x, 4:4 + width_y]
        pair = pair + widened[4:4 + inner, 4:4 + width_x, 4 + offset:4 + offset + width_y]
        pair = pair + widened[4:4 + inner, 4:4 + width_x, 4 - offset:4 - offset + width_y]
        summed = summed + STENCIL_WEIGHTS[offset] * pair
    return summed


def reference(adjoint_now, adjoint_prior, velocity_term, forward_field, traces, time_filter, slab_of_trace, cell_index):
    sources = jnp.dot(traces, time_filter.T, preferred_element_type=jnp.float32)
    flat_target = (slab_of_trace[:, 0] * (CZ * NX * NY) + cell_index).astype(jnp.int32)
    current = adjoint_now
    previous = adjoint_prior
    image_sum = jnp.zeros(adjoint_now.shape, jnp.float32)
    for section_index in range(STEPS):
        inject = jnp.zeros((NZ * NX * NY,), jnp.float32).at[flat_target].add(sources[:, section_index])
        inject = inject.reshape(NZ, NX, NY)
        extended = jnp.pad(current, ((4, 4), (0, 0), (0, 0)))
        advanced = 2.0 * current - previous + velocity_term * (laplace(extended) + inject)
        image_sum = image_sum + forward_field[section_index] * advanced
        previous = current
        current = advanced
    return (image_sum, current, previous)
```

```python
import functools

import jax
import jax.numpy as jnp
from jax import lax
from jax.experimental import pallas as pl
from jax.experimental.pallas import tpu as pltpu
from jax.sharding import PartitionSpec as P

CAP = 4
STEPS = 2
W = (-205.0 / 72.0, 8.0 / 5.0, -1.0 / 5.0, 8.0 / 315.0, -1.0 / 560.0)
HALO = 4
ROWS = 16
LANES = 128
F32 = jnp.float32
BF16 = jnp.bfloat16
VMEM = pl.BlockSpec(memory_space=pltpu.VMEM)
SMEM = pl.BlockSpec(memory_space=pltpu.SMEM)


def params():
    return pltpu.CompilerParams(vmem_limit_bytes=24 << 20)


def payload_lanes(width):
    full = width // LANES * LANES
    rest = width - full
    if rest == 0:
        return HALO * full
    return HALO * full + (2 * LANES if rest * 2 <= LANES else HALO * LANES)


def depth_at(j, depth):
    odd = lax.rem(lax.axis_index("slab"), 2)
    return j + (1 - odd) * (depth - 1 - 2 * j)


def encode(u):
    t1 = u[0].astype(BF16).astype(F32)
    e1 = u[0] - t1
    t2 = (u[1] + (W[2] / W[3]) * e1).astype(BF16).astype(F32)
    t3 = u[2].astype(BF16).astype(F32)
    t0 = W[1] * e1 + W[2] * (u[1] - t2) + W[3] * (u[2] - t3) + W[4] * u[3]
    return (t0, t1, t2, t3)


def decode(t):
    t0, t1, t2, t3 = t
    return (
        t0 + W[1] * t1 + W[2] * t2 + W[3] * t3,
        W[2] * t1 + W[3] * t2 + W[4] * t3,
        W[3] * t1 + W[4] * t2,
        W[4] * t1,
    )


def put(ref, rows, t):
    width = t[0].shape[1]
    full = width // LANES * LANES
    rest = width - full
    for k in range(HALO):
        ref[rows, k * full : (k + 1) * full] = t[k][:, :full].astype(BF16)
    if rest == 0:
        return
    base = HALO * full
    if rest * 2 <= LANES:
        half = LANES // 2
        for k in range(0, HALO, 2):
            a = jnp.pad(t[k][:, full:], ((0, 0), (0, half - rest)))
            b = jnp.pad(t[k + 1][:, full:], ((0, 0), (0, half - rest)))
            ref[rows, base : base + LANES] = jnp.concatenate([a, b], axis=1).astype(BF16)
            base += LANES
    else:
        for k in range(HALO):
            tail = jnp.pad(t[k][:, full:], ((0, 0), (0, LANES - rest)))
            ref[rows, base : base + LANES] = tail.astype(BF16)
            base += LANES


def take(ref, rows, width):
    full = width // LANES * LANES
    rest = width - full
    main = [ref[rows, k * full : (k + 1) * full].astype(F32) for k in range(HALO)]
    if rest == 0:
        return main
    base = HALO * full
    tails = []
    if rest * 2 <= LANES:
        half = LANES // 2
        for k in range(0, HALO, 2):
            both = ref[rows, base : base + LANES].astype(F32)
            tails.append(both[:, :rest])
            tails.append(pltpu.roll(both, half, 1)[:, :rest])
            base += LANES
    else:
        for k in range(HALO):
            tails.append(ref[rows, base : base + LANES].astype(F32)[:, :rest])
            base += LANES
    return [jnp.concatenate([m, t], axis=1) for m, t in zip(main, tails)]


def row_loop(count, body):
    def step(i, carry):
        body(pl.multiple_of(i * ROWS, ROWS))
        return carry

    lax.fori_loop(0, count // ROWS, step, 0)


def pack_kernel(now, on_ref, off_ref):
    depth, width_x, _ = now.shape

    def body(r):
        rows = pl.ds(r, ROWS)
        u = [now[depth_at(j, depth), rows, :] for j in range(depth)]
        put(off_ref, rows, encode(u[::-1][:HALO]))
        put(on_ref, rows, encode(u[:HALO]))

    row_loop(width_x, body)


def route_kernel(slabs, width_y, traces, weights, target, cell, out):
    rows = traces.shape[0]
    lane = lax.broadcasted_iota(jnp.int32, (rows, rows), 1)
    row = lax.broadcasted_iota(jnp.int32, (rows, rows), 0)
    eye = lane == row
    target_row = jnp.broadcast_to(target[...], (rows, rows))
    cell_row = jnp.broadcast_to(cell[...], (rows, rows))
    target_col = jnp.sum(jnp.where(eye, target_row, 0), axis=1, keepdims=True)
    cell_col = jnp.sum(jnp.where(eye, cell_row, 0), axis=1, keepdims=True)
    same = (target_row == target_col) & (lane < row)
    rank = jnp.sum(jnp.where(same, 1, 0), axis=1, keepdims=True)
    values = traces[...].astype(F32)
    columns = [
        jnp.sum(values * weights[s : s + 1, :].astype(F32), axis=1, keepdims=True)
        for s in range(STEPS)
    ]
    cell_line = cell_col // width_y
    columns.append(cell_line.astype(F32))
    columns.append((cell_col - cell_line * width_y).astype(F32))
    spot = lax.broadcasted_iota(jnp.int32, (rows, LANES), 1)
    spread = jnp.zeros((rows, LANES), F32)
    for j, column in enumerate(columns):
        spread = jnp.where(spot == j * CAP + rank, column, spread)
    taker = lax.broadcasted_iota(jnp.int32, (slabs, rows), 0)
    chosen = (taker == jnp.broadcast_to(target[...], (slabs, rows))).astype(F32)
    picked = jnp.dot(
        chosen, spread, precision=lax.Precision.HIGHEST, preferred_element_type=F32
    )
    out[...] = picked.reshape(out.shape)


def fill(pad, source):
    depth, width_x, width_y = source.shape
    lanes = pad.shape[2]
    for z in range(depth):
        pad[z, 0:8, :] = jnp.zeros((8, lanes), F32)
        pad[z, 8 + width_x : 16 + width_x, :] = jnp.zeros((8, lanes), F32)

    def body(r):
        for z in range(depth):
            value = source[z, pl.ds(r, ROWS), :]
            pad[z, pl.ds(r + 8, ROWS), :] = jnp.pad(value, ((0, 0), (0, lanes - width_y)))

    row_loop(width_x, body)


def own_laplace(pad, r):
    depth = pad.shape[0]
    span = ROWS + 16
    blocks = [pad[z, pl.ds(r, span), :] for z in range(depth)]
    centre = [block[8 : 8 + ROWS, :] for block in blocks]
    lanes = pad.shape[2]
    out = []
    for z in range(depth):
        total = 3.0 * W[0] * centre[z]
        for k in range(1, HALO + 1):
            pair = pltpu.roll(blocks[z], k, 0)[8 : 8 + ROWS, :]
            pair = pair + pltpu.roll(blocks[z], span - k, 0)[8 : 8 + ROWS, :]
            pair = pair + pltpu.roll(centre[z], k, 1) + pltpu.roll(centre[z], lanes - k, 1)
            if z - k >= 0:
                pair = pair + centre[z - k]
            if z + k < depth:
                pair = pair + centre[z + k]
            total = total + W[k] * pair
        out.append(total)
    return centre, out


def inject(step, got, velocity, grid):
    depth, width_x, width_y = grid.shape
    lane = lax.broadcasted_iota(jnp.int32, (1, width_y), 1)

    def body(i, carry):
        for slot in range(CAP):
            source = got[i, 0, step * CAP + slot]
            line = got[i, 0, STEPS * CAP + slot].astype(jnp.int32)
            column = got[i, 0, (STEPS + 1) * CAP + slot].astype(jnp.int32)
            z = lax.div(line, jnp.int32(width_x))
            row = pl.ds(line - z * width_x, 1)
            extra = jnp.where(lane == column, velocity[z, row, :] * source, 0.0)
            grid[z, row, :] = grid[z, row, :] + extra
        return carry

    lax.fori_loop(0, got.shape[0], body, 0)


def own_kernel(now, prior, velocity, out, pad):
    depth, width_x, width_y = now.shape
    fill(pad, now)

    def body(r):
        rows = pl.ds(r, ROWS)
        centre, lap = own_laplace(pad, r)
        for z in range(depth):
            c, l = centre[z][:, :width_y], lap[z][:, :width_y]
            out[z, rows, :] = 2.0 * c - prior[z, rows, :] + velocity[z, rows, :] * l

    row_loop(width_x, body)


def inject_kernel(step, got, velocity, grid_in, out):
    del grid_in
    inject(step, got, velocity, out)


def halo_sum(got_on, got_off, rows, width_y, depth):
    near = decode(take(got_on, rows, width_y))
    far = decode(take(got_off, rows, width_y))
    out = []
    for j in range(depth):
        terms = [near[j]] if j < HALO else []
        if depth - 1 - j < HALO:
            terms.append(far[depth - 1 - j])
        out.append(functools.reduce(lambda a, b: a + b, terms) if terms else None)
    return out


def close_kernel(partial, velocity, got_on, got_off, out, on_ref, off_ref):
    depth, width_x, width_y = out.shape

    def body(r):
        rows = pl.ds(r, ROWS)
        halo = halo_sum(got_on, got_off, rows, width_y, depth)
        u = []
        for j in range(depth):
            z = depth_at(j, depth)
            value = partial[z, rows, :]
            if halo[j] is not None:
                value = value + velocity[z, rows, :] * halo[j]
            out[z, rows, :] = value
            u.append(value)
        put(off_ref, rows, encode(u[::-1][:HALO]))
        put(on_ref, rows, encode(u[:HALO]))

    row_loop(width_x, body)


def second_kernel(got, current, previous, velocity, forward, out, image, pad):
    depth, width_x, width_y = current.shape
    fill(pad, current)

    def body(r):
        rows = pl.ds(r, ROWS)
        centre, lap = own_laplace(pad, r)
        for z in range(depth):
            c, l = centre[z][:, :width_y], lap[z][:, :width_y]
            out[z, rows, :] = 2.0 * c - previous[z, rows, :] + velocity[z, rows, :] * l

    row_loop(width_x, body)
    inject(1, got, velocity, out)

    def body_image(r):
        rows = pl.ds(r, ROWS)
        for z in range(depth):
            image[z, rows, :] = (
                forward[0, z, rows, :] * current[z, rows, :]
                + forward[1, z, rows, :] * out[z, rows, :]
            )

    row_loop(width_x, body_image)


def last_kernel(partial, image_in, velocity, forward, got_on, got_off, out, image):
    depth, width_x, width_y = out.shape

    def body(r):
        rows = pl.ds(r, ROWS)
        halo = halo_sum(got_on, got_off, rows, width_y, depth)
        for j in range(depth):
            z = depth_at(j, depth)
            extra = velocity[z, rows, :] * halo[j] if halo[j] is not None else 0.0
            out[z, rows, :] = partial[z, rows, :] + extra
            image[z, rows, :] = image_in[z, rows, :] + forward[1, z, rows, :] * extra

    row_loop(width_x, body)


def on_device(now, prior, velocity, forward, traces, weights, target, cell):
    slabs = lax.axis_size("slab")
    depth, width_x, width_y = now.shape
    rows = traces.shape[0]
    lanes = -(-(width_y + HALO) // LANES) * LANES
    field = jax.ShapeDtypeStruct(now.shape, F32)
    face = jax.ShapeDtypeStruct((width_x, payload_lanes(width_y)), BF16)
    pad = pltpu.VMEM((depth, width_x + 16, lanes), F32)
    on_pairs = [(i, j) for i, j in ((k, k ^ 1) for k in range(slabs)) if j < slabs]
    off_pairs = [(i + 1, j + 1) for i, j in ((k, k ^ 1) for k in range(slabs)) if i + 1 < slabs and j + 1 < slabs]

    def call(kernel, ins, outs, scratch=(), **kw):
        return pl.pallas_call(
            kernel,
            in_specs=ins,
            out_specs=[VMEM] * len(outs),
            out_shape=outs,
            scratch_shapes=scratch,
            compiler_params=params(),
            **kw,
        )

    def swap(on_face, off_face):
        off = lax.ppermute(off_face, "slab", off_pairs)
        on = lax.ppermute(on_face, "slab", on_pairs)
        return on, off

    on_face, off_face = call(pack_kernel, [VMEM], [face, face])(now)
    (sent,) = call(
        functools.partial(route_kernel, slabs, width_y),
        [VMEM] * 4,
        [jax.ShapeDtypeStruct((slabs, 1, LANES), F32)],
    )(traces, weights, target.reshape(1, rows), cell.reshape(1, rows))
    got_on, got_off = swap(on_face, off_face)
    got = lax.all_to_all(sent, "slab", split_axis=0, concat_axis=0, tiled=True)
    (partial,) = call(own_kernel, [VMEM] * 3, [field], (pad,))(now, prior, velocity)
    (partial,) = call(
        functools.partial(inject_kernel, 0),
        [SMEM, VMEM, VMEM],
        [field],
        input_output_aliases={2: 0},
    )(got, velocity, partial)
    first, on_face, off_face = call(close_kernel, [VMEM] * 4, [field, face, face])(
        partial, velocity, got_on, got_off
    )
    got_on, got_off = swap(on_face, off_face)
    partial, image = call(second_kernel, [SMEM] + [VMEM] * 4, [field, field], (pad,))(
        got, first, now, velocity, forward
    )
    second, image = call(last_kernel, [VMEM] * 6, [field, field])(
        partial, image, velocity, forward, got_on, got_off
    )
    return (image, second, first)


def solution(mesh):
    split = P(("groups", "slab"), None, None)
    return jax.shard_map(
        on_device,
        mesh=mesh,
        in_specs=(
            split,
            split,
            split,
            P(None, ("groups", "slab"), None, None),
            P(("groups", "slab"), None),
            P(),
            P(("groups", "slab"), None),
            P(("groups", "slab")),
        ),
        out_specs=(split, split, split),
        check_vma=False,
    )
```

```python
import functools

import jax
import jax.numpy as jnp
from jax import lax
from jax.experimental import pallas as pl
from jax.experimental.pallas import tpu as pltpu
from jax.sharding import PartitionSpec as P


CAP = 4
STEPS = 2
W = (-205.0 / 72.0, 8.0 / 5.0, -1.0 / 5.0, 8.0 / 315.0, -1.0 / 560.0)
HALO = 4
ROWS = 16
BLOCK = 32
LANES = 128
F32 = jnp.float32
BF16 = jnp.bfloat16
VMEM = pl.BlockSpec(memory_space=pltpu.VMEM)
SMEM = pl.BlockSpec(memory_space=pltpu.SMEM)
HBM = pl.BlockSpec(memory_space=pltpu.HBM)


def params():
    return pltpu.CompilerParams(vmem_limit_bytes=12 << 20)


def payload_lanes(width):
    full = width // LANES * LANES
    rest = width - full
    if rest == 0:
        return HALO * full
    return HALO * full + (2 * LANES if rest * 2 <= LANES else HALO * LANES)


def depth_at(j, depth):
    odd = lax.rem(lax.axis_index("slab"), 2)
    return j + (1 - odd) * (depth - 1 - 2 * j)


def encode(u):
    t1 = u[0].astype(BF16).astype(F32)
    e1 = u[0] - t1
    t2 = (u[1] + (W[2] / W[3]) * e1).astype(BF16).astype(F32)
    t3 = u[2].astype(BF16).astype(F32)
    t0 = W[1] * e1 + W[2] * (u[1] - t2) + W[3] * (u[2] - t3) + W[4] * u[3]
    return (t0, t1, t2, t3)


def decode(t):
    t0, t1, t2, t3 = t
    return (
        t0 + W[1] * t1 + W[2] * t2 + W[3] * t3,
        W[2] * t1 + W[3] * t2 + W[4] * t3,
        W[3] * t1 + W[4] * t2,
        W[4] * t1,
    )


def put(ref, rows, t):
    width = t[0].shape[1]
    full = width // LANES * LANES
    rest = width - full
    for k in range(HALO):
        ref[rows, k * full : (k + 1) * full] = t[k][:, :full].astype(BF16)
    if rest == 0:
        return
    base = HALO * full
    if rest * 2 <= LANES:
        half = LANES // 2
        for k in range(0, HALO, 2):
            a = jnp.pad(t[k][:, full:], ((0, 0), (0, half - rest)))
            b = jnp.pad(t[k + 1][:, full:], ((0, 0), (0, half - rest)))
            ref[rows, base : base + LANES] = jnp.concatenate([a, b], axis=1).astype(BF16)
            base += LANES
    else:
        for k in range(HALO):
            tail = jnp.pad(t[k][:, full:], ((0, 0), (0, LANES - rest)))
            ref[rows, base : base + LANES] = tail.astype(BF16)
            base += LANES


def take(ref, rows, width):
    full = width // LANES * LANES
    rest = width - full
    main = [ref[rows, k * full : (k + 1) * full].astype(F32) for k in range(HALO)]
    if rest == 0:
        return main
    base = HALO * full
    tails = []
    if rest * 2 <= LANES:
        half = LANES // 2
        for _ in range(0, HALO, 2):
            both = ref[rows, base : base + LANES].astype(F32)
            tails.append(both[:, :rest])
            tails.append(pltpu.roll(both, half, 1)[:, :rest])
            base += LANES
    else:
        for _ in range(HALO):
            tails.append(ref[rows, base : base + LANES].astype(F32)[:, :rest])
            base += LANES
    return [jnp.concatenate([m, t], axis=1) for m, t in zip(main, tails)]


def row_loop(count, body):
    def step(i, carry):
        body(pl.multiple_of(i * ROWS, ROWS))
        return carry

    lax.fori_loop(0, count // ROWS, step, 0)


def fetch(source, buf, sems, first, count):
    copies = []
    for i in range(0, count, BLOCK):
        rows = pl.ds(first + i, BLOCK)
        copies.append(
            pltpu.make_async_copy(source.at[:, rows], buf.at[:, pl.ds(i, BLOCK)], sems.at[i // BLOCK])
        )
        copies[-1].start()
    return copies


def pack_kernel(first, with_on, now, *refs):
    refs = list(refs)
    on_ref = refs.pop(0) if with_on else None
    off_ref, buf, sems = refs
    depth = now.shape[0]
    base = 0 if with_on else first
    copies = fetch(now, buf, sems, base, buf.shape[1])

    for i, copy in enumerate(copies):
        copy.wait()

        def body(r):
            r = r + i * BLOCK
            rows = pl.ds(r, ROWS)
            u = [buf[depth_at(j, depth), rows, :] for j in range(depth)]
            if base + i * BLOCK >= first and base + i * BLOCK < first + off_ref.shape[0]:
                put(off_ref, pl.ds(r + base - first, ROWS), encode(u[::-1][:HALO]))
            if with_on:
                put(on_ref, rows, encode(u[:HALO]))

        row_loop(BLOCK, body)


def route_kernel(slabs, width_y, traces, weights, target, cell, out):
    rows = traces.shape[0]
    lane = lax.broadcasted_iota(jnp.int32, (rows, rows), 1)
    row = lax.broadcasted_iota(jnp.int32, (rows, rows), 0)
    eye = lane == row
    target_row = jnp.broadcast_to(target[...], (rows, rows))
    cell_row = jnp.broadcast_to(cell[...], (rows, rows))
    target_col = jnp.sum(jnp.where(eye, target_row, 0), axis=1, keepdims=True)
    cell_col = jnp.sum(jnp.where(eye, cell_row, 0), axis=1, keepdims=True)
    same = (target_row == target_col) & (lane < row)
    rank = jnp.sum(jnp.where(same, 1, 0), axis=1, keepdims=True)
    values = traces[...].astype(F32)
    columns = [
        jnp.sum(values * weights[s : s + 1, :].astype(F32), axis=1, keepdims=True)
        for s in range(STEPS)
    ]
    cell_line = cell_col // width_y
    columns.append(cell_line.astype(F32))
    columns.append((cell_col - cell_line * width_y).astype(F32))
    spot = lax.broadcasted_iota(jnp.int32, (rows, LANES), 1)
    spread = jnp.zeros((rows, LANES), F32)
    for j, column in enumerate(columns):
        spread = jnp.where(spot == j * CAP + rank, column, spread)
    taker = lax.broadcasted_iota(jnp.int32, (slabs, rows), 0)
    chosen = (taker == jnp.broadcast_to(target[...], (slabs, rows))).astype(F32)
    picked = jnp.dot(
        chosen, spread, precision=lax.Precision.HIGHEST, preferred_element_type=F32
    )
    out[...] = picked.reshape(out.shape)


def clear(pad, width_x):
    depth, _, lanes = pad.shape
    for z in range(depth):
        pad[z, 0:8, :] = jnp.zeros((8, lanes), F32)
        pad[z, 8 + width_x : 16 + width_x, :] = jnp.zeros((8, lanes), F32)


def fill(pad, first, source, start, count):
    depth, _, width_y = source.shape
    lanes = pad.shape[2]

    def body(r):
        for z in range(depth):
            value = source[z, pl.ds(r + start, ROWS), :]
            value = jnp.pad(value, ((0, 0), (0, lanes - width_y)))
            pad[z, pl.ds(r + (first + 8), ROWS), :] = value

    row_loop(count, body)


def own_laplace(pad, r):
    depth = pad.shape[0]
    span = ROWS + 16
    blocks = [pad[z, pl.ds(r, span), :] for z in range(depth)]
    centre = [block[8 : 8 + ROWS, :] for block in blocks]
    lanes = pad.shape[2]
    out = []
    for z in range(depth):
        total = 3.0 * W[0] * centre[z]
        for k in range(1, HALO + 1):
            pair = pltpu.roll(blocks[z], k, 0)[8 : 8 + ROWS, :]
            pair = pair + pltpu.roll(blocks[z], span - k, 0)[8 : 8 + ROWS, :]
            pair = pair + pltpu.roll(centre[z], k, 1) + pltpu.roll(centre[z], lanes - k, 1)
            if z - k >= 0:
                pair = pair + centre[z - k]
            if z + k < depth:
                pair = pair + centre[z + k]
            total = total + W[k] * pair
        out.append(total)
    return centre, out


def inject(step, got, velocity, grid):
    _, width_x, width_y = grid.shape
    lane = lax.broadcasted_iota(jnp.int32, (1, width_y), 1)

    def body(i, carry):
        for slot in range(CAP):
            source = got[i, 0, step * CAP + slot]
            line = got[i, 0, STEPS * CAP + slot].astype(jnp.int32)
            column = got[i, 0, (STEPS + 1) * CAP + slot].astype(jnp.int32)
            z = lax.div(line, jnp.int32(width_x))
            row = pl.ds(line - z * width_x, 1)
            extra = jnp.where(lane == column, velocity[z, row, :] * source, 0.0)
            grid[z, row, :] = grid[z, row, :] + extra
        return carry

    lax.fori_loop(0, got.shape[0], body, 0)


def own_kernel(now, prior, velocity, got, out, pad, now_buf, prior_buf, sems):
    depth, width_x, width_y = now.shape
    now_copies = fetch(now, now_buf, sems.at[0], 0, width_x)
    prior_copies = fetch(prior, prior_buf, sems.at[1], 0, width_x)
    clear(pad, width_x)
    for i, copy in enumerate(now_copies):
        copy.wait()
        fill(pad, i * BLOCK, now_buf, i * BLOCK, BLOCK)
    for copy in prior_copies:
        copy.wait()

    def body(r):
        rows = pl.ds(r, ROWS)
        centre, lap = own_laplace(pad, r)
        for z in range(depth):
            c, l = centre[z][:, :width_y], lap[z][:, :width_y]
            out[z, rows, :] = 2.0 * c - prior_buf[z, rows, :] + velocity[z, rows, :] * l

    row_loop(width_x, body)
    inject(0, got, velocity, out)


def halo_sum(got_on, rows_on, got_off, rows_off, width_y, depth):
    near = decode(take(got_on, rows_on, width_y))
    far = decode(take(got_off, rows_off, width_y))
    out = []
    for j in range(depth):
        terms = [near[j]] if j < HALO else []
        if depth - 1 - j < HALO:
            terms.append(far[depth - 1 - j])
        out.append(functools.reduce(lambda a, b: a + b, terms) if terms else None)
    return out


def close_kernel(first, partial, velocity, got_on, got_off, out, on_ref, off_ref):
    depth, count, width_y = out.shape

    def body(r):
        rows = pl.ds(r, ROWS)
        whole = pl.ds(r + first, ROWS)
        halo = halo_sum(got_on, whole, got_off, rows, width_y, depth)
        u = []
        for j in range(depth):
            z = depth_at(j, depth)
            value = partial[z, whole, :]
            if halo[j] is not None:
                value = value + velocity[z, whole, :] * halo[j]
            out[z, rows, :] = value
            u.append(value)
        put(off_ref, rows, encode(u[::-1][:HALO]))
        put(on_ref, rows, encode(u[:HALO]))

    row_loop(count, body)


def second_kernel(starts, *refs):
    parts, refs = refs[: len(starts)], refs[len(starts) :]
    now, velocity, forward, got, out, image, current, pad, now_buf, sems, out_sems = refs
    depth, width_x, width_y = now.shape
    copies = fetch(now, now_buf, sems, 0, width_x)
    writes = []
    for i, (first, part) in enumerate(zip(starts, parts)):
        write = pltpu.make_async_copy(
            part, current.at[:, pl.ds(first, part.shape[1])], out_sems.at[i]
        )
        write.start()
        writes.append(write)
    clear(pad, width_x)
    for first, part in zip(starts, parts):
        fill(pad, first, part, 0, part.shape[1])
    for copy in copies:
        copy.wait()

    def body(r):
        rows = pl.ds(r, ROWS)
        centre, lap = own_laplace(pad, r)
        for z in range(depth):
            c, l = centre[z][:, :width_y], lap[z][:, :width_y]
            out[z, rows, :] = 2.0 * c - now_buf[z, rows, :] + velocity[z, rows, :] * l

    row_loop(width_x, body)
    inject(1, got, velocity, out)

    def body_image(r):
        rows = pl.ds(r, ROWS)
        for z in range(depth):
            image[z, rows, :] = (
                forward[0, z, rows, :] * pad[z, pl.ds(r + 8, ROWS), :][:, :width_y]
                + forward[1, z, rows, :] * out[z, rows, :]
            )

    row_loop(width_x, body_image)
    for write in writes:
        write.wait()


def last_kernel(first, count, partial, image_in, velocity, forward, got_on, got_off, *refs):
    out, image, out_buf, image_buf, sems = refs[-5:]
    depth, width_y = out.shape[0], out.shape[2]
    writes = []
    for i in range(0, count, BLOCK):

        def body(r):
            rows = pl.ds(r + i, ROWS)
            whole = pl.ds(r + (first + i), ROWS)
            halo = halo_sum(got_on, rows, got_off, rows, width_y, depth)
            for j in range(depth):
                z = depth_at(j, depth)
                extra = velocity[z, whole, :] * halo[j] if halo[j] is not None else 0.0
                out_buf[z, rows, :] = partial[z, whole, :] + extra
                image_buf[z, rows, :] = image_in[z, whole, :] + forward[1, z, whole, :] * extra

        row_loop(BLOCK, body)
        for k, (buf, target) in enumerate(((out_buf, out), (image_buf, image))):
            write = pltpu.make_async_copy(
                buf.at[:, pl.ds(i, BLOCK)],
                target.at[:, pl.ds(first + i, BLOCK)],
                sems.at[k, i // BLOCK],
            )
            write.start()
            writes.append(write)
    for write in writes:
        write.wait()


def shard(now, prior, velocity, forward, traces, weights, target, cell):
    slabs = lax.axis_size("slab")
    depth, width_x, width_y = now.shape
    rows = traces.shape[0]
    lanes = -(-(width_y + HALO) // LANES) * LANES
    face_lanes = payload_lanes(width_y)
    half = width_x // (2 * BLOCK) * BLOCK
    chunks = ((0, half), (half, width_x - half))
    starts = tuple(first for first, _ in chunks)
    blocks = width_x // BLOCK
    field = jax.ShapeDtypeStruct(now.shape, F32)
    pad = pltpu.VMEM((depth, width_x + 16, lanes), F32)
    dma = pltpu.SemaphoreType.DMA
    on_pairs = [(k, k ^ 1) for k in range(slabs) if k ^ 1 < slabs]
    off_pairs = [(i + 1, j + 1) for i, j in on_pairs if i + 1 < slabs and j + 1 < slabs]

    def plane(count):
        return jax.ShapeDtypeStruct((count, face_lanes), BF16)

    def buffer(count):
        return pltpu.VMEM((depth, count, width_y), F32)

    def call(kernel, ins, outs, scratch=(), out_spec=None, **kw):
        return pl.pallas_call(
            kernel,
            in_specs=ins,
            out_specs=out_spec or [VMEM] * len(outs),
            out_shape=outs,
            scratch_shapes=scratch,
            compiler_params=params(),
            **kw,
        )

    def swap(face, pairs):
        return lax.ppermute(face, "slab", pairs)

    got_off = []
    (face,) = call(
        functools.partial(pack_kernel, 0, False),
        [HBM],
        [plane(half)],
        (buffer(half), dma((half // BLOCK,))),
    )(now)
    got_off.append(swap(face, off_pairs))
    face, traces = lax.optimization_barrier((face, traces))
    (sent,) = call(
        functools.partial(route_kernel, slabs, width_y),
        [VMEM] * 4,
        [jax.ShapeDtypeStruct((slabs, 1, LANES), F32)],
    )(traces, weights, target.reshape(1, rows), cell.reshape(1, rows))
    got = lax.all_to_all(sent, "slab", split_axis=0, concat_axis=0, tiled=True)
    sent, later = lax.optimization_barrier((sent, now))
    on_face, face = call(
        functools.partial(pack_kernel, half, True),
        [HBM],
        [plane(width_x), plane(width_x - half)],
        (buffer(width_x), dma((blocks,))),
    )(later)
    got_off.append(swap(face, off_pairs))
    got_on = swap(on_face, on_pairs)
    (partial,) = call(
        own_kernel,
        [HBM, HBM, VMEM, SMEM],
        [field],
        (pad, buffer(width_x), buffer(width_x), dma((2, blocks))),
    )(now, prior, velocity, got)
    parts, second_on, second_off = [], [], []
    for (first, count), got_face in zip(chunks, got_off):
        part, on_face, face = call(
            functools.partial(close_kernel, first),
            [VMEM] * 4,
            [jax.ShapeDtypeStruct((depth, count, width_y), F32), plane(count), plane(count)],
        )(partial, velocity, got_on, got_face)
        second_off.append(swap(face, off_pairs))
        second_on.append(swap(on_face, on_pairs))
        parts.append(part)
        part, partial = lax.optimization_barrier((part, partial))
    partial, image, current = call(
        functools.partial(second_kernel, starts),
        [VMEM] * len(parts) + [HBM, VMEM, VMEM, SMEM],
        [field, field, field],
        (pad, buffer(width_x), dma((blocks,)), dma((len(parts),))),
        [VMEM, VMEM, HBM],
    )(*parts, now, velocity, forward, got)
    done = ()
    for i, (first, count) in enumerate(chunks):
        done = call(
            functools.partial(last_kernel, first, count),
            [VMEM] * 6 + [HBM] * len(done),
            [field, field],
            (buffer(count), buffer(count), dma((2, count // BLOCK))),
            [HBM, HBM],
            input_output_aliases={6: 0, 7: 1} if done else {},
        )(partial, image, velocity, forward, second_on[i], second_off[i], *done)
    second, image = done
    return (image, second, current)


def solution(mesh):
    split = P(("groups", "slab"), None, None)
    return jax.shard_map(
        shard,
        mesh=mesh,
        in_specs=(
            split,
            split,
            split,
            P(None, ("groups", "slab"), None, None),
            P(("groups", "slab"), None),
            P(),
            P(("groups", "slab"), None),
            P(("groups", "slab")),
        ),
        out_specs=(split, split, split),
        check_vma=False,
    )
```

```python
import functools

import jax
import jax.numpy as jnp
from jax import lax
from jax.experimental import pallas as pl
from jax.experimental.pallas import tpu as pltpu
from jax.sharding import PartitionSpec as P


CAP = 4
STEPS = 2
W = (-205.0 / 72.0, 8.0 / 5.0, -1.0 / 5.0, 8.0 / 315.0, -1.0 / 560.0)
HALO = 4
ROWS = 16
BLOCK = 32
EDGE = 8
SUB = 8
UNROLL = 4
LANES = 128
F32 = jnp.float32
BF16 = jnp.bfloat16
VMEM = pl.BlockSpec(memory_space=pltpu.VMEM)
SMEM = pl.BlockSpec(memory_space=pltpu.SMEM)
HBM = pl.BlockSpec(memory_space=pltpu.HBM)


def params():
    return pltpu.CompilerParams(vmem_limit_bytes=16 << 20)


def payload_lanes(width):
    full = width // LANES * LANES
    rest = width - full
    if rest == 0:
        return HALO * full
    return HALO * full + (2 * LANES if rest * 2 <= LANES else HALO * LANES)


def depth_at(j, depth):
    odd = lax.rem(lax.axis_index("slab"), 2)
    return j + (1 - odd) * (depth - 1 - 2 * j)


def encode(u):
    t1 = u[0].astype(BF16).astype(F32)
    e1 = u[0] - t1
    t2 = (u[1] + (W[2] / W[3]) * e1).astype(BF16).astype(F32)
    t3 = u[2].astype(BF16).astype(F32)
    t0 = W[1] * e1 + W[2] * (u[1] - t2) + W[3] * (u[2] - t3) + W[4] * u[3]
    return (t0, t1, t2, t3)


def decode(t):
    t0, t1, t2, t3 = t
    return (
        t0 + W[1] * t1 + W[2] * t2 + W[3] * t3,
        W[2] * t1 + W[3] * t2 + W[4] * t3,
        W[3] * t1 + W[4] * t2,
        W[4] * t1,
    )


def put(ref, rows, t):
    width = t[0].shape[1]
    full = width // LANES * LANES
    rest = width - full
    for k in range(HALO):
        ref[rows, k * full : (k + 1) * full] = t[k][:, :full].astype(BF16)
    if rest == 0:
        return
    base = HALO * full
    if rest * 2 <= LANES:
        half = LANES // 2
        for k in range(0, HALO, 2):
            a = jnp.pad(t[k][:, full:], ((0, 0), (0, half - rest)))
            b = jnp.pad(t[k + 1][:, full:], ((0, 0), (0, half - rest)))
            ref[rows, base : base + LANES] = jnp.concatenate([a, b], axis=1).astype(BF16)
            base += LANES
    else:
        for k in range(HALO):
            tail = jnp.pad(t[k][:, full:], ((0, 0), (0, LANES - rest)))
            ref[rows, base : base + LANES] = tail.astype(BF16)
            base += LANES


def take(ref, rows, width):
    full = width // LANES * LANES
    rest = width - full
    main = [ref[rows, k * full : (k + 1) * full].astype(F32) for k in range(HALO)]
    if rest == 0:
        return main
    base = HALO * full
    tails = []
    if rest * 2 <= LANES:
        half = LANES // 2
        for _ in range(0, HALO, 2):
            both = ref[rows, base : base + LANES].astype(F32)
            tails.append(both[:, :rest])
            tails.append(pltpu.roll(both, half, 1)[:, :rest])
            base += LANES
    else:
        for _ in range(HALO):
            tails.append(ref[rows, base : base + LANES].astype(F32)[:, :rest])
            base += LANES
    return [jnp.concatenate([m, t], axis=1) for m, t in zip(main, tails)]


def row_loop(count, body):
    def step(i, carry):
        body(pl.multiple_of(i * ROWS, ROWS))
        return carry

    lax.fori_loop(0, count // ROWS, step, 0)


def fetch(source, buf, sems, first, count):
    copies = []
    for i in range(0, count, BLOCK):
        rows = pl.ds(first + i, BLOCK)
        copies.append(
            pltpu.make_async_copy(source.at[:, rows], buf.at[:, pl.ds(i, BLOCK)], sems.at[i // BLOCK])
        )
        copies[-1].start()
    return copies


def pack_kernel(first, with_on, now, *refs):
    refs = list(refs)
    on_ref = refs.pop(0) if with_on else None
    off_ref, buf, sems = refs
    depth = now.shape[0]
    base = 0 if with_on else first
    copies = fetch(now, buf, sems, base, buf.shape[1])

    for i, copy in enumerate(copies):
        copy.wait()

        def body(r):
            r = r + i * BLOCK
            rows = pl.ds(r, ROWS)
            u = [buf[depth_at(j, depth), rows, :] for j in range(depth)]
            if base + i * BLOCK >= first and base + i * BLOCK < first + off_ref.shape[0]:
                put(off_ref, pl.ds(r + base - first, ROWS), encode(u[::-1][:HALO]))
            if with_on:
                put(on_ref, rows, encode(u[:HALO]))

        row_loop(BLOCK, body)


def route_kernel(slabs, lines, width_y, traces, weights, target, cell, out):
    rows = traces.shape[0]
    lane = lax.broadcasted_iota(jnp.int32, (rows, rows), 1)
    row = lax.broadcasted_iota(jnp.int32, (rows, rows), 0)
    eye = lane == row
    target_row = jnp.broadcast_to(target[...], (rows, rows))
    cell_row = jnp.broadcast_to(cell[...], (rows, rows))
    target_col = jnp.sum(jnp.where(eye, target_row, 0), axis=1, keepdims=True)
    cell_col = jnp.sum(jnp.where(eye, cell_row, 0), axis=1, keepdims=True)
    same = (target_row == target_col) & (lane < row)
    rank = jnp.sum(jnp.where(same, 1, 0), axis=1, keepdims=True)
    values = traces[...].astype(F32)
    columns = [
        jnp.sum(values * weights[s : s + 1, :].astype(F32), axis=1, keepdims=True)
        for s in range(STEPS)
    ]
    cell_line = cell_col // width_y
    column = cell_col - cell_line * width_y
    tile = column // LANES
    columns.append((tile * lines + cell_line).astype(F32))
    columns.append((column - tile * LANES).astype(F32))
    spot = lax.broadcasted_iota(jnp.int32, (rows, LANES), 1)
    spread = jnp.zeros((rows, LANES), F32)
    for j, column in enumerate(columns):
        spread = jnp.where(spot == j * CAP + rank, column, spread)
    taker = lax.broadcasted_iota(jnp.int32, (slabs, rows), 0)
    chosen = (taker == jnp.broadcast_to(target[...], (slabs, rows))).astype(F32)
    picked = jnp.dot(
        chosen, spread, precision=lax.Precision.HIGHEST, preferred_element_type=F32
    )
    out[...] = picked.reshape(out.shape)


def spread(tiles, source, first, start, count):
    depth, _, width_y = source.shape
    width_x = (tiles.shape[1] - 2 * EDGE) // depth

    def body(r):
        for z in range(depth):
            into = pl.ds(r + (EDGE + z * width_x + first), ROWS)
            for j in range(tiles.shape[0]):
                lo, hi = j * LANES, min((j + 1) * LANES, width_y)
                value = source[z, pl.ds(r + start, ROWS), lo:hi]
                if hi - lo < LANES:
                    value = jnp.pad(value, ((0, 0), (0, LANES - (hi - lo))))
                tiles[j, into, :] = value

    row_loop(count, body)


def own_laplace(tiles, lap, depth, width_y):
    count, _ = lap.shape
    count = count // tiles.shape[0]
    parts = SUB // depth
    stride = count // SUB
    number = tiles.shape[0]
    shape = (SUB, LANES)
    lane = lax.broadcasted_iota(jnp.int32, shape, 1)
    sub = lax.broadcasted_iota(jnp.int32, shape, 0)
    part = lax.rem(sub, parts)

    def weight(k):
        return W[k] if k <= HALO else 0.0

    mixes = [jnp.where(sub >= d * parts, weight(d), weight(depth - d)) for d in range(1, depth)]

    def rows_at(j, x):
        return tiles[j, pl.ds(x + EDGE, SUB, stride=stride), :]

    def one(x, low=None, high=None):
        centre = [rows_at(j, x) for j in range(number)]
        right = [[pltpu.roll(c, k, 1) for k in range(1, HALO + 1)] for c in centre]
        left = [[pltpu.roll(c, LANES - k, 1) for k in range(1, HALO + 1)] for c in centre]
        for j in range(number):
            total = 3.0 * W[0] * centre[j]
            for d in range(1, depth):
                total = total + mixes[d - 1] * pltpu.roll(centre[j], d * parts, 0)
            for k in range(1, HALO + 1):
                before, after = rows_at(j, x - k), rows_at(j, x + k)
                if low is not None and low < k:
                    before = jnp.where(part == 0, 0.0, before)
                if high is not None and high < k:
                    after = jnp.where(part == parts - 1, 0.0, after)
                side = right[j - 1][k - 1] if j else 0.0
                pair = before + after + jnp.where(lane < k, side, right[j][k - 1])
                if j + 1 < number:
                    pair = pair + jnp.where(lane >= LANES - k, left[j + 1][k - 1], left[j][k - 1])
                elif width_y % LANES > LANES - HALO or width_y % LANES == 0:
                    pair = pair + jnp.where(lane >= LANES - k, 0.0, left[j][k - 1])
                else:
                    pair = pair + left[j][k - 1]
                total = total + W[k] * pair
            lap[pl.ds(x + j * count, SUB, stride=stride), :] = total

    for x in range(HALO):
        one(x, low=x)

    def step(i, carry):
        for u in range(UNROLL):
            one(HALO + i * UNROLL + u)
        return carry

    steps = (stride - 2 * HALO) // UNROLL
    lax.fori_loop(0, steps, step, 0)
    for x in range(HALO + steps * UNROLL, stride):
        one(x, high=stride - 1 - x)


def inject(step, got, lap):
    lane = lax.broadcasted_iota(jnp.int32, (1, LANES), 1)

    def body(i, carry):
        for slot in range(CAP):
            source = got[i, 0, step * CAP + slot]
            row = pl.ds(got[i, 0, STEPS * CAP + slot].astype(jnp.int32), 1)
            spot = got[i, 0, (STEPS + 1) * CAP + slot].astype(jnp.int32)
            lap[row, :] = lap[row, :] + jnp.where(lane == spot, source, 0.0)
        return carry

    lax.fori_loop(0, got.shape[0], body, 0)


def tile_parts(width_y):
    return [(lo, min(lo + LANES, width_y)) for lo in range(0, width_y, LANES)]


def own_kernel(now, prior, velocity, got, out, tiles, lap, now_buf, prior_buf, sems):
    depth, width_x, width_y = now.shape
    now_copies = fetch(now, now_buf, sems.at[0], 0, width_x)
    prior_copies = fetch(prior, prior_buf, sems.at[1], 0, width_x)
    for i, copy in enumerate(now_copies):
        copy.wait()
        spread(tiles, now_buf, i * BLOCK, i * BLOCK, BLOCK)
    own_laplace(tiles, lap, depth, width_y)
    inject(0, got, lap)
    for copy in prior_copies:
        copy.wait()

    def body(r):
        rows = pl.ds(r, ROWS)
        for z in range(depth):
            for j, (lo, hi) in enumerate(tile_parts(width_y)):
                change = lap[pl.ds(r + (j * depth + z) * width_x, ROWS), :][:, : hi - lo]
                value = 2.0 * now_buf[z, rows, lo:hi] - prior_buf[z, rows, lo:hi]
                out[z, rows, lo:hi] = value + velocity[z, rows, lo:hi] * change

    row_loop(width_x, body)


def halo_sum(got_on, rows_on, got_off, rows_off, width_y, depth):
    near = decode(take(got_on, rows_on, width_y))
    far = decode(take(got_off, rows_off, width_y))
    out = []
    for j in range(depth):
        terms = [near[j]] if j < HALO else []
        if depth - 1 - j < HALO:
            terms.append(far[depth - 1 - j])
        out.append(functools.reduce(lambda a, b: a + b, terms) if terms else None)
    return out


def close_kernel(first, partial, velocity, got_on, got_off, out, on_ref, off_ref):
    depth, count, width_y = out.shape

    def body(r):
        rows = pl.ds(r, ROWS)
        whole = pl.ds(r + first, ROWS)
        halo = halo_sum(got_on, whole, got_off, rows, width_y, depth)
        u = []
        for j in range(depth):
            z = depth_at(j, depth)
            value = partial[z, whole, :]
            if halo[j] is not None:
                value = value + velocity[z, whole, :] * halo[j]
            out[z, rows, :] = value
            u.append(value)
        put(off_ref, rows, encode(u[::-1][:HALO]))
        put(on_ref, rows, encode(u[:HALO]))

    row_loop(count, body)


def second_kernel(starts, *refs):
    parts, refs = refs[: len(starts)], refs[len(starts) :]
    now, velocity, forward, got, out, image, current, tiles, lap, now_buf, sems, out_sems = refs
    depth, width_x, width_y = now.shape
    copies = fetch(now, now_buf, sems, 0, width_x)
    writes = []
    for i, (first, part) in enumerate(zip(starts, parts)):
        write = pltpu.make_async_copy(
            part, current.at[:, pl.ds(first, part.shape[1])], out_sems.at[i]
        )
        write.start()
        writes.append(write)
    for first, part in zip(starts, parts):
        spread(tiles, part, first, 0, part.shape[1])
    own_laplace(tiles, lap, depth, width_y)
    inject(1, got, lap)
    for copy in copies:
        copy.wait()

    for first, part in zip(starts, parts):

        def body(r):
            rows = pl.ds(r, ROWS)
            whole = pl.ds(r + first, ROWS)
            for z in range(depth):
                for j, (lo, hi) in enumerate(tile_parts(width_y)):
                    change = lap[pl.ds(r + ((j * depth + z) * width_x + first), ROWS), :]
                    here = part[z, rows, lo:hi]
                    value = 2.0 * here - now_buf[z, whole, lo:hi]
                    value = value + velocity[z, whole, lo:hi] * change[:, : hi - lo]
                    out[z, whole, lo:hi] = value
                    image[z, whole, lo:hi] = (
                        forward[0, z, whole, lo:hi] * here + forward[1, z, whole, lo:hi] * value
                    )

        row_loop(part.shape[1], body)
    for write in writes:
        write.wait()


def last_kernel(first, count, partial, image_in, velocity, forward, got_on, got_off, *refs):
    out, image, out_buf, image_buf, sems = refs[-5:]
    depth, width_y = out.shape[0], out.shape[2]
    writes = []
    for i in range(0, count, BLOCK):

        def body(r):
            rows = pl.ds(r + i, ROWS)
            whole = pl.ds(r + (first + i), ROWS)
            halo = halo_sum(got_on, rows, got_off, rows, width_y, depth)
            for j in range(depth):
                z = depth_at(j, depth)
                extra = velocity[z, whole, :] * halo[j] if halo[j] is not None else 0.0
                out_buf[z, rows, :] = partial[z, whole, :] + extra
                image_buf[z, rows, :] = image_in[z, whole, :] + forward[1, z, whole, :] * extra

        row_loop(BLOCK, body)
        for k, (buf, target) in enumerate(((out_buf, out), (image_buf, image))):
            write = pltpu.make_async_copy(
                buf.at[:, pl.ds(i, BLOCK)],
                target.at[:, pl.ds(first + i, BLOCK)],
                sems.at[k, i // BLOCK],
            )
            write.start()
            writes.append(write)
    for write in writes:
        write.wait()


def shard(now, prior, velocity, forward, traces, weights, target, cell):
    now = pltpu.with_memory_space_constraint(now, pltpu.HBM)
    prior = pltpu.with_memory_space_constraint(prior, pltpu.HBM)
    slabs = lax.axis_size("slab")
    depth, width_x, width_y = now.shape
    rows = traces.shape[0]
    face_lanes = payload_lanes(width_y)
    half = width_x // (2 * BLOCK) * BLOCK
    chunks = ((0, half), (half, width_x - half))
    starts = tuple(first for first, _ in chunks)
    blocks = width_x // BLOCK
    field = jax.ShapeDtypeStruct(now.shape, F32)
    number = -(-width_y // LANES)
    tiles = pltpu.VMEM((number, depth * width_x + 2 * EDGE, LANES), F32)
    lap = pltpu.VMEM((number * depth * width_x, LANES), F32)
    dma = pltpu.SemaphoreType.DMA
    on_pairs = [(k, k ^ 1) for k in range(slabs) if k ^ 1 < slabs]
    off_pairs = [(i + 1, j + 1) for i, j in on_pairs if i + 1 < slabs and j + 1 < slabs]

    def plane(count):
        return jax.ShapeDtypeStruct((count, face_lanes), BF16)

    def buffer(count):
        return pltpu.VMEM((depth, count, width_y), F32)

    def call(kernel, ins, outs, scratch=(), out_spec=None, **kw):
        return pl.pallas_call(
            kernel,
            in_specs=ins,
            out_specs=out_spec or [VMEM] * len(outs),
            out_shape=outs,
            scratch_shapes=scratch,
            compiler_params=params(),
            **kw,
        )

    def swap(face, pairs):
        return lax.ppermute(face, "slab", pairs)

    got_off = []
    (face,) = call(
        functools.partial(pack_kernel, 0, False),
        [HBM],
        [plane(half)],
        (buffer(half), dma((half // BLOCK,))),
    )(now)
    got_off.append(swap(face, off_pairs))
    face, traces = lax.optimization_barrier((face, traces))
    (sent,) = call(
        functools.partial(route_kernel, slabs, depth * width_x, width_y),
        [VMEM] * 4,
        [jax.ShapeDtypeStruct((slabs, 1, LANES), F32)],
    )(traces, weights, target.reshape(1, rows), cell.reshape(1, rows))
    got = lax.all_to_all(sent, "slab", split_axis=0, concat_axis=0, tiled=True)
    sent, later = lax.optimization_barrier((sent, now))
    on_face, face = call(
        functools.partial(pack_kernel, half, True),
        [HBM],
        [plane(width_x), plane(width_x - half)],
        (buffer(width_x), dma((blocks,))),
    )(later)
    got_off.append(swap(face, off_pairs))
    got_on = swap(on_face, on_pairs)
    (partial,) = call(
        own_kernel,
        [HBM, HBM, VMEM, SMEM],
        [field],
        (tiles, lap, buffer(width_x), buffer(width_x), dma((2, blocks))),
    )(now, prior, velocity, got)
    parts, second_on, second_off = [], [], []
    for (first, count), got_face in zip(chunks, got_off):
        part, on_face, face = call(
            functools.partial(close_kernel, first),
            [VMEM] * 4,
            [jax.ShapeDtypeStruct((depth, count, width_y), F32), plane(count), plane(count)],
        )(partial, velocity, got_on, got_face)
        second_off.append(swap(face, off_pairs))
        second_on.append(swap(on_face, on_pairs))
        parts.append(part)
        part, partial = lax.optimization_barrier((part, partial))
    partial, image, current = call(
        functools.partial(second_kernel, starts),
        [VMEM] * len(parts) + [HBM, VMEM, VMEM, SMEM],
        [field, field, field],
        (tiles, lap, buffer(width_x), dma((blocks,)), dma((len(parts),))),
        [VMEM, VMEM, HBM],
    )(*parts, now, velocity, forward, got)
    done = ()
    for i, (first, count) in enumerate(chunks):
        done = call(
            functools.partial(last_kernel, first, count),
            [VMEM] * 6 + [HBM] * len(done),
            [field, field],
            (buffer(count), buffer(count), dma((2, count // BLOCK))),
            [HBM, HBM],
            input_output_aliases={6: 0, 7: 1} if done else {},
        )(partial, image, velocity, forward, second_on[i], second_off[i], *done)
    second, image = done
    return (image, second, current)


def solution(mesh):
    split = P(("groups", "slab"), None, None)
    return jax.shard_map(
        shard,
        mesh=mesh,
        in_specs=(
            split,
            split,
            split,
            P(None, ("groups", "slab"), None, None),
            P(("groups", "slab"), None),
            P(),
            P(("groups", "slab"), None),
            P(("groups", "slab")),
        ),
        out_specs=(split, split, split),
        check_vma=False,
    )
```

```python
import functools

import jax
import jax.numpy as jnp
from jax import lax
from jax.experimental import pallas as pl
from jax.experimental.pallas import tpu as pltpu
from jax.sharding import PartitionSpec as P


CAP = 4
STEPS = 2
W = (-205.0 / 72.0, 8.0 / 5.0, -1.0 / 5.0, 8.0 / 315.0, -1.0 / 560.0)
HALO = 4
ROWS = 16
BLOCK = 32
SUB = 8
LANES = 128
F32 = jnp.float32
BF16 = jnp.bfloat16
VMEM = pl.BlockSpec(memory_space=pltpu.VMEM)
SMEM = pl.BlockSpec(memory_space=pltpu.SMEM)
HBM = pl.BlockSpec(memory_space=pltpu.HBM)


def params():
    return pltpu.CompilerParams(vmem_limit_bytes=16 << 20)


def payload_lanes(width):
    full = width // LANES * LANES
    rest = width - full
    if rest == 0:
        return HALO * full
    return HALO * full + (2 * LANES if rest * 2 <= LANES else HALO * LANES)


def depth_at(j, depth):
    odd = lax.rem(lax.axis_index("slab"), 2)
    return j + (1 - odd) * (depth - 1 - 2 * j)


def encode(u):
    t1 = u[0].astype(BF16).astype(F32)
    e1 = u[0] - t1
    t2 = (u[1] + (W[2] / W[3]) * e1).astype(BF16).astype(F32)
    t3 = u[2].astype(BF16).astype(F32)
    t0 = W[1] * e1 + W[2] * (u[1] - t2) + W[3] * (u[2] - t3) + W[4] * u[3]
    return (t0, t1, t2, t3)


def decode(t):
    t0, t1, t2, t3 = t
    return (
        t0 + W[1] * t1 + W[2] * t2 + W[3] * t3,
        W[2] * t1 + W[3] * t2 + W[4] * t3,
        W[3] * t1 + W[4] * t2,
        W[4] * t1,
    )


def put(ref, rows, t):
    width = t[0].shape[1]
    full = width // LANES * LANES
    rest = width - full
    for k in range(HALO):
        ref[rows, k * full : (k + 1) * full] = t[k][:, :full].astype(BF16)
    if rest == 0:
        return
    base = HALO * full
    if rest * 2 <= LANES:
        half = LANES // 2
        for k in range(0, HALO, 2):
            a = jnp.pad(t[k][:, full:], ((0, 0), (0, half - rest)))
            b = jnp.pad(t[k + 1][:, full:], ((0, 0), (0, half - rest)))
            ref[rows, base : base + LANES] = jnp.concatenate([a, b], axis=1).astype(BF16)
            base += LANES
    else:
        for k in range(HALO):
            tail = jnp.pad(t[k][:, full:], ((0, 0), (0, LANES - rest)))
            ref[rows, base : base + LANES] = tail.astype(BF16)
            base += LANES


def take(ref, rows, width):
    full = width // LANES * LANES
    rest = width - full
    main = [ref[rows, k * full : (k + 1) * full].astype(F32) for k in range(HALO)]
    if rest == 0:
        return main
    base = HALO * full
    tails = []
    if rest * 2 <= LANES:
        half = LANES // 2
        for _ in range(0, HALO, 2):
            both = ref[rows, base : base + LANES].astype(F32)
            tails.append(both[:, :rest])
            tails.append(pltpu.roll(both, half, 1)[:, :rest])
            base += LANES
    else:
        for _ in range(HALO):
            tails.append(ref[rows, base : base + LANES].astype(F32)[:, :rest])
            base += LANES
    return [jnp.concatenate([m, t], axis=1) for m, t in zip(main, tails)]


def row_loop(count, body):
    def step(i, carry):
        body(pl.multiple_of(i * ROWS, ROWS))
        return carry

    lax.fori_loop(0, count // ROWS, step, 0)


def fetch(source, buf, sems, first, count):
    copies = []
    for i in range(0, count, BLOCK):
        rows = pl.ds(first + i, BLOCK)
        copies.append(
            pltpu.make_async_copy(source.at[:, rows], buf.at[:, pl.ds(i, BLOCK)], sems.at[i // BLOCK])
        )
        copies[-1].start()
    return copies


def pack_kernel(first, with_on, now, *refs):
    refs = list(refs)
    on_ref = refs.pop(0) if with_on else None
    off_ref, buf, sems = refs
    depth = now.shape[0]
    base = 0 if with_on else first
    copies = fetch(now, buf, sems, base, buf.shape[1])

    for i, copy in enumerate(copies):
        copy.wait()

        def body(r):
            r = r + i * BLOCK
            rows = pl.ds(r, ROWS)
            u = [buf[depth_at(j, depth), rows, :] for j in range(depth)]
            if base + i * BLOCK >= first and base + i * BLOCK < first + off_ref.shape[0]:
                put(off_ref, pl.ds(r + base - first, ROWS), encode(u[::-1][:HALO]))
            if with_on:
                put(on_ref, rows, encode(u[:HALO]))

        row_loop(BLOCK, body)


def route_kernel(slabs, lines, width_y, traces, weights, target, cell, out):
    rows = traces.shape[0]
    lane = lax.broadcasted_iota(jnp.int32, (rows, rows), 1)
    row = lax.broadcasted_iota(jnp.int32, (rows, rows), 0)
    eye = lane == row
    target_row = jnp.broadcast_to(target[...], (rows, rows))
    cell_row = jnp.broadcast_to(cell[...], (rows, rows))
    target_col = jnp.sum(jnp.where(eye, target_row, 0), axis=1, keepdims=True)
    cell_col = jnp.sum(jnp.where(eye, cell_row, 0), axis=1, keepdims=True)
    same = (target_row == target_col) & (lane < row)
    rank = jnp.sum(jnp.where(same, 1, 0), axis=1, keepdims=True)
    values = traces[...].astype(F32)
    columns = [
        jnp.sum(values * weights[s : s + 1, :].astype(F32), axis=1, keepdims=True)
        for s in range(STEPS)
    ]
    cell_line = cell_col // width_y
    column = cell_col - cell_line * width_y
    tile = column // LANES
    columns.append((tile * lines + cell_line).astype(F32))
    columns.append((column - tile * LANES).astype(F32))
    spot = lax.broadcasted_iota(jnp.int32, (rows, LANES), 1)
    spread = jnp.zeros((rows, LANES), F32)
    for j, column in enumerate(columns):
        spread = jnp.where(spot == j * CAP + rank, column, spread)
    taker = lax.broadcasted_iota(jnp.int32, (slabs, rows), 0)
    chosen = (taker == jnp.broadcast_to(target[...], (slabs, rows))).astype(F32)
    picked = jnp.dot(
        chosen, spread, precision=lax.Precision.HIGHEST, preferred_element_type=F32
    )
    out[...] = picked.reshape(out.shape)


def tile_parts(width_y):
    return [(lo, min(lo + LANES, width_y)) for lo in range(0, width_y, LANES)]


def tile_rows(z, row, j, width_x, number):
    return pl.ds((z * (width_x + SUB) + SUB + row) * number + j, SUB, stride=number)


def clear(tiles, depth, width_x, number):
    for z in range(depth + 1):
        first = z * (width_x + SUB) * number
        tiles[first : first + SUB * number, :] = jnp.zeros((SUB * number, LANES), F32)


def spread(tiles, source, first, start, count):
    depth, _, width_y = source.shape
    parts = tile_parts(width_y)
    number = len(parts)
    width_x = (tiles.shape[0] // number - SUB) // depth - SUB

    def body(r):
        for z in range(depth):
            for j, (lo, hi) in enumerate(parts):
                for u in range(0, ROWS, SUB):
                    value = source[z, pl.ds(r + (start + u), SUB), lo:hi]
                    if hi - lo < LANES:
                        value = jnp.pad(value, ((0, 0), (0, LANES - (hi - lo))))
                    tiles[tile_rows(z, r + (first + u), j, width_x, number), :] = value

    row_loop(count, body)


def own_laplace(tiles, lap, depth, width_y):
    number = -(-width_y // LANES)
    width_x = lap.shape[0] // (number * depth)
    lane = lax.broadcasted_iota(jnp.int32, (SUB, LANES), 1)
    wraps = width_y % LANES == 0 or width_y % LANES > LANES - HALO

    def step(i, carry):
        r = i * SUB

        def at(z, j, shift=0):
            return tiles[tile_rows(z, r + shift, j, width_x, number), :]

        centre = [[at(z, j) for j in range(number)] for z in range(depth)]
        for z in range(depth):
            total = [3.0 * W[0] * centre[z][j] for j in range(number)]
            for k in range(1, HALO + 1):
                right = [pltpu.roll(c, k, 1) for c in centre[z]]
                left = [pltpu.roll(c, LANES - k, 1) for c in centre[z]]
                for j in range(number):
                    pair = at(z, j, -k) + at(z, j, k)
                    pair = pair + jnp.where(lane < k, right[j - 1] if j else 0.0, right[j])
                    if j + 1 < number or wraps:
                        side = left[j + 1] if j + 1 < number else 0.0
                        pair = pair + jnp.where(lane >= LANES - k, side, left[j])
                    else:
                        pair = pair + left[j]
                    if z - k >= 0:
                        pair = pair + centre[z - k][j]
                    if z + k < depth:
                        pair = pair + centre[z + k][j]
                    total[j] = total[j] + W[k] * pair
            for j in range(number):
                place = pl.multiple_of(r + (j * depth + z) * width_x, SUB)
                lap[pl.ds(place, SUB), :] = total[j]
        return carry

    lax.fori_loop(0, width_x // SUB, step, 0)


def inject(step, got, lap):
    lane = lax.broadcasted_iota(jnp.int32, (1, LANES), 1)

    def body(i, carry):
        for slot in range(CAP):
            source = got[i, 0, step * CAP + slot]
            row = pl.ds(got[i, 0, STEPS * CAP + slot].astype(jnp.int32), 1)
            spot = got[i, 0, (STEPS + 1) * CAP + slot].astype(jnp.int32)
            lap[row, :] = lap[row, :] + jnp.where(lane == spot, source, 0.0)
        return carry

    lax.fori_loop(0, got.shape[0], body, 0)


def own_kernel(now, prior, velocity, got, out, tiles, lap, now_buf, prior_buf, sems):
    depth, width_x, width_y = now.shape
    now_copies = fetch(now, now_buf, sems.at[0], 0, width_x)
    prior_copies = fetch(prior, prior_buf, sems.at[1], 0, width_x)
    clear(tiles, depth, width_x, len(tile_parts(width_y)))
    for i, copy in enumerate(now_copies):
        copy.wait()
        spread(tiles, now_buf, i * BLOCK, i * BLOCK, BLOCK)
    own_laplace(tiles, lap, depth, width_y)
    inject(0, got, lap)
    for copy in prior_copies:
        copy.wait()

    def body(r):
        rows = pl.ds(r, ROWS)
        for z in range(depth):
            for j, (lo, hi) in enumerate(tile_parts(width_y)):
                change = lap[pl.ds(r + (j * depth + z) * width_x, ROWS), :][:, : hi - lo]
                value = 2.0 * now_buf[z, rows, lo:hi] - prior_buf[z, rows, lo:hi]
                out[z, rows, lo:hi] = value + velocity[z, rows, lo:hi] * change

    row_loop(width_x, body)


def halo_sum(got_on, rows_on, got_off, rows_off, width_y, depth):
    near = decode(take(got_on, rows_on, width_y))
    far = decode(take(got_off, rows_off, width_y))
    out = []
    for j in range(depth):
        terms = [near[j]] if j < HALO else []
        if depth - 1 - j < HALO:
            terms.append(far[depth - 1 - j])
        out.append(functools.reduce(lambda a, b: a + b, terms) if terms else None)
    return out


def close_kernel(first, partial, velocity, got_on, got_off, out, on_ref, off_ref):
    depth, count, width_y = out.shape

    def body(r):
        rows = pl.ds(r, ROWS)
        whole = pl.ds(r + first, ROWS)
        halo = halo_sum(got_on, whole, got_off, rows, width_y, depth)
        u = []
        for j in range(depth):
            z = depth_at(j, depth)
            value = partial[z, whole, :]
            if halo[j] is not None:
                value = value + velocity[z, whole, :] * halo[j]
            out[z, rows, :] = value
            u.append(value)
        put(off_ref, rows, encode(u[::-1][:HALO]))
        put(on_ref, rows, encode(u[:HALO]))

    row_loop(count, body)


def second_kernel(starts, *refs):
    parts, refs = refs[: len(starts)], refs[len(starts) :]
    now, velocity, forward, got, out, image, current, tiles, lap, now_buf, sems, out_sems = refs
    depth, width_x, width_y = now.shape
    copies = fetch(now, now_buf, sems, 0, width_x)
    writes = []
    for i, (first, part) in enumerate(zip(starts, parts)):
        write = pltpu.make_async_copy(
            part, current.at[:, pl.ds(first, part.shape[1])], out_sems.at[i]
        )
        write.start()
        writes.append(write)
    clear(tiles, depth, width_x, len(tile_parts(width_y)))
    for first, part in zip(starts, parts):
        spread(tiles, part, first, 0, part.shape[1])
    own_laplace(tiles, lap, depth, width_y)
    inject(1, got, lap)
    for copy in copies:
        copy.wait()

    for first, part in zip(starts, parts):

        def body(r):
            rows = pl.ds(r, ROWS)
            whole = pl.ds(r + first, ROWS)
            for z in range(depth):
                for j, (lo, hi) in enumerate(tile_parts(width_y)):
                    change = lap[pl.ds(r + ((j * depth + z) * width_x + first), ROWS), :]
                    here = part[z, rows, lo:hi]
                    value = 2.0 * here - now_buf[z, whole, lo:hi]
                    value = value + velocity[z, whole, lo:hi] * change[:, : hi - lo]
                    out[z, whole, lo:hi] = value
                    image[z, whole, lo:hi] = (
                        forward[0, z, whole, lo:hi] * here + forward[1, z, whole, lo:hi] * value
                    )

        row_loop(part.shape[1], body)
    for write in writes:
        write.wait()


def last_kernel(first, count, partial, image_in, velocity, forward, got_on, got_off, *refs):
    out, image, out_buf, image_buf, sems = refs[-5:]
    depth, width_y = out.shape[0], out.shape[2]
    writes = []
    for i in range(0, count, BLOCK):

        def body(r):
            rows = pl.ds(r + i, ROWS)
            whole = pl.ds(r + (first + i), ROWS)
            halo = halo_sum(got_on, rows, got_off, rows, width_y, depth)
            for j in range(depth):
                z = depth_at(j, depth)
                extra = velocity[z, whole, :] * halo[j] if halo[j] is not None else 0.0
                out_buf[z, rows, :] = partial[z, whole, :] + extra
                image_buf[z, rows, :] = image_in[z, whole, :] + forward[1, z, whole, :] * extra

        row_loop(BLOCK, body)
        for k, (buf, target) in enumerate(((out_buf, out), (image_buf, image))):
            write = pltpu.make_async_copy(
                buf.at[:, pl.ds(i, BLOCK)],
                target.at[:, pl.ds(first + i, BLOCK)],
                sems.at[k, i // BLOCK],
            )
            write.start()
            writes.append(write)
    for write in writes:
        write.wait()


def shard(now, prior, velocity, forward, traces, weights, target, cell):
    now = pltpu.with_memory_space_constraint(now, pltpu.HBM)
    prior = pltpu.with_memory_space_constraint(prior, pltpu.HBM)
    slabs = lax.axis_size("slab")
    depth, width_x, width_y = now.shape
    rows = traces.shape[0]
    face_lanes = payload_lanes(width_y)
    half = width_x // (2 * BLOCK) * BLOCK
    chunks = ((0, half), (half, width_x - half))
    starts = tuple(first for first, _ in chunks)
    blocks = width_x // BLOCK
    field = jax.ShapeDtypeStruct(now.shape, F32)
    number = -(-width_y // LANES)
    tiles = pltpu.VMEM((number * (depth * (width_x + SUB) + SUB), LANES), F32)
    lap = pltpu.VMEM((number * depth * width_x, LANES), F32)
    dma = pltpu.SemaphoreType.DMA
    on_pairs = [(k, k ^ 1) for k in range(slabs) if k ^ 1 < slabs]
    off_pairs = [(i + 1, j + 1) for i, j in on_pairs if i + 1 < slabs and j + 1 < slabs]

    def plane(count):
        return jax.ShapeDtypeStruct((count, face_lanes), BF16)

    def buffer(count):
        return pltpu.VMEM((depth, count, width_y), F32)

    def call(kernel, ins, outs, scratch=(), out_spec=None, **kw):
        return pl.pallas_call(
            kernel,
            in_specs=ins,
            out_specs=out_spec or [VMEM] * len(outs),
            out_shape=outs,
            scratch_shapes=scratch,
            compiler_params=params(),
            **kw,
        )

    def swap(face, pairs):
        return lax.ppermute(face, "slab", pairs)

    got_off = []
    (face,) = call(
        functools.partial(pack_kernel, 0, False),
        [HBM],
        [plane(half)],
        (buffer(half), dma((half // BLOCK,))),
    )(now)
    got_off.append(swap(face, off_pairs))
    face, traces = lax.optimization_barrier((face, traces))
    (sent,) = call(
        functools.partial(route_kernel, slabs, depth * width_x, width_y),
        [VMEM] * 4,
        [jax.ShapeDtypeStruct((slabs, 1, LANES), F32)],
    )(traces, weights, target.reshape(1, rows), cell.reshape(1, rows))
    got = lax.all_to_all(sent, "slab", split_axis=0, concat_axis=0, tiled=True)
    sent, later = lax.optimization_barrier((sent, now))
    on_face, face = call(
        functools.partial(pack_kernel, half, True),
        [HBM],
        [plane(width_x), plane(width_x - half)],
        (buffer(width_x), dma((blocks,))),
    )(later)
    got_off.append(swap(face, off_pairs))
    got_on = swap(on_face, on_pairs)
    (partial,) = call(
        own_kernel,
        [HBM, HBM, VMEM, SMEM],
        [field],
        (tiles, lap, buffer(width_x), buffer(width_x), dma((2, blocks))),
    )(now, prior, velocity, got)
    parts, second_on, second_off = [], [], []
    for (first, count), got_face in zip(chunks, got_off):
        part, on_face, face = call(
            functools.partial(close_kernel, first),
            [VMEM] * 4,
            [jax.ShapeDtypeStruct((depth, count, width_y), F32), plane(count), plane(count)],
        )(partial, velocity, got_on, got_face)
        second_off.append(swap(face, off_pairs))
        second_on.append(swap(on_face, on_pairs))
        parts.append(part)
        part, partial = lax.optimization_barrier((part, partial))
    partial, image, current = call(
        functools.partial(second_kernel, starts),
        [VMEM] * len(parts) + [HBM, VMEM, VMEM, SMEM],
        [field, field, field],
        (tiles, lap, buffer(width_x), dma((blocks,)), dma((len(parts),))),
        [VMEM, VMEM, HBM],
    )(*parts, now, velocity, forward, got)
    done = ()
    for i, (first, count) in enumerate(chunks):
        done = call(
            functools.partial(last_kernel, first, count),
            [VMEM] * 6 + [HBM] * len(done),
            [field, field],
            (buffer(count), buffer(count), dma((2, count // BLOCK))),
            [HBM, HBM],
            input_output_aliases={6: 0, 7: 1} if done else {},
        )(partial, image, velocity, forward, second_on[i], second_off[i], *done)
    second, image = done
    return (image, second, current)


def solution(mesh):
    split = P(("groups", "slab"), None, None)
    return jax.shard_map(
        shard,
        mesh=mesh,
        in_specs=(
            split,
            split,
            split,
            P(None, ("groups", "slab"), None, None),
            P(("groups", "slab"), None),
            P(),
            P(("groups", "slab"), None),
            P(("groups", "slab")),
        ),
        out_specs=(split, split, split),
        check_vma=False,
    )
```

```python
import functools

import jax
import jax.numpy as jnp
from jax import lax
from jax.experimental import pallas as pl
from jax.experimental.pallas import tpu as pltpu
from jax.sharding import PartitionSpec as P


CAP = 4
STEPS = 2
W = (-205.0 / 72.0, 8.0 / 5.0, -1.0 / 5.0, 8.0 / 315.0, -1.0 / 560.0)
HALO = 4
ROWS = 16
BLOCK = 32
SUB = 8
UNROLL = 4
SHARE = (3, 2)
LANES = 128
F32 = jnp.float32
BF16 = jnp.bfloat16
VMEM = pl.BlockSpec(memory_space=pltpu.VMEM)
SMEM = pl.BlockSpec(memory_space=pltpu.SMEM)
HBM = pl.BlockSpec(memory_space=pltpu.HBM)


def params():
    return pltpu.CompilerParams(vmem_limit_bytes=16 << 20)


def payload_lanes(width):
    full = width // LANES * LANES
    rest = width - full
    if rest == 0:
        return HALO * full
    return HALO * full + (2 * LANES if rest * 2 <= LANES else HALO * LANES)


def depth_at(j, depth):
    odd = lax.rem(lax.axis_index("slab"), 2)
    return j + (1 - odd) * (depth - 1 - 2 * j)


def encode(u):
    t1 = u[0].astype(BF16).astype(F32)
    e1 = u[0] - t1
    t2 = (u[1] + (W[2] / W[3]) * e1).astype(BF16).astype(F32)
    t3 = u[2].astype(BF16).astype(F32)
    t0 = W[1] * e1 + W[2] * (u[1] - t2) + W[3] * (u[2] - t3) + W[4] * u[3]
    return (t0, t1, t2, t3)


def decode(t):
    t0, t1, t2, t3 = t
    return (
        t0 + W[1] * t1 + W[2] * t2 + W[3] * t3,
        W[2] * t1 + W[3] * t2 + W[4] * t3,
        W[3] * t1 + W[4] * t2,
        W[4] * t1,
    )


def put(ref, rows, t):
    width = t[0].shape[1]
    full = width // LANES * LANES
    rest = width - full
    for k in range(HALO):
        ref[rows, k * full : (k + 1) * full] = t[k][:, :full].astype(BF16)
    if rest == 0:
        return
    base = HALO * full
    if rest * 2 <= LANES:
        half = LANES // 2
        for k in range(0, HALO, 2):
            a = jnp.pad(t[k][:, full:], ((0, 0), (0, half - rest)))
            b = jnp.pad(t[k + 1][:, full:], ((0, 0), (0, half - rest)))
            ref[rows, base : base + LANES] = jnp.concatenate([a, b], axis=1).astype(BF16)
            base += LANES
    else:
        for k in range(HALO):
            tail = jnp.pad(t[k][:, full:], ((0, 0), (0, LANES - rest)))
            ref[rows, base : base + LANES] = tail.astype(BF16)
            base += LANES


def take(ref, rows, width):
    full = width // LANES * LANES
    rest = width - full
    main = [ref[rows, k * full : (k + 1) * full].astype(F32) for k in range(HALO)]
    if rest == 0:
        return main
    base = HALO * full
    tails = []
    if rest * 2 <= LANES:
        half = LANES // 2
        for _ in range(0, HALO, 2):
            both = ref[rows, base : base + LANES].astype(F32)
            tails.append(both[:, :rest])
            tails.append(pltpu.roll(both, half, 1)[:, :rest])
            base += LANES
    else:
        for _ in range(HALO):
            tails.append(ref[rows, base : base + LANES].astype(F32)[:, :rest])
            base += LANES
    return [jnp.concatenate([m, t], axis=1) for m, t in zip(main, tails)]


def row_loop(count, body):
    def step(i, carry):
        body(pl.multiple_of(i * ROWS, ROWS))
        return carry

    lax.fori_loop(0, count // ROWS, step, 0)


def row_span(width_x):
    return 1 << (width_x - 1).bit_length()


def blocks_of(first, count):
    return [(i, min(BLOCK, first + count - i)) for i in range(first, first + count, BLOCK)]


def fetch(source, buf, sems, first, count):
    copies = []
    for n, (row, size) in enumerate(blocks_of(first, count)):
        rows = pl.ds(row, size)
        copies.append(
            pltpu.make_async_copy(source.at[:, rows], buf.at[:, pl.ds(row - first, size)], sems.at[n])
        )
        copies[-1].start()
    return copies


def pack_kernel(first, with_on, now, *refs):
    refs = list(refs)
    on_ref = refs.pop(0) if with_on else None
    off_ref, buf, sems = refs
    depth = now.shape[0]
    base = 0 if with_on else first
    copies = fetch(now, buf, sems, base, buf.shape[1])

    for i, copy in enumerate(copies):
        copy.wait()

        def body(r):
            r = r + i * BLOCK
            rows = pl.ds(r, ROWS)
            u = [buf[depth_at(j, depth), rows, :] for j in range(depth)]
            if base + i * BLOCK >= first and base + i * BLOCK < first + off_ref.shape[0]:
                put(off_ref, pl.ds(r + base - first, ROWS), encode(u[::-1][:HALO]))
            if with_on:
                put(on_ref, rows, encode(u[:HALO]))

        row_loop(BLOCK, body)


def route_kernel(slabs, field, traces, weights, target, cell, out):
    depth, width_x, width_y = field
    rows = traces.shape[0]
    lane = lax.broadcasted_iota(jnp.int32, (rows, rows), 1)
    row = lax.broadcasted_iota(jnp.int32, (rows, rows), 0)
    eye = lane == row
    target_row = jnp.broadcast_to(target[...], (rows, rows))
    cell_row = jnp.broadcast_to(cell[...], (rows, rows))
    target_col = jnp.sum(jnp.where(eye, target_row, 0), axis=1, keepdims=True)
    cell_col = jnp.sum(jnp.where(eye, cell_row, 0), axis=1, keepdims=True)
    same = (target_row == target_col) & (lane < row)
    rank = jnp.sum(jnp.where(same, 1, 0), axis=1, keepdims=True)
    values = traces[...].astype(F32)
    columns = [
        jnp.sum(values * weights[s : s + 1, :].astype(F32), axis=1, keepdims=True)
        for s in range(STEPS)
    ]
    line = cell_col // width_y
    layer = line // width_x
    column = cell_col - line * width_y
    plane = (column // LANES) * depth + layer
    code = (plane * row_span(width_x) + line - layer * width_x) * LANES + column % LANES
    columns.append(code.astype(F32))
    spot = lax.broadcasted_iota(jnp.int32, (rows, LANES), 1)
    spread = jnp.zeros((rows, LANES), F32)
    for j, column in enumerate(columns):
        spread = jnp.where(spot == j * CAP + rank, column, spread)
    taker = lax.broadcasted_iota(jnp.int32, (slabs, rows), 0)
    chosen = (taker == jnp.broadcast_to(target[...], (slabs, rows))).astype(F32)
    picked = jnp.dot(
        chosen, spread, precision=lax.Precision.HIGHEST, preferred_element_type=F32
    )
    out[...] = picked.reshape(out.shape)


def tile_parts(width_y):
    return [(lo, min(lo + LANES, width_y)) for lo in range(0, width_y, LANES)]


def join(pieces, width_y):
    last = width_y - (len(pieces) - 1) * LANES
    return jnp.concatenate([*pieces[:-1], pieces[-1][:, :last]], axis=1)


def tile_rows(z, row, j, count, number):
    return pl.ds((z * (count + 2 * SUB) + SUB + row) * number + j, SUB, stride=number)


def spread(tiles, count, source, start, row, size):
    depth, _, width_y = source.shape
    parts = tile_parts(width_y)

    def body(i, carry):
        r = i * SUB
        for z in range(depth):
            for j, (lo, hi) in enumerate(parts):
                value = source[z, pl.ds(pl.multiple_of(r + start, SUB), SUB), lo:hi]
                if hi - lo < LANES:
                    value = jnp.pad(value, ((0, 0), (0, LANES - (hi - lo))))
                tiles[tile_rows(z, r + row, j, count, len(parts)), :] = value
        return carry

    lax.fori_loop(0, size // SUB, body, 0)


def clear(tiles, count, depth, number, row):
    for z in range(depth):
        for j in range(number):
            tiles[tile_rows(z, row, j, count, number), :] = jnp.zeros((SUB, LANES), F32)


def own_laplace(tiles, lap, depth, count, width_y):
    number = len(tile_parts(width_y))
    lane = lax.broadcasted_iota(jnp.int32, (SUB, LANES), 1)
    wraps = width_y % LANES == 0 or width_y % LANES > LANES - HALO
    groups = count // SUB
    unroll = max(u for u in range(1, UNROLL + 1) if groups % u == 0)

    def one(r):
        def at(z, j, shift=0):
            return tiles[tile_rows(z, r + shift, j, count, number), :]

        centre = [[at(z, j) for j in range(number)] for z in range(depth)]
        for z in range(depth):
            total = [3.0 * W[0] * centre[z][j] for j in range(number)]
            for k in range(1, HALO + 1):
                right = [pltpu.roll(c, k, 1) for c in centre[z]]
                left = [pltpu.roll(c, LANES - k, 1) for c in centre[z]]
                for j in range(number):
                    pair = at(z, j, -k) + at(z, j, k)
                    pair = pair + jnp.where(lane < k, right[j - 1] if j else 0.0, right[j])
                    if j + 1 < number or wraps:
                        side = left[j + 1] if j + 1 < number else 0.0
                        pair = pair + jnp.where(lane >= LANES - k, side, left[j])
                    else:
                        pair = pair + left[j]
                    if z - k >= 0:
                        pair = pair + centre[z - k][j]
                    if z + k < depth:
                        pair = pair + centre[z + k][j]
                    total[j] = total[j] + W[k] * pair
            for j in range(number):
                place = pl.multiple_of(r + (j * depth + z) * count, SUB)
                lap[pl.ds(place, SUB), :] = total[j]

    def step(i, carry):
        for u in range(unroll):
            one((i * unroll + u) * SUB)
        return carry

    lax.fori_loop(0, groups // unroll, step, 0)


def inject(step, got, lap, planes, first, count, width_x):
    lane = lax.broadcasted_iota(jnp.int32, (1, LANES), 1)
    span = row_span(width_x)
    shift = LANES.bit_length() - 1

    def body(i, carry):
        for slot in range(CAP):
            source = got[i, 0, step * CAP + slot]
            code = got[i, 0, STEPS * CAP + slot].astype(jnp.int32)
            line = lax.shift_right_logical(code, jnp.int32(shift))
            row = (line & (span - 1)) - first
            plane = lax.shift_right_logical(line, jnp.int32(span.bit_length() - 1))
            inside = (row >= 0) & (row < count)
            place = pl.ds(jnp.where(inside, plane * count + row, planes * count), 1)
            lap[place, :] = lap[place, :] + jnp.where(lane == (code & (LANES - 1)), source, 0.0)
        return carry

    lax.fori_loop(0, got.shape[0], body, 0)


def lap_rows(lap, z, r, depth, count, width_y):
    pieces = []
    for j in range(len(tile_parts(width_y))):
        place = pl.multiple_of((j * depth + z) * count + r, ROWS)
        pieces.append(lap[pl.ds(place, ROWS), :])
    return join(pieces, width_y)


def halo_sum(got_on, rows_on, got_off, rows_off, width_y, depth):
    near = decode(take(got_on, rows_on, width_y))
    far = decode(take(got_off, rows_off, width_y))
    out = []
    for j in range(depth):
        terms = [near[j]] if j < HALO else []
        if depth - 1 - j < HALO:
            terms.append(far[depth - 1 - j])
        out.append(functools.reduce(lambda a, b: a + b, terms) if terms else None)
    return out


def first_kernel(
    first, now, prior, velocity, got, got_on, got_off, part, on_ref, off_ref,
    tiles, lap, now_buf, prior_buf, speed_buf, sems
):
    depth, width_x, width_y = now.shape
    count = part.shape[1]
    number = len(tile_parts(width_y))
    low, high = max(first - SUB, 0), min(first + count + SUB, width_x)
    now_copies = fetch(now, now_buf, sems.at[0], low, high - low)
    prior_copies = fetch(prior, prior_buf, sems.at[1], first, count)
    speed_copies = fetch(velocity, speed_buf, sems.at[2], first, count)
    if low == first:
        clear(tiles, count, depth, number, -SUB)
    if high == first + count:
        clear(tiles, count, depth, number, count)
    for copy, (row, size) in zip(now_copies, blocks_of(low, high - low)):
        copy.wait()
        spread(tiles, count, now_buf, row - low, row - first, size)
    own_laplace(tiles, lap, depth, count, width_y)
    inject(0, got, lap, number * depth, first, count, width_x)
    for copy in prior_copies + speed_copies:
        copy.wait()

    def body(r):
        rows = pl.ds(r, ROWS)
        here = pl.ds(pl.multiple_of(r + (first - low), SUB), ROWS)
        halo = halo_sum(got_on, pl.ds(r + first, ROWS), got_off, rows, width_y, depth)
        u = []
        for j in range(depth):
            z = depth_at(j, depth)
            change = lap_rows(lap, z, r, depth, count, width_y)
            if halo[j] is not None:
                change = change + halo[j]
            value = 2.0 * now_buf[z, here, :] - prior_buf[z, rows, :]
            value = value + speed_buf[z, rows, :] * change
            part[z, rows, :] = value
            u.append(value)
        put(off_ref, rows, encode(u[::-1][:HALO]))
        put(on_ref, rows, encode(u[:HALO]))

    row_loop(count, body)


def second_local(first, starts, parts, now, velocity, forward, got, tiles, lap, bufs, sems):
    now_buf, speed_buf, *forward_bufs = bufs
    depth, width_x, width_y = now.shape
    count = now_buf.shape[1]
    number = len(tile_parts(width_y))
    low, high = max(first - SUB, 0), min(first + count + SUB, width_x)
    copies = fetch(now, now_buf, sems.at[0], first, count)
    copies += fetch(velocity, speed_buf, sems.at[1], first, count)
    for s in range(STEPS):
        copies += fetch(forward.at[s], forward_bufs[s], sems.at[2 + s], first, count)
    if low == first:
        clear(tiles, count, depth, number, -SUB)
    if high == first + count:
        clear(tiles, count, depth, number, count)
    for start, part in zip(starts, parts):
        row, end = max(low, start), min(high, start + part.shape[1])
        spread(tiles, count, part, row - start, row - first, end - row)
    own_laplace(tiles, lap, depth, count, width_y)
    inject(1, got, lap, number * depth, first, count, width_x)
    for copy in copies:
        copy.wait()
    return parts[starts.index(first)]


def send_rows(pairs, first, row, sems, n):
    writes = []
    for k, (buf, target) in enumerate(pairs):
        write = pltpu.make_async_copy(
            buf.at[:, pl.ds(row, BLOCK)], target.at[:, pl.ds(first + row, BLOCK)], sems.at[k, n]
        )
        write.start()
        writes.append(write)
    return writes


def second_kernel(first, starts, *refs):
    parts, refs = refs[: len(starts)], refs[len(starts) :]
    now, velocity, forward, got, got_on, got_off, out, image, current, tiles, lap = refs[:11]
    *bufs, out_buf, image_buf, sems, out_sems, part_sems = refs[11:]
    depth, _, width_y = now.shape
    count = out_buf.shape[1]
    writes = []
    for i, (start, part) in enumerate(zip(starts, parts)):
        write = pltpu.make_async_copy(
            part, current.at[:, pl.ds(start, part.shape[1])], part_sems.at[i]
        )
        write.start()
        writes.append(write)
    here = second_local(first, starts, parts, now, velocity, forward, got, tiles, lap, bufs, sems)
    now_buf, speed_buf, early, late = bufs
    for n, i in enumerate(range(0, count, BLOCK)):

        def body(r):
            r = r + i
            rows = pl.ds(r, ROWS)
            halo = halo_sum(got_on, rows, got_off, rows, width_y, depth)
            for j in range(depth):
                z = depth_at(j, depth)
                change = lap_rows(lap, z, r, depth, count, width_y)
                if halo[j] is not None:
                    change = change + halo[j]
                mine = here[z, rows, :]
                value = 2.0 * mine - now_buf[z, rows, :] + speed_buf[z, rows, :] * change
                out_buf[z, rows, :] = value
                image_buf[z, rows, :] = early[z, rows, :] * mine + late[z, rows, :] * value

        row_loop(BLOCK, body)
        writes += send_rows(((out_buf, out), (image_buf, image)), first, i, out_sems, n)
    for write in writes:
        write.wait()


def partial_kernel(first, starts, *refs):
    parts, refs = refs[: len(starts)], refs[len(starts) :]
    now, velocity, forward, got, out, image, speed, late, tiles, lap, now_buf, early, sems = refs
    depth, _, width_y = now.shape
    count = now_buf.shape[1]
    bufs = (now_buf, speed, early, late)
    here = second_local(first, starts, parts, now, velocity, forward, got, tiles, lap, bufs, sems)

    def body(r):
        rows = pl.ds(r, ROWS)
        for z in range(depth):
            change = lap_rows(lap, z, r, depth, count, width_y)
            mine = here[z, rows, :]
            value = 2.0 * mine - now_buf[z, rows, :] + speed[z, rows, :] * change
            out[z, rows, :] = value
            image[z, rows, :] = early[z, rows, :] * mine + late[z, rows, :] * value

    row_loop(count, body)


def last_kernel(first, partial, image_in, speed, late, got_on, got_off, *refs):
    out, image, out_buf, image_buf, sems = refs[-5:]
    depth, count, width_y = out_buf.shape
    writes = []
    for n, i in enumerate(range(0, count, BLOCK)):

        def body(r):
            rows = pl.ds(r + i, ROWS)
            halo = halo_sum(got_on, rows, got_off, rows, width_y, depth)
            for j in range(depth):
                z = depth_at(j, depth)
                extra = speed[z, rows, :] * halo[j] if halo[j] is not None else 0.0
                out_buf[z, rows, :] = partial[z, rows, :] + extra
                image_buf[z, rows, :] = image_in[z, rows, :] + late[z, rows, :] * extra

        row_loop(BLOCK, body)
        writes += send_rows(((out_buf, out), (image_buf, image)), first, i, sems, n)
    for write in writes:
        write.wait()


def shard(now, prior, velocity, forward, traces, weights, target, cell):
    now, prior, velocity, forward = (
        pltpu.with_memory_space_constraint(x, pltpu.HBM) for x in (now, prior, velocity, forward)
    )
    slabs = lax.axis_size("slab")
    depth, width_x, width_y = now.shape
    rows = traces.shape[0]
    face_lanes = payload_lanes(width_y)
    split = width_x * SHARE[0] // (sum(SHARE) * BLOCK) * BLOCK
    chunks = ((0, split), (split, width_x - split))
    starts = tuple(first for first, _ in chunks)
    field = jax.ShapeDtypeStruct(now.shape, F32)
    number = len(tile_parts(width_y))
    dma = pltpu.SemaphoreType.DMA
    on_pairs = [(k, k ^ 1) for k in range(slabs) if k ^ 1 < slabs]
    off_pairs = [(i + 1, j + 1) for i, j in on_pairs if i + 1 < slabs and j + 1 < slabs]

    def plane(count):
        return jax.ShapeDtypeStruct((count, face_lanes), BF16)

    def rows_of(count):
        return jax.ShapeDtypeStruct((depth, count, width_y), F32)

    def buffer(count):
        return pltpu.VMEM((depth, count, width_y), F32)

    def stencil(count):
        tiles = pltpu.VMEM((number * depth * (count + 2 * SUB), LANES), F32)
        lap = pltpu.VMEM((number * depth * count + SUB, LANES), F32)
        return (tiles, lap)

    def blocks(count):
        return -(-count // BLOCK)

    def call(kernel, ins, outs, scratch=(), out_spec=None, **kw):
        return pl.pallas_call(
            kernel,
            in_specs=ins,
            out_specs=out_spec or [VMEM] * len(outs),
            out_shape=outs,
            scratch_shapes=scratch,
            compiler_params=params(),
            **kw,
        )

    def swap(face, pairs):
        return lax.ppermute(face, "slab", pairs)

    got_off = []
    (face,) = call(
        functools.partial(pack_kernel, 0, False),
        [HBM],
        [plane(split)],
        (buffer(split), dma((blocks(split),))),
    )(now)
    got_off.append(swap(face, off_pairs))
    face, traces = lax.optimization_barrier((face, traces))
    (sent,) = call(
        functools.partial(route_kernel, slabs, now.shape),
        [VMEM] * 4,
        [jax.ShapeDtypeStruct((slabs, 1, LANES), F32)],
    )(traces, weights, target.reshape(1, rows), cell.reshape(1, rows))
    got = lax.all_to_all(sent, "slab", split_axis=0, concat_axis=0, tiled=True)
    sent, later = lax.optimization_barrier((sent, now))
    on_face, face = call(
        functools.partial(pack_kernel, split, True),
        [HBM],
        [plane(width_x), plane(width_x - split)],
        (buffer(width_x), dma((blocks(width_x),))),
    )(later)
    got_off.append(swap(face, off_pairs))
    got_on = swap(on_face, on_pairs)
    parts, second_on, second_off = [], [], []
    for (first, count), got_face in zip(chunks, got_off):
        part, on_face, face = call(
            functools.partial(first_kernel, first),
            [HBM] * 3 + [SMEM, VMEM, VMEM],
            [rows_of(count), plane(count), plane(count)],
            (
                *stencil(count),
                buffer(count + 2 * SUB),
                buffer(count),
                buffer(count),
                dma((3, blocks(count + 2 * SUB))),
            ),
        )(now, prior, velocity, got, got_on, got_face)
        second_off.append(swap(face, off_pairs))
        second_on.append(swap(on_face, on_pairs))
        parts.append(part)
        part, prior = lax.optimization_barrier((part, prior))
    (first, count), (last, size) = chunks
    second, image, current = call(
        functools.partial(second_kernel, first, starts),
        [VMEM] * len(parts) + [HBM] * 3 + [SMEM, VMEM, VMEM],
        [field, field, field],
        (
            *stencil(count),
            *[buffer(count)] * 6,
            dma((2 + STEPS, blocks(count))),
            dma((2, blocks(count))),
            dma((len(parts),)),
        ),
        [HBM] * 3,
    )(*parts, now, velocity, forward, got, second_on[0], second_off[0])
    partial, image_part, speed, late = call(
        functools.partial(partial_kernel, last, starts),
        [VMEM] * len(parts) + [HBM] * 3 + [SMEM],
        [rows_of(size)] * 4,
        (*stencil(size), buffer(size), buffer(size), dma((2 + STEPS, blocks(size)))),
    )(*parts, now, velocity, forward, got)
    second, image = call(
        functools.partial(last_kernel, last),
        [VMEM] * 6 + [HBM] * 2,
        [field, field],
        (buffer(size), buffer(size), dma((2, blocks(size)))),
        [HBM] * 2,
        input_output_aliases={6: 0, 7: 1},
    )(partial, image_part, speed, late, second_on[1], second_off[1], second, image)
    return (image, second, current)


def solution(mesh):
    split = P(("groups", "slab"), None, None)
    return jax.shard_map(
        shard,
        mesh=mesh,
        in_specs=(
            split,
            split,
            split,
            P(None, ("groups", "slab"), None, None),
            P(("groups", "slab"), None),
            P(),
            P(("groups", "slab"), None),
            P(("groups", "slab")),
        ),
        out_specs=(split, split, split),
        check_vma=False,
    )
```

```python
import functools

import jax
import jax.numpy as jnp
from jax import lax
from jax.experimental import pallas as pl
from jax.experimental.pallas import tpu as pltpu
from jax.sharding import PartitionSpec as P


CAP = 4
STEPS = 2
W = (-205.0 / 72.0, 8.0 / 5.0, -1.0 / 5.0, 8.0 / 315.0, -1.0 / 560.0)
HALO = 4
ROWS = 16
BLOCK = 32
SUB = 8
SHARE = (3, 2)
LANES = 128
F32 = jnp.float32
BF16 = jnp.bfloat16
VMEM = pl.BlockSpec(memory_space=pltpu.VMEM)
SMEM = pl.BlockSpec(memory_space=pltpu.SMEM)
HBM = pl.BlockSpec(memory_space=pltpu.HBM)


def params():
    return pltpu.CompilerParams(vmem_limit_bytes=16 << 20)


def payload_lanes(width):
    full = width // LANES * LANES
    rest = width - full
    if rest == 0:
        return HALO * full
    return HALO * full + (2 * LANES if rest * 2 <= LANES else HALO * LANES)


def depth_at(j, depth):
    odd = lax.rem(lax.axis_index("slab"), 2)
    return j + (1 - odd) * (depth - 1 - 2 * j)


def encode(u):
    t1 = u[0].astype(BF16).astype(F32)
    e1 = u[0] - t1
    t2 = (u[1] + (W[2] / W[3]) * e1).astype(BF16).astype(F32)
    t3 = u[2].astype(BF16).astype(F32)
    t0 = W[1] * e1 + W[2] * (u[1] - t2) + W[3] * (u[2] - t3) + W[4] * u[3]
    return (t0, t1, t2, t3)


def decode(t):
    t0, t1, t2, t3 = t
    return (
        t0 + W[1] * t1 + W[2] * t2 + W[3] * t3,
        W[2] * t1 + W[3] * t2 + W[4] * t3,
        W[3] * t1 + W[4] * t2,
        W[4] * t1,
    )


def put(ref, rows, t):
    width = t[0].shape[1]
    full = width // LANES * LANES
    rest = width - full
    for k in range(HALO):
        ref[rows, k * full : (k + 1) * full] = t[k][:, :full].astype(BF16)
    if rest == 0:
        return
    base = HALO * full
    if rest * 2 <= LANES:
        half = LANES // 2
        for k in range(0, HALO, 2):
            a = jnp.pad(t[k][:, full:], ((0, 0), (0, half - rest)))
            b = jnp.pad(t[k + 1][:, full:], ((0, 0), (0, half - rest)))
            ref[rows, base : base + LANES] = jnp.concatenate([a, b], axis=1).astype(BF16)
            base += LANES
    else:
        for k in range(HALO):
            tail = jnp.pad(t[k][:, full:], ((0, 0), (0, LANES - rest)))
            ref[rows, base : base + LANES] = tail.astype(BF16)
            base += LANES


def take(ref, rows, width):
    full = width // LANES * LANES
    rest = width - full
    main = [ref[rows, k * full : (k + 1) * full].astype(F32) for k in range(HALO)]
    if rest == 0:
        return main
    base = HALO * full
    tails = []
    if rest * 2 <= LANES:
        half = LANES // 2
        for _ in range(0, HALO, 2):
            both = ref[rows, base : base + LANES].astype(F32)
            tails.append(both[:, :rest])
            tails.append(pltpu.roll(both, half, 1)[:, :rest])
            base += LANES
    else:
        for _ in range(HALO):
            tails.append(ref[rows, base : base + LANES].astype(F32)[:, :rest])
            base += LANES
    return [jnp.concatenate([m, t], axis=1) for m, t in zip(main, tails)]


def row_loop(count, body):
    def step(i, carry):
        body(pl.multiple_of(i * ROWS, ROWS))
        return carry

    lax.fori_loop(0, count // ROWS, step, 0)


def row_span(width_x):
    return 1 << (width_x - 1).bit_length()


def blocks_of(first, count):
    return [(i, min(BLOCK, first + count - i)) for i in range(first, first + count, BLOCK)]


def fetch(source, buf, sems, first, count):
    copies = []
    for n, (row, size) in enumerate(blocks_of(first, count)):
        rows = pl.ds(row, size)
        copies.append(
            pltpu.make_async_copy(source.at[:, rows], buf.at[:, pl.ds(row - first, size)], sems.at[n])
        )
        copies[-1].start()
    return copies


def pack_kernel(first, now, off_ref, buf, sems):
    depth = now.shape[0]
    count = off_ref.shape[0]
    copies = fetch(now, buf, sems, first, count)
    for copy, (row, size) in zip(copies, blocks_of(0, count)):
        copy.wait()

        def body(r):
            rows = pl.ds(r + row, ROWS)
            u = [buf[depth_at(j, depth), rows, :] for j in range(depth)]
            put(off_ref, rows, encode(u[::-1][:HALO]))

        row_loop(size, body)


def pack_all_kernel(first, now, on_ref, off_ref, field, sems):
    depth, width_x, _ = now.shape
    copies = fetch(now, field, sems, 0, width_x)
    for copy, (row, size) in zip(copies, blocks_of(0, width_x)):
        copy.wait()

        def body(r):
            rows = pl.ds(r + row, ROWS)
            u = [field[depth_at(j, depth), rows, :] for j in range(depth)]
            if row >= first:
                put(off_ref, pl.ds(r + (row - first), ROWS), encode(u[::-1][:HALO]))
            put(on_ref, rows, encode(u[:HALO]))

        row_loop(size, body)


def route_kernel(slabs, field, traces, weights, target, cell, out):
    depth, width_x, width_y = field
    rows = traces.shape[0]
    lane = lax.broadcasted_iota(jnp.int32, (rows, rows), 1)
    row = lax.broadcasted_iota(jnp.int32, (rows, rows), 0)
    eye = lane == row
    target_row = jnp.broadcast_to(target[...], (rows, rows))
    cell_row = jnp.broadcast_to(cell[...], (rows, rows))
    target_col = jnp.sum(jnp.where(eye, target_row, 0), axis=1, keepdims=True)
    cell_col = jnp.sum(jnp.where(eye, cell_row, 0), axis=1, keepdims=True)
    same = (target_row == target_col) & (lane < row)
    rank = jnp.sum(jnp.where(same, 1, 0), axis=1, keepdims=True)
    values = traces[...].astype(F32)
    columns = [
        jnp.sum(values * weights[s : s + 1, :].astype(F32), axis=1, keepdims=True)
        for s in range(STEPS)
    ]
    line = cell_col // width_y
    layer = line // width_x
    column = cell_col - line * width_y
    plane = (column // LANES) * depth + layer
    code = (plane * row_span(width_x) + line - layer * width_x) * LANES + column % LANES
    columns.append(code.astype(F32))
    spot = lax.broadcasted_iota(jnp.int32, (rows, LANES), 1)
    spread = jnp.zeros((rows, LANES), F32)
    for j, column in enumerate(columns):
        spread = jnp.where(spot == j * CAP + rank, column, spread)
    taker = lax.broadcasted_iota(jnp.int32, (slabs, rows), 0)
    chosen = (taker == jnp.broadcast_to(target[...], (slabs, rows))).astype(F32)
    picked = jnp.dot(
        chosen, spread, precision=lax.Precision.HIGHEST, preferred_element_type=F32
    )
    out[...] = picked.reshape(out.shape)


def tile_parts(width_y):
    return [(lo, min(lo + LANES, width_y)) for lo in range(0, width_y, LANES)]


def join(pieces, width_y):
    last = width_y - (len(pieces) - 1) * LANES
    return jnp.concatenate([*pieces[:-1], pieces[-1][:, :last]], axis=1)


def tile_rows(z, row, j, count, number):
    return pl.ds((z * (count + 2 * SUB) + SUB + row) * number + j, SUB, stride=number)


def spread(tiles, count, source, start, row, size):
    depth, _, width_y = source.shape
    parts = tile_parts(width_y)

    def body(i, carry):
        r = i * SUB
        for z in range(depth):
            for j, (lo, hi) in enumerate(parts):
                value = source[z, pl.ds(pl.multiple_of(r + start, SUB), SUB), lo:hi]
                if hi - lo < LANES:
                    value = jnp.pad(value, ((0, 0), (0, LANES - (hi - lo))))
                tiles[tile_rows(z, r + row, j, count, len(parts)), :] = value
        return carry

    lax.fori_loop(0, size // SUB, body, 0)


def clear(tiles, count, depth, number, row):
    for z in range(depth):
        for j in range(number):
            tiles[tile_rows(z, row, j, count, number), :] = jnp.zeros((SUB, LANES), F32)


def add_laplace(tiles, lap, depth, count, width_y, first):
    number = len(tile_parts(width_y))
    lane = lax.broadcasted_iota(jnp.int32, (SUB, LANES), 1)
    wraps = width_y % LANES == 0 or width_y % LANES > LANES - HALO

    def one(r):
        def at(z, j, shift=0):
            return tiles[tile_rows(z, r + shift, j, count, number), :]

        centre = [[at(z, j) for j in range(number)] for z in range(depth)]
        for z in range(depth):
            places = [
                pl.ds(pl.multiple_of(r + (j * depth + z) * count, SUB), SUB) for j in range(number)
            ]
            total = [lap[places[j], :] + 3.0 * W[0] * centre[z][j] for j in range(number)]
            for k in range(1, HALO + 1):
                right = [pltpu.roll(c, k, 1) for c in centre[z]]
                left = [pltpu.roll(c, LANES - k, 1) for c in centre[z]]
                for j in range(number):
                    pair = at(z, j, -k) + at(z, j, k)
                    pair = pair + jnp.where(lane < k, right[j - 1] if j else 0.0, right[j])
                    if j + 1 < number or wraps:
                        side = left[j + 1] if j + 1 < number else 0.0
                        pair = pair + jnp.where(lane >= LANES - k, side, left[j])
                    else:
                        pair = pair + left[j]
                    if z - k >= 0:
                        pair = pair + centre[z - k][j]
                    if z + k < depth:
                        pair = pair + centre[z + k][j]
                    total[j] = total[j] + W[k] * pair
            for j in range(number):
                lap[places[j], :] = total[j]

    for u in range(0, ROWS, SUB):
        one(first + u)


def stream(count, stencil, finish):
    stencil(0)

    def step(i, carry):
        r = pl.multiple_of(i * ROWS, ROWS)
        finish(r)
        stencil(r + ROWS)
        return carry

    lax.fori_loop(0, count // ROWS - 1, step, 0)
    finish(count - ROWS)


def blank(lap):
    def body(i, carry):
        lap[pl.ds(pl.multiple_of(i * 8 * SUB, SUB), 8 * SUB), :] = jnp.zeros((8 * SUB, LANES), F32)
        return carry

    whole = lap.shape[0] // (8 * SUB)
    lax.fori_loop(0, whole, body, 0)
    rest = lap.shape[0] - whole * 8 * SUB
    lap[whole * 8 * SUB :, :] = jnp.zeros((rest, LANES), F32)


def inject(step, got, lap, planes, first, count, width_x):
    lane = lax.broadcasted_iota(jnp.int32, (1, LANES), 1)
    span = row_span(width_x)
    shift = LANES.bit_length() - 1

    def body(i, carry):
        for slot in range(CAP):
            source = got[i, 0, step * CAP + slot]
            code = got[i, 0, STEPS * CAP + slot].astype(jnp.int32)
            line = lax.shift_right_logical(code, jnp.int32(shift))
            row = (line & (span - 1)) - first
            plane = lax.shift_right_logical(line, jnp.int32(span.bit_length() - 1))
            inside = (row >= 0) & (row < count)
            place = pl.ds(jnp.where(inside, plane * count + row, planes * count), 1)
            lap[place, :] = lap[place, :] + jnp.where(lane == (code & (LANES - 1)), source, 0.0)
        return carry

    lax.fori_loop(0, got.shape[0], body, 0)


def lap_rows(lap, z, r, depth, count, width_y):
    pieces = []
    for j in range(len(tile_parts(width_y))):
        place = pl.multiple_of((j * depth + z) * count + r, ROWS)
        pieces.append(lap[pl.ds(place, ROWS), :])
    return join(pieces, width_y)


def halo_sum(got_on, rows_on, got_off, rows_off, width_y, depth):
    near = decode(take(got_on, rows_on, width_y))
    far = decode(take(got_off, rows_off, width_y))
    out = []
    for j in range(depth):
        terms = [near[j]] if j < HALO else []
        if depth - 1 - j < HALO:
            terms.append(far[depth - 1 - j])
        out.append(functools.reduce(lambda a, b: a + b, terms) if terms else None)
    return out


def prepare(step, first, count, sources, got, tiles, lap):
    depth, _, width_y = sources[0][1].shape
    width_x = sum(source.shape[1] for _, source in sources)
    number = len(tile_parts(width_y))
    low, high = max(first - SUB, 0), min(first + count + SUB, width_x)
    blank(lap)
    if low == first:
        clear(tiles, count, depth, number, -SUB)
    if high == first + count:
        clear(tiles, count, depth, number, count)
    for start, source in sources:
        row, end = max(low, start), min(high, start + source.shape[1])
        spread(tiles, count, source, row - start, row - first, end - row)
    inject(step, got, lap, number * depth, first, count, width_x)


def first_kernel(
    first, now, prior, velocity, got, got_on, got_off, part, on_ref, off_ref,
    tiles, lap, prior_buf, speed_buf, sems
):
    depth, count, width_y = part.shape
    copies = fetch(prior, prior_buf, sems.at[0], first, count)
    copies += fetch(velocity, speed_buf, sems.at[1], first, count)
    prepare(0, first, count, ((0, now),), got, tiles, lap)
    for copy in copies:
        copy.wait()

    def finish(r):
        rows = pl.ds(r, ROWS)
        whole = pl.ds(r + first, ROWS)
        halo = halo_sum(got_on, whole, got_off, rows, width_y, depth)
        u = []
        for j in range(depth):
            z = depth_at(j, depth)
            change = lap_rows(lap, z, r, depth, count, width_y)
            if halo[j] is not None:
                change = change + halo[j]
            value = 2.0 * now[z, whole, :] - prior_buf[z, rows, :]
            value = value + speed_buf[z, rows, :] * change
            part[z, rows, :] = value
            u.append(value)
        put(off_ref, rows, encode(u[::-1][:HALO]))
        put(on_ref, rows, encode(u[:HALO]))

    stream(count, lambda r: add_laplace(tiles, lap, depth, count, width_y, r), finish)


def second_fetch(first, velocity, forward, speed_buf, early, late, sems):
    count = speed_buf.shape[1]
    copies = fetch(velocity, speed_buf, sems.at[0], first, count)
    copies += fetch(forward.at[0], early, sems.at[1], first, count)
    return copies + fetch(forward.at[1], late, sems.at[2], first, count)


def send_rows(pairs, first, r, sems):
    return [
        pltpu.make_async_copy(
            buf.at[:, pl.ds(r, ROWS)], target.at[:, pl.ds(r + first, ROWS)], sems.at[k, r // ROWS]
        )
        for k, (buf, target) in enumerate(pairs)
    ]


def await_rows(pairs, first, count, sems):
    for r in range(0, count, ROWS):
        for write in send_rows(pairs, first, r, sems):
            write.wait()


def second_kernel(first, starts, *refs):
    parts, refs = refs[: len(starts)], refs[len(starts) :]
    now, velocity, forward, got, got_on, got_off, out, image, current, tiles, lap = refs[:11]
    speed, early, late, out_buf, image_buf, sems, out_sems, part_sems = refs[11:]
    depth, count, width_y = out_buf.shape
    copies = second_fetch(first, velocity, forward, speed, early, late, sems)
    writes = []
    for i, (start, part) in enumerate(zip(starts, parts)):
        write = pltpu.make_async_copy(
            part, current.at[:, pl.ds(start, part.shape[1])], part_sems.at[i]
        )
        write.start()
        writes.append(write)
    prepare(1, first, count, tuple(zip(starts, parts)), got, tiles, lap)
    for copy in copies:
        copy.wait()
    here = parts[starts.index(first)]
    pairs = ((out_buf, out), (image_buf, image))

    def finish(r):
        rows = pl.ds(r, ROWS)
        halo = halo_sum(got_on, rows, got_off, rows, width_y, depth)
        for j in range(depth):
            z = depth_at(j, depth)
            change = lap_rows(lap, z, r, depth, count, width_y)
            if halo[j] is not None:
                change = change + halo[j]
            mine = here[z, rows, :]
            value = 2.0 * mine - now[z, pl.ds(r + first, ROWS), :] + speed[z, rows, :] * change
            out_buf[z, rows, :] = value
            image_buf[z, rows, :] = early[z, rows, :] * mine + late[z, rows, :] * value
        for write in send_rows(pairs, first, r, out_sems):
            write.start()

    stream(count, lambda r: add_laplace(tiles, lap, depth, count, width_y, r), finish)
    await_rows(pairs, first, count, out_sems)
    for write in writes:
        write.wait()


def partial_kernel(first, starts, *refs):
    parts, refs = refs[: len(starts)], refs[len(starts) :]
    now, velocity, forward, got, out, image, speed, late, tiles, lap, early, sems = refs
    depth, count, width_y = out.shape
    copies = second_fetch(first, velocity, forward, speed, early, late, sems)
    prepare(1, first, count, tuple(zip(starts, parts)), got, tiles, lap)
    for copy in copies:
        copy.wait()
    here = parts[starts.index(first)]

    def finish(r):
        rows = pl.ds(r, ROWS)
        for z in range(depth):
            change = lap_rows(lap, z, r, depth, count, width_y)
            mine = here[z, rows, :]
            value = 2.0 * mine - now[z, pl.ds(r + first, ROWS), :] + speed[z, rows, :] * change
            out[z, rows, :] = value
            image[z, rows, :] = early[z, rows, :] * mine + late[z, rows, :] * value

    stream(count, lambda r: add_laplace(tiles, lap, depth, count, width_y, r), finish)


def last_kernel(first, partial, image_in, speed, late, got_on, got_off, *refs):
    out, image, out_buf, image_buf, sems = refs[-5:]
    depth, count, width_y = out_buf.shape
    pairs = ((out_buf, out), (image_buf, image))

    def body(r):
        rows = pl.ds(r, ROWS)
        halo = halo_sum(got_on, rows, got_off, rows, width_y, depth)
        for j in range(depth):
            z = depth_at(j, depth)
            extra = speed[z, rows, :] * halo[j] if halo[j] is not None else 0.0
            out_buf[z, rows, :] = partial[z, rows, :] + extra
            image_buf[z, rows, :] = image_in[z, rows, :] + late[z, rows, :] * extra
        for write in send_rows(pairs, first, r, sems):
            write.start()

    row_loop(count, body)
    await_rows(pairs, first, count, sems)


def shard(now, prior, velocity, forward, traces, weights, target, cell):
    now, prior, velocity, forward = (
        pltpu.with_memory_space_constraint(x, pltpu.HBM) for x in (now, prior, velocity, forward)
    )
    slabs = lax.axis_size("slab")
    depth, width_x, width_y = now.shape
    rows = traces.shape[0]
    face_lanes = payload_lanes(width_y)
    split = width_x * SHARE[0] // (sum(SHARE) * BLOCK) * BLOCK
    chunks = ((0, split), (split, width_x - split))
    starts = tuple(first for first, _ in chunks)
    field = jax.ShapeDtypeStruct(now.shape, F32)
    number = len(tile_parts(width_y))
    dma = pltpu.SemaphoreType.DMA
    on_pairs = [(k, k ^ 1) for k in range(slabs) if k ^ 1 < slabs]
    off_pairs = [(i + 1, j + 1) for i, j in on_pairs if i + 1 < slabs and j + 1 < slabs]

    def plane(count):
        return jax.ShapeDtypeStruct((count, face_lanes), BF16)

    def rows_of(count):
        return jax.ShapeDtypeStruct((depth, count, width_y), F32)

    def buffer(count):
        return pltpu.VMEM((depth, count, width_y), F32)

    def stencil(count):
        tiles = pltpu.VMEM((number * depth * (count + 2 * SUB), LANES), F32)
        lap = pltpu.VMEM((number * depth * count + SUB, LANES), F32)
        return (tiles, lap)

    def blocks(count):
        return -(-count // BLOCK)

    def call(kernel, ins, outs, scratch=(), out_spec=None, **kw):
        return pl.pallas_call(
            kernel,
            in_specs=ins,
            out_specs=out_spec or [VMEM] * len(outs),
            out_shape=outs,
            scratch_shapes=scratch,
            compiler_params=params(),
            **kw,
        )

    def swap(face, pairs):
        return lax.ppermute(face, "slab", pairs)

    got_off = []
    (face,) = call(
        functools.partial(pack_kernel, 0),
        [HBM],
        [plane(split)],
        (buffer(split), dma((blocks(split),))),
    )(now)
    got_off.append(swap(face, off_pairs))
    face, traces = lax.optimization_barrier((face, traces))
    (sent,) = call(
        functools.partial(route_kernel, slabs, now.shape),
        [VMEM] * 4,
        [jax.ShapeDtypeStruct((slabs, 1, LANES), F32)],
    )(traces, weights, target.reshape(1, rows), cell.reshape(1, rows))
    got = lax.all_to_all(sent, "slab", split_axis=0, concat_axis=0, tiled=True)
    sent, later = lax.optimization_barrier((sent, now))
    on_face, face, now = call(
        functools.partial(pack_all_kernel, split),
        [HBM],
        [plane(width_x), plane(width_x - split), field],
        (dma((blocks(width_x),)),),
    )(later)
    got_off.append(swap(face, off_pairs))
    got_on = swap(on_face, on_pairs)
    parts, second_on, second_off = [], [], []
    for (first, count), got_face in zip(chunks, got_off):
        part, on_face, face = call(
            functools.partial(first_kernel, first),
            [VMEM, HBM, HBM, SMEM, VMEM, VMEM],
            [rows_of(count), plane(count), plane(count)],
            (*stencil(count), buffer(count), buffer(count), dma((2, blocks(count)))),
        )(now, prior, velocity, got, got_on, got_face)
        second_off.append(swap(face, off_pairs))
        second_on.append(swap(on_face, on_pairs))
        parts.append(part)
        part, prior = lax.optimization_barrier((part, prior))
    (first, count), (last, size) = chunks
    second, image, current = call(
        functools.partial(second_kernel, first, starts),
        [VMEM] * (len(parts) + 1) + [HBM] * 2 + [SMEM, VMEM, VMEM],
        [field, field, field],
        (
            *stencil(count),
            *[buffer(count)] * 5,
            dma((3, blocks(count))),
            dma((2, count // ROWS)),
            dma((len(parts),)),
        ),
        [HBM] * 3,
    )(*parts, now, velocity, forward, got, second_on[0], second_off[0])
    partial, image_part, speed, late = call(
        functools.partial(partial_kernel, last, starts),
        [VMEM] * (len(parts) + 1) + [HBM] * 2 + [SMEM],
        [rows_of(size)] * 4,
        (*stencil(size), buffer(size), dma((3, blocks(size)))),
    )(*parts, now, velocity, forward, got)
    second, image = call(
        functools.partial(last_kernel, last),
        [VMEM] * 6 + [HBM] * 2,
        [field, field],
        (buffer(size), buffer(size), dma((2, size // ROWS))),
        [HBM] * 2,
        input_output_aliases={6: 0, 7: 1},
    )(partial, image_part, speed, late, second_on[1], second_off[1], second, image)
    return (image, second, current)


def solution(mesh):
    split = P(("groups", "slab"), None, None)
    return jax.shard_map(
        shard,
        mesh=mesh,
        in_specs=(
            split,
            split,
            split,
            P(None, ("groups", "slab"), None, None),
            P(("groups", "slab"), None),
            P(),
            P(("groups", "slab"), None),
            P(("groups", "slab")),
        ),
        out_specs=(split, split, split),
        check_vma=False,
    )
```

```python
import functools

import jax
import jax.numpy as jnp
from jax import lax
from jax.experimental import pallas as pl
from jax.experimental.pallas import tpu as pltpu
from jax.sharding import PartitionSpec as P


CAP = 4
STEPS = 2
W = (-205.0 / 72.0, 8.0 / 5.0, -1.0 / 5.0, 8.0 / 315.0, -1.0 / 560.0)
HALO = 4
ROWS = 16
BLOCK = 32
SUB = 8
UNROLL = 4
SHARE = (3, 2)
LANES = 128
F32 = jnp.float32
BF16 = jnp.bfloat16
VMEM = pl.BlockSpec(memory_space=pltpu.VMEM)
SMEM = pl.BlockSpec(memory_space=pltpu.SMEM)
HBM = pl.BlockSpec(memory_space=pltpu.HBM)


def params():
    return pltpu.CompilerParams(vmem_limit_bytes=16 << 20)


def payload_lanes(width):
    full = width // LANES * LANES
    rest = width - full
    if rest == 0:
        return HALO * full
    return HALO * full + (2 * LANES if rest * 2 <= LANES else HALO * LANES)


def depth_at(j, depth):
    odd = lax.rem(lax.axis_index("slab"), 2)
    return j + (1 - odd) * (depth - 1 - 2 * j)


def encode(u):
    t1 = u[0].astype(BF16).astype(F32)
    e1 = u[0] - t1
    t2 = (u[1] + (W[2] / W[3]) * e1).astype(BF16).astype(F32)
    t3 = u[2].astype(BF16).astype(F32)
    t0 = W[1] * e1 + W[2] * (u[1] - t2) + W[3] * (u[2] - t3) + W[4] * u[3]
    return (t0, t1, t2, t3)


def decode(t):
    t0, t1, t2, t3 = t
    return (
        t0 + W[1] * t1 + W[2] * t2 + W[3] * t3,
        W[2] * t1 + W[3] * t2 + W[4] * t3,
        W[3] * t1 + W[4] * t2,
        W[4] * t1,
    )


def put(ref, rows, t):
    width = t[0].shape[1]
    full = width // LANES * LANES
    rest = width - full
    for k in range(HALO):
        ref[rows, k * full : (k + 1) * full] = t[k][:, :full].astype(BF16)
    if rest == 0:
        return
    base = HALO * full
    if rest * 2 <= LANES:
        half = LANES // 2
        for k in range(0, HALO, 2):
            a = jnp.pad(t[k][:, full:], ((0, 0), (0, half - rest)))
            b = jnp.pad(t[k + 1][:, full:], ((0, 0), (0, half - rest)))
            ref[rows, base : base + LANES] = jnp.concatenate([a, b], axis=1).astype(BF16)
            base += LANES
    else:
        for k in range(HALO):
            tail = jnp.pad(t[k][:, full:], ((0, 0), (0, LANES - rest)))
            ref[rows, base : base + LANES] = tail.astype(BF16)
            base += LANES


def take(ref, rows, width):
    full = width // LANES * LANES
    rest = width - full
    main = [ref[rows, k * full : (k + 1) * full].astype(F32) for k in range(HALO)]
    if rest == 0:
        return main
    base = HALO * full
    tails = []
    if rest * 2 <= LANES:
        half = LANES // 2
        for _ in range(0, HALO, 2):
            both = ref[rows, base : base + LANES].astype(F32)
            tails.append(both[:, :rest])
            tails.append(pltpu.roll(both, half, 1)[:, :rest])
            base += LANES
    else:
        for _ in range(HALO):
            tails.append(ref[rows, base : base + LANES].astype(F32)[:, :rest])
            base += LANES
    return [jnp.concatenate([m, t], axis=1) for m, t in zip(main, tails)]


def row_loop(count, body):
    def step(i, carry):
        body(pl.multiple_of(i * ROWS, ROWS))
        return carry

    lax.fori_loop(0, count // ROWS, step, 0)


def row_span(width_x):
    return 1 << (width_x - 1).bit_length()


def blocks_of(first, count):
    return [(i, min(BLOCK, first + count - i)) for i in range(first, first + count, BLOCK)]


def fetch(source, buf, sems, first, count):
    copies = []
    for n, (row, size) in enumerate(blocks_of(first, count)):
        rows = pl.ds(row, size)
        copies.append(
            pltpu.make_async_copy(source.at[:, rows], buf.at[:, pl.ds(row - first, size)], sems.at[n])
        )
        copies[-1].start()
    return copies


def pack_kernel(first, now, off_ref, buf, sems):
    depth = now.shape[0]
    count = off_ref.shape[0]
    copies = fetch(now, buf, sems, first, count)
    for copy, (row, size) in zip(copies, blocks_of(0, count)):
        copy.wait()

        def body(r):
            rows = pl.ds(r + row, ROWS)
            u = [buf[depth_at(j, depth), rows, :] for j in range(depth)]
            put(off_ref, rows, encode(u[::-1][:HALO]))

        row_loop(size, body)


def pack_both_kernel(first, now, on_ref, off_ref, buf, sems):
    depth, width_x, _ = now.shape
    copies = fetch(now, buf, sems, 0, width_x)
    for copy, (row, size) in zip(copies, blocks_of(0, width_x)):
        copy.wait()

        def body(r):
            rows = pl.ds(r + row, ROWS)
            u = [buf[depth_at(j, depth), rows, :] for j in range(depth)]
            if row >= first:
                put(off_ref, pl.ds(r + (row - first), ROWS), encode(u[::-1][:HALO]))
            else:
                put(on_ref, rows, encode(u[:HALO]))

        row_loop(size, body)


def pack_on_kernel(field, on_ref):
    depth = field.shape[0]

    def body(r):
        u = [field[depth_at(j, depth), pl.ds(r + SUB, ROWS), :] for j in range(depth)]
        put(on_ref, pl.ds(r, ROWS), encode(u[:HALO]))

    row_loop(on_ref.shape[0], body)


def route_kernel(slabs, field, traces, weights, target, cell, out):
    depth, width_x, width_y = field
    rows = traces.shape[0]
    lane = lax.broadcasted_iota(jnp.int32, (rows, rows), 1)
    row = lax.broadcasted_iota(jnp.int32, (rows, rows), 0)
    eye = lane == row
    target_row = jnp.broadcast_to(target[...], (rows, rows))
    cell_row = jnp.broadcast_to(cell[...], (rows, rows))
    target_col = jnp.sum(jnp.where(eye, target_row, 0), axis=1, keepdims=True)
    cell_col = jnp.sum(jnp.where(eye, cell_row, 0), axis=1, keepdims=True)
    same = (target_row == target_col) & (lane < row)
    rank = jnp.sum(jnp.where(same, 1, 0), axis=1, keepdims=True)
    values = traces[...].astype(F32)
    columns = [
        jnp.sum(values * weights[s : s + 1, :].astype(F32), axis=1, keepdims=True)
        for s in range(STEPS)
    ]
    line = cell_col // width_y
    layer = line // width_x
    column = cell_col - line * width_y
    plane = (column // LANES) * depth + layer
    code = (plane * row_span(width_x) + line - layer * width_x) * LANES + column % LANES
    columns.append(code.astype(F32))
    spot = lax.broadcasted_iota(jnp.int32, (rows, LANES), 1)
    spread = jnp.zeros((rows, LANES), F32)
    for j, column in enumerate(columns):
        spread = jnp.where(spot == j * CAP + rank, column, spread)
    taker = lax.broadcasted_iota(jnp.int32, (slabs, rows), 0)
    chosen = (taker == jnp.broadcast_to(target[...], (slabs, rows))).astype(F32)
    picked = jnp.dot(
        chosen, spread, precision=lax.Precision.HIGHEST, preferred_element_type=F32
    )
    out[...] = picked.reshape(out.shape)


def tile_parts(width_y):
    return [(lo, min(lo + LANES, width_y)) for lo in range(0, width_y + HALO, LANES)]


def join(pieces, width_y):
    last = width_y - (len(pieces) - 1) * LANES
    return jnp.concatenate([*pieces[:-1], pieces[-1][:, :last]], axis=1)


def tile_rows(z, row, j, count, number):
    return pl.ds((z * (count + 2 * SUB) + SUB + row) * number + j, SUB, stride=number)


def spread(tiles, count, source, start, row, size):
    depth, _, width_y = source.shape
    parts = tile_parts(width_y)

    def body(i, carry):
        r = i * SUB
        for z in range(depth):
            for j, (lo, hi) in enumerate(parts):
                if hi > lo:
                    value = source[z, pl.ds(pl.multiple_of(r + start, SUB), SUB), lo:hi]
                    if hi - lo < LANES:
                        value = jnp.pad(value, ((0, 0), (0, LANES - (hi - lo))))
                else:
                    value = jnp.zeros((SUB, LANES), F32)
                tiles[tile_rows(z, r + row, j, count, len(parts)), :] = value
        return carry

    lax.fori_loop(0, size // SUB, body, 0)


def clear(tiles, count, depth, number, row):
    for z in range(depth):
        for j in range(number):
            tiles[tile_rows(z, row, j, count, number), :] = jnp.zeros((SUB, LANES), F32)


def add_laplace(tiles, lap, depth, count, width_y):
    number = len(tile_parts(width_y))
    lane = lax.broadcasted_iota(jnp.int32, (SUB, LANES), 1)
    groups = count // SUB
    unroll = max(u for u in range(1, UNROLL + 1) if groups % u == 0)
    middle = 3.0 * W[0] - 2.0 * W[4]

    def both(values, k):
        right = [pltpu.roll(v, k, 1) for v in values]
        left = [pltpu.roll(v, LANES - k, 1) for v in values]
        return [
            jnp.where(lane < k, right[j - 1], right[j])
            + jnp.where(lane >= LANES - k, left[(j + 1) % number], left[j])
            for j in range(number)
        ]

    def one(r):
        def at(z, j, shift=0):
            return tiles[tile_rows(z, r + shift, j, count, number), :]

        centre = [[at(z, j) for j in range(number)] for z in range(depth)]
        for z in range(depth):
            places = [
                pl.ds(pl.multiple_of(r + (j * depth + z) * count, SUB), SUB) for j in range(number)
            ]
            once, twice = both(centre[z], 1), both(centre[z], 2)
            inner = [
                W[2] * centre[z][j] + W[3] * once[j] + W[4] * twice[j] for j in range(number)
            ]
            outer = both(inner, 2)
            for j in range(number):
                total = lap[places[j], :] + middle * centre[z][j]
                total = total + (W[1] - W[3]) * once[j] + outer[j]
                for k in range(1, HALO + 1):
                    pair = at(z, j, -k) + at(z, j, k)
                    if z - k >= 0:
                        pair = pair + centre[z - k][j]
                    if z + k < depth:
                        pair = pair + centre[z + k][j]
                    total = total + W[k] * pair
                lap[places[j], :] = total

    def step(i, carry):
        for u in range(unroll):
            one((i * unroll + u) * SUB)
        return carry

    lax.fori_loop(0, groups // unroll, step, 0)


def blank(lap):
    def body(i, carry):
        lap[pl.ds(pl.multiple_of(i * 8 * SUB, SUB), 8 * SUB), :] = jnp.zeros((8 * SUB, LANES), F32)
        return carry

    whole = lap.shape[0] // (8 * SUB)
    lax.fori_loop(0, whole, body, 0)
    rest = lap.shape[0] - whole * 8 * SUB
    lap[whole * 8 * SUB :, :] = jnp.zeros((rest, LANES), F32)


def inject(step, got, lap, planes, first, count, width_x):
    lane = lax.broadcasted_iota(jnp.int32, (1, LANES), 1)
    span = row_span(width_x)
    shift = LANES.bit_length() - 1

    def body(i, carry):
        for slot in range(CAP):
            source = got[i, 0, step * CAP + slot]
            code = got[i, 0, STEPS * CAP + slot].astype(jnp.int32)
            line = lax.shift_right_logical(code, jnp.int32(shift))
            row = (line & (span - 1)) - first
            plane = lax.shift_right_logical(line, jnp.int32(span.bit_length() - 1))
            inside = (row >= 0) & (row < count)
            place = pl.ds(jnp.where(inside, plane * count + row, planes * count), 1)
            lap[place, :] = lap[place, :] + jnp.where(lane == (code & (LANES - 1)), source, 0.0)
        return carry

    lax.fori_loop(0, got.shape[0], body, 0)


def lap_rows(lap, z, r, depth, count, width_y):
    pieces = []
    for j in range(-(-width_y // LANES)):
        place = pl.multiple_of((j * depth + z) * count + r, ROWS)
        pieces.append(lap[pl.ds(place, ROWS), :])
    return join(pieces, width_y)


def halo_sum(got_on, rows_on, got_off, rows_off, width_y, depth):
    near = decode(take(got_on, rows_on, width_y))
    far = decode(take(got_off, rows_off, width_y))
    out = []
    for j in range(depth):
        terms = [near[j]] if j < HALO else []
        if depth - 1 - j < HALO:
            terms.append(far[depth - 1 - j])
        out.append(functools.reduce(lambda a, b: a + b, terms) if terms else None)
    return out


def prepare(step, first, count, width_x, depth, width_y, got, tiles, lap):
    number = len(tile_parts(width_y))
    blank(lap)
    if first == 0:
        clear(tiles, count, depth, number, -SUB)
    if first + count == width_x:
        clear(tiles, count, depth, number, count)
    inject(step, got, lap, number * depth, first, count, width_x)


def first_kernel(first, width_x, more, now, prior, velocity, got, got_on, got_off, *refs):
    part, on_ref, off_ref = refs[:3]
    following = refs[3] if more else None
    tiles, lap, now_buf, prior_buf, speed_buf, sems = refs[-6:]
    depth, count, width_y = part.shape
    low, high = max(first - SUB, 0), min(first + count + SUB, width_x)
    now_copies = fetch(now, now_buf, sems.at[0], low, high - low) if more else []
    copies = fetch(prior, prior_buf, sems.at[1], first, count)
    copies += fetch(velocity, speed_buf, sems.at[2], first, count)
    if more:
        copies += fetch(now, following, sems.at[3], width_x - more, more)
    prepare(0, first, count, width_x, depth, width_y, got, tiles, lap)
    for copy, (row, size) in zip(now_copies, blocks_of(low, high - low)):
        copy.wait()
        spread(tiles, count, now_buf, row - low, row - first, size)
    held = now_buf if more else now
    if not more:
        spread(tiles, count, now, 0, low - first, high - low)
    add_laplace(tiles, lap, depth, count, width_y)
    for copy in copies:
        copy.wait()

    def body(r):
        rows = pl.ds(r, ROWS)
        here = pl.ds(pl.multiple_of(r + (first - low), SUB), ROWS)
        halo = halo_sum(got_on, rows, got_off, rows, width_y, depth)
        u = []
        for j in range(depth):
            z = depth_at(j, depth)
            change = lap_rows(lap, z, r, depth, count, width_y)
            if halo[j] is not None:
                change = change + halo[j]
            value = 2.0 * held[z, here, :] - prior_buf[z, rows, :]
            value = value + speed_buf[z, rows, :] * change
            part[z, rows, :] = value
            u.append(value)
        put(off_ref, rows, encode(u[::-1][:HALO]))
        put(on_ref, rows, encode(u[:HALO]))

    row_loop(count, body)


def second_local(first, starts, parts, now, velocity, forward, got, tiles, lap, bufs, sems):
    now_buf, speed_buf, *forward_bufs = bufs
    depth, width_x, width_y = now.shape
    count = now_buf.shape[1]
    low, high = max(first - SUB, 0), min(first + count + SUB, width_x)
    copies = fetch(now, now_buf, sems.at[0], first, count)
    copies += fetch(velocity, speed_buf, sems.at[1], first, count)
    for s in range(STEPS):
        copies += fetch(forward.at[s], forward_bufs[s], sems.at[2 + s], first, count)
    prepare(1, first, count, width_x, depth, width_y, got, tiles, lap)
    for start, part in zip(starts, parts):
        row, end = max(low, start), min(high, start + part.shape[1])
        spread(tiles, count, part, row - start, row - first, end - row)
    add_laplace(tiles, lap, depth, count, width_y)
    for copy in copies:
        copy.wait()
    return parts[starts.index(first)]


def send_rows(pairs, first, row, sems, n):
    writes = []
    for k, (buf, target) in enumerate(pairs):
        write = pltpu.make_async_copy(
            buf.at[:, pl.ds(row, BLOCK)], target.at[:, pl.ds(first + row, BLOCK)], sems.at[k, n]
        )
        write.start()
        writes.append(write)
    return writes


def second_kernel(first, starts, *refs):
    parts, refs = refs[: len(starts)], refs[len(starts) :]
    now, velocity, forward, got, got_on, got_off, out, image, current, tiles, lap = refs[:11]
    *bufs, out_buf, image_buf, sems, out_sems, part_sems = refs[11:]
    depth, _, width_y = now.shape
    count = out_buf.shape[1]
    writes = []
    for i, (start, part) in enumerate(zip(starts, parts)):
        write = pltpu.make_async_copy(
            part, current.at[:, pl.ds(start, part.shape[1])], part_sems.at[i]
        )
        write.start()
        writes.append(write)
    here = second_local(first, starts, parts, now, velocity, forward, got, tiles, lap, bufs, sems)
    now_buf, speed_buf, early, late = bufs
    for n, i in enumerate(range(0, count, BLOCK)):

        def body(r):
            r = r + i
            rows = pl.ds(r, ROWS)
            halo = halo_sum(got_on, rows, got_off, rows, width_y, depth)
            for j in range(depth):
                z = depth_at(j, depth)
                change = lap_rows(lap, z, r, depth, count, width_y)
                if halo[j] is not None:
                    change = change + halo[j]
                mine = here[z, rows, :]
                value = 2.0 * mine - now_buf[z, rows, :] + speed_buf[z, rows, :] * change
                out_buf[z, rows, :] = value
                image_buf[z, rows, :] = early[z, rows, :] * mine + late[z, rows, :] * value

        row_loop(BLOCK, body)
        writes += send_rows(((out_buf, out), (image_buf, image)), first, i, out_sems, n)
    for write in writes:
        write.wait()


def partial_kernel(first, starts, *refs):
    parts, refs = refs[: len(starts)], refs[len(starts) :]
    now, velocity, forward, got, out, image, speed, late, tiles, lap, now_buf, early, sems = refs
    depth, _, width_y = now.shape
    count = now_buf.shape[1]
    bufs = (now_buf, speed, early, late)
    here = second_local(first, starts, parts, now, velocity, forward, got, tiles, lap, bufs, sems)

    def body(r):
        rows = pl.ds(r, ROWS)
        for z in range(depth):
            change = lap_rows(lap, z, r, depth, count, width_y)
            mine = here[z, rows, :]
            value = 2.0 * mine - now_buf[z, rows, :] + speed[z, rows, :] * change
            out[z, rows, :] = value
            image[z, rows, :] = early[z, rows, :] * mine + late[z, rows, :] * value

    row_loop(count, body)


def last_kernel(first, partial, image_in, speed, late, got_on, got_off, *refs):
    out, image, out_buf, image_buf, sems = refs[-5:]
    depth, count, width_y = out_buf.shape
    writes = []
    for n, i in enumerate(range(0, count, BLOCK)):

        def body(r):
            rows = pl.ds(r + i, ROWS)
            halo = halo_sum(got_on, rows, got_off, rows, width_y, depth)
            for j in range(depth):
                z = depth_at(j, depth)
                extra = speed[z, rows, :] * halo[j] if halo[j] is not None else 0.0
                out_buf[z, rows, :] = partial[z, rows, :] + extra
                image_buf[z, rows, :] = image_in[z, rows, :] + late[z, rows, :] * extra

        row_loop(BLOCK, body)
        writes += send_rows(((out_buf, out), (image_buf, image)), first, i, sems, n)
    for write in writes:
        write.wait()


def shard(now, prior, velocity, forward, traces, weights, target, cell):
    now, prior, velocity, forward = (
        pltpu.with_memory_space_constraint(x, pltpu.HBM) for x in (now, prior, velocity, forward)
    )
    slabs = lax.axis_size("slab")
    depth, width_x, width_y = now.shape
    rows = traces.shape[0]
    face_lanes = payload_lanes(width_y)
    split = width_x * SHARE[0] // (sum(SHARE) * BLOCK) * BLOCK
    chunks = ((0, split), (split, width_x - split))
    starts = tuple(first for first, _ in chunks)
    field = jax.ShapeDtypeStruct(now.shape, F32)
    number = len(tile_parts(width_y))
    dma = pltpu.SemaphoreType.DMA
    on_pairs = [(k, k ^ 1) for k in range(slabs) if k ^ 1 < slabs]
    off_pairs = [(i + 1, j + 1) for i, j in on_pairs if i + 1 < slabs and j + 1 < slabs]

    def plane(count):
        return jax.ShapeDtypeStruct((count, face_lanes), BF16)

    def rows_of(count):
        return jax.ShapeDtypeStruct((depth, count, width_y), F32)

    def buffer(count):
        return pltpu.VMEM((depth, count, width_y), F32)

    def stencil(count):
        tiles = pltpu.VMEM((number * depth * (count + 2 * SUB), LANES), F32)
        lap = pltpu.VMEM((number * depth * count + SUB, LANES), F32)
        return (tiles, lap)

    def blocks(count):
        return -(-count // BLOCK)

    def call(kernel, ins, outs, scratch=(), out_spec=None, **kw):
        return pl.pallas_call(
            kernel,
            in_specs=ins,
            out_specs=out_spec or [VMEM] * len(outs),
            out_shape=outs,
            scratch_shapes=scratch,
            compiler_params=params(),
            **kw,
        )

    def swap(face, pairs):
        return lax.ppermute(face, "slab", pairs)

    got_off = []
    (face,) = call(
        functools.partial(pack_kernel, 0),
        [HBM],
        [plane(split)],
        (buffer(split), dma((blocks(split),))),
    )(now)
    got_off.append(swap(face, off_pairs))
    face, traces = lax.optimization_barrier((face, traces))
    (sent,) = call(
        functools.partial(route_kernel, slabs, now.shape),
        [VMEM] * 4,
        [jax.ShapeDtypeStruct((slabs, 1, LANES), F32)],
    )(traces, weights, target.reshape(1, rows), cell.reshape(1, rows))
    got = lax.all_to_all(sent, "slab", split_axis=0, concat_axis=0, tiled=True)
    sent, later = lax.optimization_barrier((sent, now))
    on_face, face = call(
        functools.partial(pack_both_kernel, split),
        [HBM],
        [plane(split), plane(width_x - split)],
        (buffer(width_x), dma((blocks(width_x),))),
    )(later)
    got_off.append(swap(face, off_pairs))
    got_on = swap(on_face, on_pairs)
    parts, second_on, second_off = [], [], []
    more = width_x - split + SUB
    held = now
    for i, (first, count) in enumerate(chunks):
        part, on_face, face, *following = call(
            functools.partial(first_kernel, first, width_x, 0 if i else more),
            [VMEM if i else HBM, HBM, HBM, SMEM, VMEM, VMEM],
            [rows_of(count), plane(count), plane(count)] + ([] if i else [rows_of(more)]),
            (
                *stencil(count),
                buffer(SUB if i else count + SUB),
                buffer(count),
                buffer(count),
                dma((4, blocks(width_x))),
            ),
        )(held, prior, velocity, got, got_on, got_off[i])
        second_off.append(swap(face, off_pairs))
        second_on.append(swap(on_face, on_pairs))
        parts.append(part)
        if i == 0:
            (held,) = following
            part, held = lax.optimization_barrier((part, held))
            (on_face,) = call(pack_on_kernel, [VMEM], [plane(width_x - split)])(held)
            got_on = swap(on_face, on_pairs)
    (first, count), (last, size) = chunks
    second, image, current = call(
        functools.partial(second_kernel, first, starts),
        [VMEM] * len(parts) + [HBM] * 3 + [SMEM, VMEM, VMEM],
        [field, field, field],
        (
            *stencil(count),
            *[buffer(count)] * 6,
            dma((2 + STEPS, blocks(count))),
            dma((2, blocks(count))),
            dma((len(parts),)),
        ),
        [HBM] * 3,
    )(*parts, now, velocity, forward, got, second_on[0], second_off[0])
    partial, image_part, speed, late = call(
        functools.partial(partial_kernel, last, starts),
        [VMEM] * len(parts) + [HBM] * 3 + [SMEM],
        [rows_of(size)] * 4,
        (*stencil(size), buffer(size), buffer(size), dma((2 + STEPS, blocks(size)))),
    )(*parts, now, velocity, forward, got)
    second, image = call(
        functools.partial(last_kernel, last),
        [VMEM] * 6 + [HBM] * 2,
        [field, field],
        (buffer(size), buffer(size), dma((2, blocks(size)))),
        [HBM] * 2,
        input_output_aliases={6: 0, 7: 1},
    )(partial, image_part, speed, late, second_on[1], second_off[1], second, image)
    return (image, second, current)


def solution(mesh):
    split = P(("groups", "slab"), None, None)
    return jax.shard_map(
        shard,
        mesh=mesh,
        in_specs=(
            split,
            split,
            split,
            P(None, ("groups", "slab"), None, None),
            P(("groups", "slab"), None),
            P(),
            P(("groups", "slab"), None),
            P(("groups", "slab")),
        ),
        out_specs=(split, split, split),
        check_vma=False,
    )
```

```python
import functools

import jax
import jax.numpy as jnp
import numpy as np
from jax import lax
from jax.experimental import pallas as pl
from jax.experimental.pallas import tpu as pltpu
from jax.sharding import PartitionSpec as P


CAP = 4
STEPS = 2
W = (-205.0 / 72.0, 8.0 / 5.0, -1.0 / 5.0, 8.0 / 315.0, -1.0 / 560.0)
HALO = 4
ROWS = 16
BLOCK = 32
SUB = 8
UNROLL = 4
SHARE = (3, 2)
LANES = 128
F32 = jnp.float32
BF16 = jnp.bfloat16
VMEM = pl.BlockSpec(memory_space=pltpu.VMEM)
SMEM = pl.BlockSpec(memory_space=pltpu.SMEM)
HBM = pl.BlockSpec(memory_space=pltpu.HBM)


def params():
    return pltpu.CompilerParams(vmem_limit_bytes=20 << 20)


def payload_lanes(width):
    full = width // LANES * LANES
    rest = width - full
    if rest == 0:
        return HALO * full
    return HALO * full + (2 * LANES if rest * 2 <= LANES else HALO * LANES)


def depth_at(j, depth):
    odd = lax.rem(lax.axis_index("slab"), 2)
    return j + (1 - odd) * (depth - 1 - 2 * j)


def encode(u):
    t1 = u[0].astype(BF16).astype(F32)
    e1 = u[0] - t1
    t2 = (u[1] + (W[2] / W[3]) * e1).astype(BF16).astype(F32)
    t3 = u[2].astype(BF16).astype(F32)
    t0 = W[1] * e1 + W[2] * (u[1] - t2) + W[3] * (u[2] - t3) + W[4] * u[3]
    return (t0, t1, t2, t3)


def decode(t):
    t0, t1, t2, t3 = t
    return (
        t0 + W[1] * t1 + W[2] * t2 + W[3] * t3,
        W[2] * t1 + W[3] * t2 + W[4] * t3,
        W[3] * t1 + W[4] * t2,
        W[4] * t1,
    )


def put(ref, rows, t):
    width = t[0].shape[1]
    full = width // LANES * LANES
    rest = width - full
    for k in range(HALO):
        ref[rows, k * full : (k + 1) * full] = t[k][:, :full].astype(BF16)
    if rest == 0:
        return
    base = HALO * full
    if rest * 2 <= LANES:
        half = LANES // 2
        for k in range(0, HALO, 2):
            a = jnp.pad(t[k][:, full:], ((0, 0), (0, half - rest)))
            b = jnp.pad(t[k + 1][:, full:], ((0, 0), (0, half - rest)))
            ref[rows, base : base + LANES] = jnp.concatenate([a, b], axis=1).astype(BF16)
            base += LANES
    else:
        for k in range(HALO):
            tail = jnp.pad(t[k][:, full:], ((0, 0), (0, LANES - rest)))
            ref[rows, base : base + LANES] = tail.astype(BF16)
            base += LANES


def take(ref, rows, width):
    full = width // LANES * LANES
    rest = width - full
    main = [ref[rows, k * full : (k + 1) * full].astype(F32) for k in range(HALO)]
    if rest == 0:
        return main
    base = HALO * full
    tails = []
    if rest * 2 <= LANES:
        half = LANES // 2
        for _ in range(0, HALO, 2):
            both = ref[rows, base : base + LANES].astype(F32)
            tails.append(both[:, :rest])
            tails.append(pltpu.roll(both, half, 1)[:, :rest])
            base += LANES
    else:
        for _ in range(HALO):
            tails.append(ref[rows, base : base + LANES].astype(F32)[:, :rest])
            base += LANES
    return [jnp.concatenate([m, t], axis=1) for m, t in zip(main, tails)]


def row_loop(count, body):
    def step(i, carry):
        body(pl.multiple_of(i * ROWS, ROWS))
        return carry

    lax.fori_loop(0, count // ROWS, step, 0)


def row_span(width_x):
    return 1 << (width_x - 1).bit_length()


def blocks_of(first, count):
    return [(i, min(BLOCK, first + count - i)) for i in range(first, first + count, BLOCK)]


def fetch(source, buf, sems, first, count):
    copies = []
    for n, (row, size) in enumerate(blocks_of(first, count)):
        rows = pl.ds(row, size)
        copies.append(
            pltpu.make_async_copy(source.at[:, rows], buf.at[:, pl.ds(row - first, size)], sems.at[n])
        )
        copies[-1].start()
    return copies


def pack_kernel(first, with_on, now, *refs):
    refs = list(refs)
    on_ref = refs.pop(0) if with_on else None
    off_ref, buf, sems = refs
    depth = now.shape[0]
    base = 0 if with_on else first
    copies = fetch(now, buf, sems, base, buf.shape[1])

    for i, copy in enumerate(copies):
        copy.wait()

        def body(r):
            r = r + i * BLOCK
            rows = pl.ds(r, ROWS)
            u = [buf[depth_at(j, depth), rows, :] for j in range(depth)]
            if base + i * BLOCK >= first and base + i * BLOCK < first + off_ref.shape[0]:
                put(off_ref, pl.ds(r + base - first, ROWS), encode(u[::-1][:HALO]))
            if with_on:
                put(on_ref, rows, encode(u[:HALO]))

        row_loop(BLOCK, body)


def route_kernel(slabs, field, traces, weights, target, cell, out):
    depth, width_x, width_y = field
    rows = traces.shape[0]
    lane = lax.broadcasted_iota(jnp.int32, (rows, rows), 1)
    row = lax.broadcasted_iota(jnp.int32, (rows, rows), 0)
    eye = lane == row
    target_row = jnp.broadcast_to(target[...], (rows, rows))
    cell_row = jnp.broadcast_to(cell[...], (rows, rows))
    target_col = jnp.sum(jnp.where(eye, target_row, 0), axis=1, keepdims=True)
    cell_col = jnp.sum(jnp.where(eye, cell_row, 0), axis=1, keepdims=True)
    same = (target_row == target_col) & (lane < row)
    rank = jnp.sum(jnp.where(same, 1, 0), axis=1, keepdims=True)
    values = traces[...].astype(F32)
    columns = [
        jnp.sum(values * weights[s : s + 1, :].astype(F32), axis=1, keepdims=True)
        for s in range(STEPS)
    ]
    line = cell_col // width_y
    layer = line // width_x
    column = cell_col - line * width_y
    plane = (column // LANES) * depth + layer
    code = (plane * row_span(width_x) + line - layer * width_x) * LANES + column % LANES
    columns.append(code.astype(F32))
    spot = lax.broadcasted_iota(jnp.int32, (rows, LANES), 1)
    spread = jnp.zeros((rows, LANES), F32)
    for j, column in enumerate(columns):
        spread = jnp.where(spot == j * CAP + rank, column, spread)
    taker = lax.broadcasted_iota(jnp.int32, (slabs, rows), 0)
    chosen = (taker == jnp.broadcast_to(target[...], (slabs, rows))).astype(F32)
    picked = jnp.dot(
        chosen, spread, precision=lax.Precision.HIGHEST, preferred_element_type=F32
    )
    out[...] = picked.reshape(out.shape)


def tile_parts(width_y):
    return [(lo, min(lo + LANES, width_y)) for lo in range(0, width_y + HALO, LANES)]


def join(pieces, width_y):
    last = width_y - (len(pieces) - 1) * LANES
    return jnp.concatenate([*pieces[:-1], pieces[-1][:, :last]], axis=1)


def tile_rows(z, row, j, count, number):
    return pl.ds((z * (count + 2 * SUB) + SUB + row) * number + j, SUB, stride=number)


def spread(tiles, count, source, start, row, size):
    depth, _, width_y = source.shape
    parts = tile_parts(width_y)

    def body(i, carry):
        r = i * SUB
        for z in range(depth):
            for j, (lo, hi) in enumerate(parts):
                if hi > lo:
                    value = source[z, pl.ds(pl.multiple_of(r + start, SUB), SUB), lo:hi]
                    if hi - lo < LANES:
                        value = jnp.pad(value, ((0, 0), (0, LANES - (hi - lo))))
                else:
                    value = jnp.zeros((SUB, LANES), F32)
                tiles[tile_rows(z, r + row, j, count, len(parts)), :] = value
        return carry

    lax.fori_loop(0, size // SUB, body, 0)


def clear(tiles, count, depth, number, row):
    for z in range(depth):
        for j in range(number):
            tiles[tile_rows(z, row, j, count, number), :] = jnp.zeros((SUB, LANES), F32)


def band(width_y):
    number = len(tile_parts(width_y))
    spot = np.arange(number * LANES)
    away = np.abs(spot[:, None] - spot[None, :])
    inside = (spot[:, None] < width_y) & (spot[None, :] < width_y)
    whole = np.zeros(away.shape, np.float32)
    for k in range(1, HALO + 1):
        whole[(away == k) & inside] = W[k]
    out = []
    for w in range(number - 1):
        part = whole[w * LANES : (w + 2) * LANES, w * LANES : (w + 2) * LANES].copy()
        if w:
            part[:LANES, :LANES] = 0.0
        high = part.astype(BF16)
        out.append([high, (part - high.astype(np.float32)).astype(BF16)])
    return np.array(out)


def halve(high, low, source, start, count):
    depth, _, width_y = source.shape
    extra = high.shape[1] - width_y

    def body(r):
        for z in range(depth):
            value = source[z, pl.ds(pl.multiple_of(r + start, SUB), ROWS), :]
            value = jnp.pad(value, ((0, 0), (0, extra)))
            top = value.astype(BF16)
            into = pl.ds(pl.multiple_of(r + z * count, ROWS), ROWS)
            high[into, :] = top
            low[into, :] = (value - top.astype(F32)).astype(BF16)

    row_loop(count, body)


def add_lanes(high, low, weights, lap):
    lines = high.shape[0]
    size = lines // 2

    def product(x, y):
        return jnp.dot(x, y, preferred_element_type=F32)

    def step(i, carry):
        rows = pl.ds(pl.multiple_of(i * size, ROWS), size)
        for w in range(weights.shape[0]):
            window = slice(w * LANES, (w + 2) * LANES)
            x, y = high[rows, window], low[rows, window]
            total = product(x, weights[w, 0]) + product(y, weights[w, 0])
            total = total + product(x, weights[w, 1])
            for q in range(2):
                into = pl.ds(pl.multiple_of(i * size + (w + q) * lines, ROWS), size)
                lap[into, :] = lap[into, :] + total[:, q * LANES : (q + 1) * LANES]
        return carry

    lax.fori_loop(0, 2, step, 0)


def add_rows(tiles, lap, depth, count, number):
    groups = count // SUB
    unroll = max(u for u in range(1, UNROLL + 1) if groups % u == 0)

    def one(r):
        def at(z, j, shift=0):
            return tiles[tile_rows(z, r + shift, j, count, number), :]

        centre = [[at(z, j) for j in range(number)] for z in range(depth)]
        for z in range(depth):
            for j in range(number):
                place = pl.ds(pl.multiple_of(r + (j * depth + z) * count, SUB), SUB)
                total = lap[place, :] + 3.0 * W[0] * centre[z][j]
                for k in range(1, HALO + 1):
                    pair = at(z, j, -k) + at(z, j, k)
                    if z - k >= 0:
                        pair = pair + centre[z - k][j]
                    if z + k < depth:
                        pair = pair + centre[z + k][j]
                    total = total + W[k] * pair
                lap[place, :] = total

    def step(i, carry):
        for u in range(unroll):
            one((i * unroll + u) * SUB)
        return carry

    lax.fori_loop(0, groups // unroll, step, 0)


def blank(lap):
    def body(i, carry):
        lap[pl.ds(pl.multiple_of(i * 8 * SUB, SUB), 8 * SUB), :] = jnp.zeros((8 * SUB, LANES), F32)
        return carry

    whole = lap.shape[0] // (8 * SUB)
    lax.fori_loop(0, whole, body, 0)
    rest = lap.shape[0] - whole * 8 * SUB
    lap[whole * 8 * SUB :, :] = jnp.zeros((rest, LANES), F32)


def inject(step, got, lap, planes, first, count, width_x):
    lane = lax.broadcasted_iota(jnp.int32, (1, LANES), 1)
    span = row_span(width_x)
    shift = LANES.bit_length() - 1

    def body(i, carry):
        for slot in range(CAP):
            source = got[i, 0, step * CAP + slot]
            code = got[i, 0, STEPS * CAP + slot].astype(jnp.int32)
            line = lax.shift_right_logical(code, jnp.int32(shift))
            row = (line & (span - 1)) - first
            plane = lax.shift_right_logical(line, jnp.int32(span.bit_length() - 1))
            inside = (row >= 0) & (row < count)
            place = pl.ds(jnp.where(inside, plane * count + row, planes * count), 1)
            lap[place, :] = lap[place, :] + jnp.where(lane == (code & (LANES - 1)), source, 0.0)
        return carry

    lax.fori_loop(0, got.shape[0], body, 0)


def lap_rows(lap, z, r, depth, count, width_y):
    pieces = []
    for j in range(-(-width_y // LANES)):
        place = pl.multiple_of((j * depth + z) * count + r, ROWS)
        pieces.append(lap[pl.ds(place, ROWS), :])
    return join(pieces, width_y)


def halo_sum(got_on, rows_on, got_off, rows_off, width_y, depth):
    near = decode(take(got_on, rows_on, width_y))
    far = decode(take(got_off, rows_off, width_y))
    out = []
    for j in range(depth):
        terms = [near[j]] if j < HALO else []
        if depth - 1 - j < HALO:
            terms.append(far[depth - 1 - j])
        out.append(functools.reduce(lambda a, b: a + b, terms) if terms else None)
    return out


def prepare(step, first, count, width_x, depth, width_y, got, tiles, lap):
    number = len(tile_parts(width_y))
    blank(lap)
    if first == 0:
        clear(tiles, count, depth, number, -SUB)
    if first + count == width_x:
        clear(tiles, count, depth, number, count)
    inject(step, got, lap, number * depth, first, count, width_x)


def first_kernel(first, width_x, more, now, prior, velocity, lanes, got, got_on, got_off, *refs):
    part, on_ref, off_ref = refs[:3]
    following = refs[3] if more else None
    tiles, lap, high_buf, low_buf, band_buf, now_buf, prior_buf, speed_buf, sems, band_sem = refs[-10:]
    depth, count, width_y = part.shape
    low, high = max(first - SUB, 0), min(first + count + SUB, width_x)
    now_copies = fetch(now, now_buf, sems.at[0], low, high - low) if more else []
    weights = pltpu.make_async_copy(lanes, band_buf, band_sem)
    weights.start()
    copies = fetch(prior, prior_buf, sems.at[1], first, count)
    copies += fetch(velocity, speed_buf, sems.at[2], first, count)
    if more:
        copies += fetch(now, following, sems.at[3], width_x - more, more)
    prepare(0, first, count, width_x, depth, width_y, got, tiles, lap)
    for copy, (row, size) in zip(now_copies, blocks_of(low, high - low)):
        copy.wait()
        spread(tiles, count, now_buf, row - low, row - first, size)
    held = now_buf if more else now
    if not more:
        spread(tiles, count, now, 0, low - first, high - low)
    halve(high_buf, low_buf, held, first - low, count)
    weights.wait()
    add_lanes(high_buf, low_buf, band_buf, lap)
    add_rows(tiles, lap, depth, count, len(tile_parts(width_y)))
    for copy in copies:
        copy.wait()

    def body(r):
        rows = pl.ds(r, ROWS)
        here = pl.ds(pl.multiple_of(r + (first - low), SUB), ROWS)
        halo = halo_sum(got_on, pl.ds(r + first, ROWS), got_off, rows, width_y, depth)
        u = []
        for j in range(depth):
            z = depth_at(j, depth)
            change = lap_rows(lap, z, r, depth, count, width_y)
            if halo[j] is not None:
                change = change + halo[j]
            value = 2.0 * held[z, here, :] - prior_buf[z, rows, :]
            value = value + speed_buf[z, rows, :] * change
            part[z, rows, :] = value
            u.append(value)
        put(off_ref, rows, encode(u[::-1][:HALO]))
        put(on_ref, rows, encode(u[:HALO]))

    row_loop(count, body)


def second_local(first, starts, parts, now, velocity, forward, lanes, got, stencil, bufs, sems):
    now_buf, speed_buf, *forward_bufs = bufs
    tiles, lap, high_buf, low_buf, band_buf, band_sem = stencil
    depth, width_x, width_y = now.shape
    count = now_buf.shape[1]
    weights = pltpu.make_async_copy(lanes, band_buf, band_sem)
    weights.start()
    low, high = max(first - SUB, 0), min(first + count + SUB, width_x)
    copies = fetch(now, now_buf, sems.at[0], first, count)
    copies += fetch(velocity, speed_buf, sems.at[1], first, count)
    for s in range(STEPS):
        copies += fetch(forward.at[s], forward_bufs[s], sems.at[2 + s], first, count)
    prepare(1, first, count, width_x, depth, width_y, got, tiles, lap)
    for start, part in zip(starts, parts):
        row, end = max(low, start), min(high, start + part.shape[1])
        spread(tiles, count, part, row - start, row - first, end - row)
    here = parts[starts.index(first)]
    halve(high_buf, low_buf, here, 0, count)
    weights.wait()
    add_lanes(high_buf, low_buf, band_buf, lap)
    add_rows(tiles, lap, depth, count, len(tile_parts(width_y)))
    for copy in copies:
        copy.wait()
    return here


def send_rows(pairs, first, row, sems, n):
    writes = []
    for k, (buf, target) in enumerate(pairs):
        write = pltpu.make_async_copy(
            buf.at[:, pl.ds(row, BLOCK)], target.at[:, pl.ds(first + row, BLOCK)], sems.at[k, n]
        )
        write.start()
        writes.append(write)
    return writes


def second_kernel(first, starts, *refs):
    parts, refs = refs[: len(starts)], refs[len(starts) :]
    now, velocity, forward, lanes, got, got_on, got_off, out, image, current = refs[:10]
    stencil, bufs = refs[10:16], refs[16:20]
    out_buf, image_buf, sems, out_sems, part_sems = refs[20:]
    lap = stencil[1]
    depth, _, width_y = now.shape
    count = out_buf.shape[1]
    writes = []
    for i, (start, part) in enumerate(zip(starts, parts)):
        write = pltpu.make_async_copy(
            part, current.at[:, pl.ds(start, part.shape[1])], part_sems.at[i]
        )
        write.start()
        writes.append(write)
    here = second_local(first, starts, parts, now, velocity, forward, lanes, got, stencil, bufs, sems)
    now_buf, speed_buf, early, late = bufs
    for n, i in enumerate(range(0, count, BLOCK)):

        def body(r):
            r = r + i
            rows = pl.ds(r, ROWS)
            halo = halo_sum(got_on, rows, got_off, rows, width_y, depth)
            for j in range(depth):
                z = depth_at(j, depth)
                change = lap_rows(lap, z, r, depth, count, width_y)
                if halo[j] is not None:
                    change = change + halo[j]
                mine = here[z, rows, :]
                value = 2.0 * mine - now_buf[z, rows, :] + speed_buf[z, rows, :] * change
                out_buf[z, rows, :] = value
                image_buf[z, rows, :] = early[z, rows, :] * mine + late[z, rows, :] * value

        row_loop(BLOCK, body)
        writes += send_rows(((out_buf, out), (image_buf, image)), first, i, out_sems, n)
    for write in writes:
        write.wait()


def partial_kernel(first, starts, *refs):
    parts, refs = refs[: len(starts)], refs[len(starts) :]
    now, velocity, forward, lanes, got, out, image, speed, late = refs[:9]
    stencil, (now_buf, early, sems) = refs[9:15], refs[15:]
    lap = stencil[1]
    depth, _, width_y = now.shape
    count = now_buf.shape[1]
    bufs = (now_buf, speed, early, late)
    here = second_local(first, starts, parts, now, velocity, forward, lanes, got, stencil, bufs, sems)

    def body(r):
        rows = pl.ds(r, ROWS)
        for z in range(depth):
            change = lap_rows(lap, z, r, depth, count, width_y)
            mine = here[z, rows, :]
            value = 2.0 * mine - now_buf[z, rows, :] + speed[z, rows, :] * change
            out[z, rows, :] = value
            image[z, rows, :] = early[z, rows, :] * mine + late[z, rows, :] * value

    row_loop(count, body)


def last_kernel(first, partial, image_in, speed, late, got_on, got_off, *refs):
    out, image, out_buf, image_buf, sems = refs[-5:]
    depth, count, width_y = out_buf.shape
    writes = []
    for n, i in enumerate(range(0, count, BLOCK)):

        def body(r):
            rows = pl.ds(r + i, ROWS)
            halo = halo_sum(got_on, rows, got_off, rows, width_y, depth)
            for j in range(depth):
                z = depth_at(j, depth)
                extra = speed[z, rows, :] * halo[j] if halo[j] is not None else 0.0
                out_buf[z, rows, :] = partial[z, rows, :] + extra
                image_buf[z, rows, :] = image_in[z, rows, :] + late[z, rows, :] * extra

        row_loop(BLOCK, body)
        writes += send_rows(((out_buf, out), (image_buf, image)), first, i, sems, n)
    for write in writes:
        write.wait()


def shard(now, prior, velocity, forward, traces, weights, target, cell):
    now, prior, velocity, forward = (
        pltpu.with_memory_space_constraint(x, pltpu.HBM) for x in (now, prior, velocity, forward)
    )
    slabs = lax.axis_size("slab")
    depth, width_x, width_y = now.shape
    lanes = pltpu.with_memory_space_constraint(jnp.asarray(band(width_y)), pltpu.HBM)
    rows = traces.shape[0]
    face_lanes = payload_lanes(width_y)
    split = width_x * SHARE[0] // (sum(SHARE) * BLOCK) * BLOCK
    chunks = ((0, split), (split, width_x - split))
    starts = tuple(first for first, _ in chunks)
    field = jax.ShapeDtypeStruct(now.shape, F32)
    number = len(tile_parts(width_y))
    dma = pltpu.SemaphoreType.DMA
    on_pairs = [(k, k ^ 1) for k in range(slabs) if k ^ 1 < slabs]
    off_pairs = [(i + 1, j + 1) for i, j in on_pairs if i + 1 < slabs and j + 1 < slabs]

    def plane(count):
        return jax.ShapeDtypeStruct((count, face_lanes), BF16)

    def rows_of(count):
        return jax.ShapeDtypeStruct((depth, count, width_y), F32)

    def buffer(count):
        return pltpu.VMEM((depth, count, width_y), F32)

    def stencil(count):
        tiles = pltpu.VMEM((number * depth * (count + 2 * SUB), LANES), F32)
        lap = pltpu.VMEM((number * depth * count + SUB, LANES), F32)
        half = pltpu.VMEM((depth * count, number * LANES), BF16)
        return (tiles, lap, half, half, pltpu.VMEM(lanes.shape, BF16))

    def blocks(count):
        return -(-count // BLOCK)

    def call(kernel, ins, outs, scratch=(), out_spec=None, **kw):
        return pl.pallas_call(
            kernel,
            in_specs=ins,
            out_specs=out_spec or [VMEM] * len(outs),
            out_shape=outs,
            scratch_shapes=scratch,
            compiler_params=params(),
            **kw,
        )

    def swap(face, pairs):
        return lax.ppermute(face, "slab", pairs)

    got_off = []
    (face,) = call(
        functools.partial(pack_kernel, 0, False),
        [HBM],
        [plane(split)],
        (buffer(split), dma((blocks(split),))),
    )(now)
    got_off.append(swap(face, off_pairs))
    face, traces = lax.optimization_barrier((face, traces))
    (sent,) = call(
        functools.partial(route_kernel, slabs, now.shape),
        [VMEM] * 4,
        [jax.ShapeDtypeStruct((slabs, 1, LANES), F32)],
    )(traces, weights, target.reshape(1, rows), cell.reshape(1, rows))
    got = lax.all_to_all(sent, "slab", split_axis=0, concat_axis=0, tiled=True)
    sent, later = lax.optimization_barrier((sent, now))
    on_face, face = call(
        functools.partial(pack_kernel, split, True),
        [HBM],
        [plane(width_x), plane(width_x - split)],
        (buffer(width_x), dma((blocks(width_x),))),
    )(later)
    got_off.append(swap(face, off_pairs))
    got_on = swap(on_face, on_pairs)
    parts, second_on, second_off = [], [], []
    more = width_x - split + SUB
    held = now
    for i, (first, count) in enumerate(chunks):
        part, on_face, face, *following = call(
            functools.partial(first_kernel, first, width_x, 0 if i else more),
            [VMEM if i else HBM, HBM, HBM, HBM, SMEM, VMEM, VMEM],
            [rows_of(count), plane(count), plane(count)] + ([] if i else [rows_of(more)]),
            (
                *stencil(count),
                buffer(SUB if i else count + SUB),
                buffer(count),
                buffer(count),
                dma((4, blocks(width_x))),
                dma,
            ),
        )(held, prior, velocity, lanes, got, got_on, got_off[i])
        second_off.append(swap(face, off_pairs))
        second_on.append(swap(on_face, on_pairs))
        parts.append(part)
        if i == 0:
            (held,) = following
            part, prior = lax.optimization_barrier((part, prior))
    (first, count), (last, size) = chunks
    second, image, current = call(
        functools.partial(second_kernel, first, starts),
        [VMEM] * len(parts) + [HBM] * 4 + [SMEM, VMEM, VMEM],
        [field, field, field],
        (
            *stencil(count),
            dma,
            *[buffer(count)] * 6,
            dma((2 + STEPS, blocks(count))),
            dma((2, blocks(count))),
            dma((len(parts),)),
        ),
        [HBM] * 3,
    )(*parts, now, velocity, forward, lanes, got, second_on[0], second_off[0])
    partial, image_part, speed, late = call(
        functools.partial(partial_kernel, last, starts),
        [VMEM] * len(parts) + [HBM] * 4 + [SMEM],
        [rows_of(size)] * 4,
        (*stencil(size), dma, buffer(size), buffer(size), dma((2 + STEPS, blocks(size)))),
    )(*parts, now, velocity, forward, lanes, got)
    second, image = call(
        functools.partial(last_kernel, last),
        [VMEM] * 6 + [HBM] * 2,
        [field, field],
        (buffer(size), buffer(size), dma((2, blocks(size)))),
        [HBM] * 2,
        input_output_aliases={6: 0, 7: 1},
    )(partial, image_part, speed, late, second_on[1], second_off[1], second, image)
    return (image, second, current)


def solution(mesh):
    split = P(("groups", "slab"), None, None)
    return jax.shard_map(
        shard,
        mesh=mesh,
        in_specs=(
            split,
            split,
            split,
            P(None, ("groups", "slab"), None, None),
            P(("groups", "slab"), None),
            P(),
            P(("groups", "slab"), None),
            P(("groups", "slab")),
        ),
        out_specs=(split, split, split),
        check_vma=False,
    )
```

```python
import functools

import jax
import jax.numpy as jnp
import numpy as np
from jax import lax
from jax.experimental import pallas as pl
from jax.experimental.pallas import tpu as pltpu
from jax.sharding import PartitionSpec as P


CAP = 4
STEPS = 2
W = (-205.0 / 72.0, 8.0 / 5.0, -1.0 / 5.0, 8.0 / 315.0, -1.0 / 560.0)
HALO = 4
ROWS = 16
BLOCK = 32
SUB = 8
UNROLL = 4
SHARE = (3, 2)
LANES = 128
F32 = jnp.float32
BF16 = jnp.bfloat16
VMEM = pl.BlockSpec(memory_space=pltpu.VMEM)
SMEM = pl.BlockSpec(memory_space=pltpu.SMEM)
HBM = pl.BlockSpec(memory_space=pltpu.HBM)


def params():
    return pltpu.CompilerParams(vmem_limit_bytes=20 << 20)


def payload_lanes(width):
    full = width // LANES * LANES
    rest = width - full
    if rest == 0:
        return HALO * full
    return HALO * full + (2 * LANES if rest * 2 <= LANES else HALO * LANES)


def depth_at(j, depth):
    odd = lax.rem(lax.axis_index("slab"), 2)
    return j + (1 - odd) * (depth - 1 - 2 * j)


def encode(u):
    t1 = u[0].astype(BF16).astype(F32)
    e1 = u[0] - t1
    t2 = (u[1] + (W[2] / W[3]) * e1).astype(BF16).astype(F32)
    t3 = u[2].astype(BF16).astype(F32)
    t0 = W[1] * e1 + W[2] * (u[1] - t2) + W[3] * (u[2] - t3) + W[4] * u[3]
    return (t0, t1, t2, t3)


def decode(t):
    t0, t1, t2, t3 = t
    return (
        t0 + W[1] * t1 + W[2] * t2 + W[3] * t3,
        W[2] * t1 + W[3] * t2 + W[4] * t3,
        W[3] * t1 + W[4] * t2,
        W[4] * t1,
    )


def put(ref, rows, t):
    width = t[0].shape[1]
    full = width // LANES * LANES
    rest = width - full
    for k in range(HALO):
        ref[rows, k * full : (k + 1) * full] = t[k][:, :full].astype(BF16)
    if rest == 0:
        return
    base = HALO * full
    if rest * 2 <= LANES:
        half = LANES // 2
        for k in range(0, HALO, 2):
            a = jnp.pad(t[k][:, full:], ((0, 0), (0, half - rest)))
            b = jnp.pad(t[k + 1][:, full:], ((0, 0), (0, half - rest)))
            ref[rows, base : base + LANES] = jnp.concatenate([a, b], axis=1).astype(BF16)
            base += LANES
    else:
        for k in range(HALO):
            tail = jnp.pad(t[k][:, full:], ((0, 0), (0, LANES - rest)))
            ref[rows, base : base + LANES] = tail.astype(BF16)
            base += LANES


def take(ref, rows, width):
    full = width // LANES * LANES
    rest = width - full
    main = [ref[rows, k * full : (k + 1) * full].astype(F32) for k in range(HALO)]
    if rest == 0:
        return main
    base = HALO * full
    tails = []
    if rest * 2 <= LANES:
        half = LANES // 2
        for _ in range(0, HALO, 2):
            both = ref[rows, base : base + LANES].astype(F32)
            tails.append(both[:, :rest])
            tails.append(pltpu.roll(both, half, 1)[:, :rest])
            base += LANES
    else:
        for _ in range(HALO):
            tails.append(ref[rows, base : base + LANES].astype(F32)[:, :rest])
            base += LANES
    return [jnp.concatenate([m, t], axis=1) for m, t in zip(main, tails)]


def row_loop(count, body):
    def step(i, carry):
        body(pl.multiple_of(i * ROWS, ROWS))
        return carry

    lax.fori_loop(0, count // ROWS, step, 0)


def row_span(width_x):
    return 1 << (width_x - 1).bit_length()


def blocks_of(first, count):
    return [(i, min(BLOCK, first + count - i)) for i in range(first, first + count, BLOCK)]


def fetch(source, buf, sems, first, count):
    copies = []
    for n, (row, size) in enumerate(blocks_of(first, count)):
        rows = pl.ds(row, size)
        copies.append(
            pltpu.make_async_copy(source.at[:, rows], buf.at[:, pl.ds(row - first, size)], sems.at[n])
        )
        copies[-1].start()
    return copies


def pack_kernel(first, with_on, now, *refs):
    refs = list(refs)
    on_ref = refs.pop(0) if with_on else None
    off_ref, buf, sems = refs
    depth = now.shape[0]
    base = 0 if with_on else first
    copies = fetch(now, buf, sems, base, buf.shape[1])

    for i, copy in enumerate(copies):
        copy.wait()

        def body(r):
            r = r + i * BLOCK
            rows = pl.ds(r, ROWS)
            u = [buf[depth_at(j, depth), rows, :] for j in range(depth)]
            if base + i * BLOCK >= first and base + i * BLOCK < first + off_ref.shape[0]:
                put(off_ref, pl.ds(r + base - first, ROWS), encode(u[::-1][:HALO]))
            if with_on:
                put(on_ref, rows, encode(u[:HALO]))

        row_loop(BLOCK, body)


def route_kernel(slabs, field, traces, weights, target, cell, out):
    depth, width_x, width_y = field
    rows = traces.shape[0]
    lane = lax.broadcasted_iota(jnp.int32, (rows, rows), 1)
    row = lax.broadcasted_iota(jnp.int32, (rows, rows), 0)
    eye = lane == row
    target_row = jnp.broadcast_to(target[...], (rows, rows))
    cell_row = jnp.broadcast_to(cell[...], (rows, rows))
    target_col = jnp.sum(jnp.where(eye, target_row, 0), axis=1, keepdims=True)
    cell_col = jnp.sum(jnp.where(eye, cell_row, 0), axis=1, keepdims=True)
    same = (target_row == target_col) & (lane < row)
    rank = jnp.sum(jnp.where(same, 1, 0), axis=1, keepdims=True)
    values = traces[...].astype(F32)
    columns = [
        jnp.sum(values * weights[s : s + 1, :].astype(F32), axis=1, keepdims=True)
        for s in range(STEPS)
    ]
    line = cell_col // width_y
    layer = line // width_x
    column = cell_col - line * width_y
    plane = (column // LANES) * depth + layer
    code = (plane * row_span(width_x) + line - layer * width_x) * LANES + column % LANES
    columns.append(code.astype(F32))
    spot = lax.broadcasted_iota(jnp.int32, (rows, LANES), 1)
    spread = jnp.zeros((rows, LANES), F32)
    for j, column in enumerate(columns):
        spread = jnp.where(spot == j * CAP + rank, column, spread)
    taker = lax.broadcasted_iota(jnp.int32, (slabs, rows), 0)
    chosen = (taker == jnp.broadcast_to(target[...], (slabs, rows))).astype(F32)
    picked = jnp.dot(
        chosen, spread, precision=lax.Precision.HIGHEST, preferred_element_type=F32
    )
    out[...] = picked.reshape(out.shape)


def tile_parts(width_y):
    return [(lo, min(lo + LANES, width_y)) for lo in range(0, width_y + HALO, LANES)]


def join(pieces, width_y):
    last = width_y - (len(pieces) - 1) * LANES
    return jnp.concatenate([*pieces[:-1], pieces[-1][:, :last]], axis=1)


def tile_rows(z, row, j, count, number):
    return pl.ds((z * (count + 2 * SUB) + SUB + row) * number + j, SUB, stride=number)


def spread(tiles, count, source, start, row, size):
    depth, _, width_y = source.shape
    parts = tile_parts(width_y)

    def body(i, carry):
        r = i * SUB
        for z in range(depth):
            for j, (lo, hi) in enumerate(parts):
                if hi > lo:
                    value = source[z, pl.ds(pl.multiple_of(r + start, SUB), SUB), lo:hi]
                    if hi - lo < LANES:
                        value = jnp.pad(value, ((0, 0), (0, LANES - (hi - lo))))
                else:
                    value = jnp.zeros((SUB, LANES), F32)
                tiles[tile_rows(z, r + row, j, count, len(parts)), :] = value
        return carry

    lax.fori_loop(0, size // SUB, body, 0)


def clear(tiles, count, depth, number, row):
    for z in range(depth):
        for j in range(number):
            tiles[tile_rows(z, row, j, count, number), :] = jnp.zeros((SUB, LANES), F32)


def band(width_y):
    number = len(tile_parts(width_y))
    spot = np.arange(number * LANES)
    away = np.abs(spot[:, None] - spot[None, :])
    inside = (spot[:, None] < width_y) & (spot[None, :] < width_y)
    whole = np.zeros(away.shape, np.float32)
    for k in range(1, HALO + 1):
        whole[(away == k) & inside] = W[k]
    out = []
    for w in range(number - 1):
        part = whole[w * LANES : (w + 2) * LANES, w * LANES : (w + 2) * LANES].copy()
        if w:
            part[:LANES, :LANES] = 0.0
        high = part.astype(BF16)
        out.append([high, (part - high.astype(np.float32)).astype(BF16)])
    return np.array(out)


def halve(high, low, source, start, count):
    depth, _, width_y = source.shape
    extra = high.shape[1] - width_y

    def body(r):
        for z in range(depth):
            value = source[z, pl.ds(pl.multiple_of(r + start, SUB), ROWS), :]
            value = jnp.pad(value, ((0, 0), (0, extra)))
            top = value.astype(BF16)
            into = pl.ds(pl.multiple_of(r + z * count, ROWS), ROWS)
            high[into, :] = top
            low[into, :] = (value - top.astype(F32)).astype(BF16)

    row_loop(count, body)


def add_lanes(high, low, weights, lap):
    lines = high.shape[0]
    size = lines // 2

    def product(x, y):
        return jnp.dot(x, y, preferred_element_type=F32)

    def step(i, carry):
        rows = pl.ds(pl.multiple_of(i * size, ROWS), size)
        for w in range(weights.shape[0]):
            window = slice(w * LANES, (w + 2) * LANES)
            x, y = high[rows, window], low[rows, window]
            total = product(x, weights[w, 0]) + product(y, weights[w, 0])
            total = total + product(x, weights[w, 1])
            for q in range(2):
                into = pl.ds(pl.multiple_of(i * size + (w + q) * lines, ROWS), size)
                lap[into, :] = lap[into, :] + total[:, q * LANES : (q + 1) * LANES]
        return carry

    lax.fori_loop(0, 2, step, 0)


def add_rows(tiles, lap, depth, count, number):
    groups = count // SUB
    unroll = max(u for u in range(1, UNROLL + 1) if groups % u == 0)

    def one(r):
        def at(z, j, shift=0):
            return tiles[tile_rows(z, r + shift, j, count, number), :]

        centre = [[at(z, j) for j in range(number)] for z in range(depth)]
        for z in range(depth):
            for j in range(number):
                place = pl.ds(pl.multiple_of(r + (j * depth + z) * count, SUB), SUB)
                total = lap[place, :] + 3.0 * W[0] * centre[z][j]
                for k in range(1, HALO + 1):
                    pair = at(z, j, -k) + at(z, j, k)
                    if z - k >= 0:
                        pair = pair + centre[z - k][j]
                    if z + k < depth:
                        pair = pair + centre[z + k][j]
                    total = total + W[k] * pair
                lap[place, :] = total

    def step(i, carry):
        for u in range(unroll):
            one((i * unroll + u) * SUB)
        return carry

    lax.fori_loop(0, groups // unroll, step, 0)


def blank(lap):
    def body(i, carry):
        lap[pl.ds(pl.multiple_of(i * 8 * SUB, SUB), 8 * SUB), :] = jnp.zeros((8 * SUB, LANES), F32)
        return carry

    whole = lap.shape[0] // (8 * SUB)
    lax.fori_loop(0, whole, body, 0)
    rest = lap.shape[0] - whole * 8 * SUB
    lap[whole * 8 * SUB :, :] = jnp.zeros((rest, LANES), F32)


def inject(step, got, lap, planes, first, count, width_x):
    lane = lax.broadcasted_iota(jnp.int32, (1, LANES), 1)
    span = row_span(width_x)
    shift = LANES.bit_length() - 1

    def body(i, carry):
        for slot in range(CAP):
            source = got[i, 0, step * CAP + slot]
            code = got[i, 0, STEPS * CAP + slot].astype(jnp.int32)
            line = lax.shift_right_logical(code, jnp.int32(shift))
            row = (line & (span - 1)) - first
            plane = lax.shift_right_logical(line, jnp.int32(span.bit_length() - 1))
            inside = (row >= 0) & (row < count)
            place = pl.ds(jnp.where(inside, plane * count + row, planes * count), 1)
            lap[place, :] = lap[place, :] + jnp.where(lane == (code & (LANES - 1)), source, 0.0)
        return carry

    lax.fori_loop(0, got.shape[0], body, 0)


def lap_rows(lap, z, r, depth, count, width_y):
    pieces = []
    for j in range(-(-width_y // LANES)):
        place = pl.multiple_of((j * depth + z) * count + r, ROWS)
        pieces.append(lap[pl.ds(place, ROWS), :])
    return join(pieces, width_y)


def halo_sum(got_on, rows_on, got_off, rows_off, width_y, depth):
    near = decode(take(got_on, rows_on, width_y))
    far = decode(take(got_off, rows_off, width_y))
    out = []
    for j in range(depth):
        terms = [near[j]] if j < HALO else []
        if depth - 1 - j < HALO:
            terms.append(far[depth - 1 - j])
        out.append(functools.reduce(lambda a, b: a + b, terms) if terms else None)
    return out


def prepare(step, first, count, width_x, depth, width_y, got, tiles, lap):
    number = len(tile_parts(width_y))
    blank(lap)
    if first == 0:
        clear(tiles, count, depth, number, -SUB)
    if first + count == width_x:
        clear(tiles, count, depth, number, count)
    inject(step, got, lap, number * depth, first, count, width_x)


def first_kernel(first, width_x, now, prior, velocity, lanes, got, got_on, got_off, *refs):
    part, on_ref, off_ref, held, speed = refs[:5]
    tiles, lap, high_buf, low_buf, prior_buf, sems, band_sem = refs[-7:]
    depth, count, width_y = part.shape
    low, high = max(first - SUB, 0), min(first + count + SUB, width_x)
    now_copies = fetch(now, held, sems.at[0], low, high - low)
    keep_band = len(refs) > 12
    if keep_band:
        weights = pltpu.make_async_copy(lanes, refs[5], band_sem)
        weights.start()
    copies = fetch(prior, prior_buf, sems.at[1], first, count)
    copies += fetch(velocity, speed, sems.at[2], first, count)
    prepare(0, first, count, width_x, depth, width_y, got, tiles, lap)
    for copy, (row, size) in zip(now_copies, blocks_of(low, high - low)):
        copy.wait()
        spread(tiles, count, held, row - low, row - first, size)
    halve(high_buf, low_buf, held, first - low, count)
    if keep_band:
        weights.wait()
    add_lanes(high_buf, low_buf, refs[5] if keep_band else lanes, lap)
    add_rows(tiles, lap, depth, count, len(tile_parts(width_y)))
    for copy in copies:
        copy.wait()

    def body(r):
        rows = pl.ds(r, ROWS)
        here = pl.ds(pl.multiple_of(r + (first - low), SUB), ROWS)
        halo = halo_sum(got_on, pl.ds(r + first, ROWS), got_off, rows, width_y, depth)
        u = []
        for j in range(depth):
            z = depth_at(j, depth)
            change = lap_rows(lap, z, r, depth, count, width_y)
            if halo[j] is not None:
                change = change + halo[j]
            value = 2.0 * held[z, here, :] - prior_buf[z, rows, :]
            value = value + speed[z, rows, :] * change
            part[z, rows, :] = value
            u.append(value)
        put(off_ref, rows, encode(u[::-1][:HALO]))
        put(on_ref, rows, encode(u[:HALO]))

    row_loop(count, body)


def second_local(first, starts, parts, width_x, lanes, got, stencil):
    tiles, lap, high_buf, low_buf = stencil
    here = parts[starts.index(first)]
    depth, count, width_y = here.shape
    low, high = max(first - SUB, 0), min(first + count + SUB, width_x)
    prepare(1, first, count, width_x, depth, width_y, got, tiles, lap)
    for start, part in zip(starts, parts):
        row, end = max(low, start), min(high, start + part.shape[1])
        spread(tiles, count, part, row - start, row - first, end - row)
    halve(high_buf, low_buf, here, 0, count)
    add_lanes(high_buf, low_buf, lanes, lap)
    add_rows(tiles, lap, depth, count, len(tile_parts(width_y)))
    return here


def send_rows(pairs, first, row, sems, n):
    writes = []
    for k, (buf, target) in enumerate(pairs):
        write = pltpu.make_async_copy(
            buf.at[:, pl.ds(row, BLOCK)], target.at[:, pl.ds(first + row, BLOCK)], sems.at[k, n]
        )
        write.start()
        writes.append(write)
    return writes


def second_kernel(first, starts, *refs):
    parts, refs = refs[: len(starts)], refs[len(starts) :]
    held, speed, forward, lanes, got, got_on, got_off, out, image = refs[:9]
    stencil = refs[9:13]
    out_buf, image_buf, out_sems = refs[13:]
    lap = stencil[1]
    depth, width_x, width_y = out.shape
    count = out_buf.shape[1]
    back = first - max(first - SUB, 0)
    writes = []
    here = second_local(first, starts, parts, width_x, lanes, got, stencil)
    for n, i in enumerate(range(0, count, BLOCK)):

        def body(r):
            r = r + i
            rows = pl.ds(r, ROWS)
            whole = pl.ds(r + first, ROWS)
            before = pl.ds(pl.multiple_of(r + back, SUB), ROWS)
            halo = halo_sum(got_on, rows, got_off, rows, width_y, depth)
            for j in range(depth):
                z = depth_at(j, depth)
                change = lap_rows(lap, z, r, depth, count, width_y)
                if halo[j] is not None:
                    change = change + halo[j]
                mine = here[z, rows, :]
                value = 2.0 * mine - held[z, before, :] + speed[z, rows, :] * change
                out_buf[z, rows, :] = value
                image_buf[z, rows, :] = forward[0, z, whole, :] * mine + forward[1, z, whole, :] * value

        row_loop(BLOCK, body)
        writes += send_rows(((out_buf, out), (image_buf, image)), first, i, out_sems, n)
    for write in writes:
        write.wait()


def partial_kernel(first, starts, *refs):
    parts, refs = refs[: len(starts)], refs[len(starts) :]
    held, speed, forward, lanes, got, current, out, image = refs[:8]
    stencil, sems = refs[8:12], refs[12]
    lap = stencil[1]
    width_x = current.shape[1]
    depth, count, width_y = out.shape
    back = first - max(first - SUB, 0)
    writes = []
    for i, (start, part) in enumerate(zip(starts, parts)):
        write = pltpu.make_async_copy(part, current.at[:, pl.ds(start, part.shape[1])], sems.at[i])
        write.start()
        writes.append(write)
    here = second_local(first, starts, parts, width_x, lanes, got, stencil)

    def body(r):
        rows = pl.ds(r, ROWS)
        whole = pl.ds(r + first, ROWS)
        before = pl.ds(pl.multiple_of(r + back, SUB), ROWS)
        for z in range(depth):
            change = lap_rows(lap, z, r, depth, count, width_y)
            mine = here[z, rows, :]
            value = 2.0 * mine - held[z, before, :] + speed[z, rows, :] * change
            out[z, rows, :] = value
            image[z, rows, :] = forward[0, z, whole, :] * mine + forward[1, z, whole, :] * value

    row_loop(count, body)
    for write in writes:
        write.wait()


def last_kernel(first, partial, image_in, speed, forward, got_on, got_off, *refs):
    out, image, out_buf, image_buf, sems = refs[-5:]
    depth, count, width_y = out_buf.shape
    writes = []
    for n, i in enumerate(range(0, count, BLOCK)):

        def body(r):
            rows = pl.ds(r + i, ROWS)
            whole = pl.ds(r + (first + i), ROWS)
            halo = halo_sum(got_on, rows, got_off, rows, width_y, depth)
            for j in range(depth):
                z = depth_at(j, depth)
                extra = speed[z, rows, :] * halo[j] if halo[j] is not None else 0.0
                out_buf[z, rows, :] = partial[z, rows, :] + extra
                image_buf[z, rows, :] = image_in[z, rows, :] + forward[1, z, whole, :] * extra

        row_loop(BLOCK, body)
        writes += send_rows(((out_buf, out), (image_buf, image)), first, i, sems, n)
    for write in writes:
        write.wait()


def shard(now, prior, velocity, forward, traces, weights, target, cell):
    now, prior, velocity = (
        pltpu.with_memory_space_constraint(x, pltpu.HBM) for x in (now, prior, velocity)
    )
    slabs = lax.axis_size("slab")
    depth, width_x, width_y = now.shape
    lanes = pltpu.with_memory_space_constraint(jnp.asarray(band(width_y)), pltpu.HBM)
    rows = traces.shape[0]
    face_lanes = payload_lanes(width_y)
    split = width_x * SHARE[0] // (sum(SHARE) * BLOCK) * BLOCK
    chunks = ((0, split), (split, width_x - split))
    starts = tuple(first for first, _ in chunks)
    field = jax.ShapeDtypeStruct(now.shape, F32)
    number = len(tile_parts(width_y))
    dma = pltpu.SemaphoreType.DMA
    on_pairs = [(k, k ^ 1) for k in range(slabs) if k ^ 1 < slabs]
    off_pairs = [(i + 1, j + 1) for i, j in on_pairs if i + 1 < slabs and j + 1 < slabs]

    def plane(count):
        return jax.ShapeDtypeStruct((count, face_lanes), BF16)

    def rows_of(count):
        return jax.ShapeDtypeStruct((depth, count, width_y), F32)

    def buffer(count):
        return pltpu.VMEM((depth, count, width_y), F32)

    def stencil(count):
        tiles = pltpu.VMEM((number * depth * (count + 2 * SUB), LANES), F32)
        lap = pltpu.VMEM((number * depth * count + SUB, LANES), F32)
        half = pltpu.VMEM((depth * count, number * LANES), BF16)
        return (tiles, lap, half, half)

    def blocks(count):
        return -(-count // BLOCK)

    def call(kernel, ins, outs, scratch=(), out_spec=None, **kw):
        return pl.pallas_call(
            kernel,
            in_specs=ins,
            out_specs=out_spec or [VMEM] * len(outs),
            out_shape=outs,
            scratch_shapes=scratch,
            compiler_params=params(),
            **kw,
        )

    def swap(face, pairs):
        return lax.ppermute(face, "slab", pairs)

    got_off = []
    (face,) = call(
        functools.partial(pack_kernel, 0, False),
        [HBM],
        [plane(split)],
        (buffer(split), dma((blocks(split),))),
    )(now)
    got_off.append(swap(face, off_pairs))
    face, traces = lax.optimization_barrier((face, traces))
    (sent,) = call(
        functools.partial(route_kernel, slabs, now.shape),
        [VMEM] * 4,
        [jax.ShapeDtypeStruct((slabs, 1, LANES), F32)],
    )(traces, weights, target.reshape(1, rows), cell.reshape(1, rows))
    got = lax.all_to_all(sent, "slab", split_axis=0, concat_axis=0, tiled=True)
    sent, later = lax.optimization_barrier((sent, now))
    on_face, face = call(
        functools.partial(pack_kernel, split, True),
        [HBM],
        [plane(width_x), plane(width_x - split)],
        (buffer(width_x), dma((blocks(width_x),))),
    )(later)
    got_off.append(swap(face, off_pairs))
    got_on = swap(on_face, on_pairs)
    parts, held, speed, second_on, second_off = [], [], [], [], []
    for i, (first, count) in enumerate(chunks):
        near = min(first + count + SUB, width_x) - max(first - SUB, 0)
        keep = [] if i else [jax.ShapeDtypeStruct(lanes.shape, BF16)]
        part, on_face, face, rows_held, rows_speed, *kept = call(
            functools.partial(first_kernel, first, width_x),
            [HBM] * 3 + [VMEM if i else HBM, SMEM, VMEM, VMEM],
            [rows_of(count), plane(count), plane(count), rows_of(near), rows_of(count)] + keep,
            (*stencil(count), buffer(count), dma((3, blocks(near))), dma),
        )(now, prior, velocity, lanes, got, got_on, got_off[i])
        lanes = kept[0] if kept else lanes
        second_off.append(swap(face, off_pairs))
        second_on.append(swap(on_face, on_pairs))
        parts.append(part)
        held.append(rows_held)
        speed.append(rows_speed)
    parts[-1], forward = lax.optimization_barrier((parts[-1], forward))
    (first, count), (last, size) = chunks
    current, partial, image_part = call(
        functools.partial(partial_kernel, last, starts),
        [VMEM] * (len(parts) + 4) + [SMEM],
        [field, rows_of(size), rows_of(size)],
        (*stencil(size), dma((len(parts),))),
        [HBM, VMEM, VMEM],
    )(*parts, held[1], speed[1], forward, lanes, got)
    second, image = call(
        functools.partial(second_kernel, first, starts),
        [VMEM] * (len(parts) + 4) + [SMEM, VMEM, VMEM],
        [field, field],
        (*stencil(count), buffer(count), buffer(count), dma((2, blocks(count)))),
        [HBM] * 2,
    )(*parts, held[0], speed[0], forward, lanes, got, second_on[0], second_off[0])
    second, image = call(
        functools.partial(last_kernel, last),
        [VMEM] * 6 + [HBM] * 2,
        [field, field],
        (buffer(size), buffer(size), dma((2, blocks(size)))),
        [HBM] * 2,
        input_output_aliases={6: 0, 7: 1},
    )(partial, image_part, speed[1], forward, second_on[1], second_off[1], second, image)
    return (image, second, current)


def solution(mesh):
    split = P(("groups", "slab"), None, None)
    return jax.shard_map(
        shard,
        mesh=mesh,
        in_specs=(
            split,
            split,
            split,
            P(None, ("groups", "slab"), None, None),
            P(("groups", "slab"), None),
            P(),
            P(("groups", "slab"), None),
            P(("groups", "slab")),
        ),
        out_specs=(split, split, split),
        check_vma=False,
    )
```

```python
import functools

import jax
import jax.numpy as jnp
import numpy as np
from jax import lax
from jax.experimental import pallas as pl
from jax.experimental.pallas import tpu as pltpu
from jax.sharding import PartitionSpec as P


CAP = 4
STEPS = 2
W = (-205.0 / 72.0, 8.0 / 5.0, -1.0 / 5.0, 8.0 / 315.0, -1.0 / 560.0)
HALO = 4
ROWS = 16
BLOCK = 32
SUB = 8
UNROLL = 4
SHARE = (3, 2)
LATER = (1, 1)
LANES = 128
F32 = jnp.float32
BF16 = jnp.bfloat16
VMEM = pl.BlockSpec(memory_space=pltpu.VMEM)
SMEM = pl.BlockSpec(memory_space=pltpu.SMEM)
HBM = pl.BlockSpec(memory_space=pltpu.HBM)


def params():
    return pltpu.CompilerParams(vmem_limit_bytes=20 << 20)


def payload_lanes(width):
    full = width // LANES * LANES
    rest = width - full
    if rest == 0:
        return HALO * full
    return HALO * full + (2 * LANES if rest * 2 <= LANES else HALO * LANES)


def depth_at(j, depth):
    odd = lax.rem(lax.axis_index("slab"), 2)
    return j + (1 - odd) * (depth - 1 - 2 * j)


def encode(u):
    t1 = u[0].astype(BF16).astype(F32)
    e1 = u[0] - t1
    t2 = (u[1] + (W[2] / W[3]) * e1).astype(BF16).astype(F32)
    t3 = u[2].astype(BF16).astype(F32)
    t0 = W[1] * e1 + W[2] * (u[1] - t2) + W[3] * (u[2] - t3) + W[4] * u[3]
    return (t0, t1, t2, t3)


def decode(t):
    t0, t1, t2, t3 = t
    return (
        t0 + W[1] * t1 + W[2] * t2 + W[3] * t3,
        W[2] * t1 + W[3] * t2 + W[4] * t3,
        W[3] * t1 + W[4] * t2,
        W[4] * t1,
    )


def put(ref, rows, t):
    width = t[0].shape[1]
    full = width // LANES * LANES
    rest = width - full
    for k in range(HALO):
        ref[rows, k * full : (k + 1) * full] = t[k][:, :full].astype(BF16)
    if rest == 0:
        return
    base = HALO * full
    if rest * 2 <= LANES:
        half = LANES // 2
        for k in range(0, HALO, 2):
            a = jnp.pad(t[k][:, full:], ((0, 0), (0, half - rest)))
            b = jnp.pad(t[k + 1][:, full:], ((0, 0), (0, half - rest)))
            ref[rows, base : base + LANES] = jnp.concatenate([a, b], axis=1).astype(BF16)
            base += LANES
    else:
        for k in range(HALO):
            tail = jnp.pad(t[k][:, full:], ((0, 0), (0, LANES - rest)))
            ref[rows, base : base + LANES] = tail.astype(BF16)
            base += LANES


def take(ref, rows, width):
    full = width // LANES * LANES
    rest = width - full
    main = [ref[rows, k * full : (k + 1) * full].astype(F32) for k in range(HALO)]
    if rest == 0:
        return main
    base = HALO * full
    tails = []
    if rest * 2 <= LANES:
        half = LANES // 2
        for _ in range(0, HALO, 2):
            both = ref[rows, base : base + LANES].astype(F32)
            tails.append(both[:, :rest])
            tails.append(pltpu.roll(both, half, 1)[:, :rest])
            base += LANES
    else:
        for _ in range(HALO):
            tails.append(ref[rows, base : base + LANES].astype(F32)[:, :rest])
            base += LANES
    return [jnp.concatenate([m, t], axis=1) for m, t in zip(main, tails)]


def row_loop(count, body):
    def step(i, carry):
        body(pl.multiple_of(i * ROWS, ROWS))
        return carry

    lax.fori_loop(0, count // ROWS, step, 0)


def row_span(width_x):
    return 1 << (width_x - 1).bit_length()


def blocks_of(first, count):
    return [(i, min(BLOCK, first + count - i)) for i in range(first, first + count, BLOCK)]


def fetch(source, buf, sems, first, count):
    copies = []
    for n, (row, size) in enumerate(blocks_of(first, count)):
        rows = pl.ds(row, size)
        copies.append(
            pltpu.make_async_copy(source.at[:, rows], buf.at[:, pl.ds(row - first, size)], sems.at[n])
        )
        copies[-1].start()
    return copies


def pack_kernel(first, with_on, now, *refs):
    refs = list(refs)
    on_ref = refs.pop(0) if with_on else None
    off_ref, buf, sems = refs
    depth = now.shape[0]
    base = 0 if with_on else first
    copies = fetch(now, buf, sems, base, buf.shape[1])

    for i, copy in enumerate(copies):
        copy.wait()

        def body(r):
            r = r + i * BLOCK
            rows = pl.ds(r, ROWS)
            u = [buf[depth_at(j, depth), rows, :] for j in range(depth)]
            if base + i * BLOCK >= first and base + i * BLOCK < first + off_ref.shape[0]:
                put(off_ref, pl.ds(r + base - first, ROWS), encode(u[::-1][:HALO]))
            if with_on:
                put(on_ref, rows, encode(u[:HALO]))

        row_loop(BLOCK, body)


def route_kernel(slabs, field, traces, weights, target, cell, out):
    depth, width_x, width_y = field
    rows = traces.shape[0]
    lane = lax.broadcasted_iota(jnp.int32, (rows, rows), 1)
    row = lax.broadcasted_iota(jnp.int32, (rows, rows), 0)
    eye = lane == row
    target_row = jnp.broadcast_to(target[...], (rows, rows))
    cell_row = jnp.broadcast_to(cell[...], (rows, rows))
    target_col = jnp.sum(jnp.where(eye, target_row, 0), axis=1, keepdims=True)
    cell_col = jnp.sum(jnp.where(eye, cell_row, 0), axis=1, keepdims=True)
    same = (target_row == target_col) & (lane < row)
    rank = jnp.sum(jnp.where(same, 1, 0), axis=1, keepdims=True)
    values = traces[...].astype(F32)
    columns = [
        jnp.sum(values * weights[s : s + 1, :].astype(F32), axis=1, keepdims=True)
        for s in range(STEPS)
    ]
    line = cell_col // width_y
    layer = line // width_x
    column = cell_col - line * width_y
    plane = (column // LANES) * depth + layer
    code = (plane * row_span(width_x) + line - layer * width_x) * LANES + column % LANES
    columns.append(code.astype(F32))
    spot = lax.broadcasted_iota(jnp.int32, (rows, LANES), 1)
    spread = jnp.zeros((rows, LANES), F32)
    for j, column in enumerate(columns):
        spread = jnp.where(spot == j * CAP + rank, column, spread)
    taker = lax.broadcasted_iota(jnp.int32, (slabs, rows), 0)
    chosen = (taker == jnp.broadcast_to(target[...], (slabs, rows))).astype(F32)
    picked = jnp.dot(
        chosen, spread, precision=lax.Precision.HIGHEST, preferred_element_type=F32
    )
    out[...] = picked.reshape(out.shape)


def tile_parts(width_y):
    return [(lo, min(lo + LANES, width_y)) for lo in range(0, width_y + HALO, LANES)]


def join(pieces, width_y):
    last = width_y - (len(pieces) - 1) * LANES
    return jnp.concatenate([*pieces[:-1], pieces[-1][:, :last]], axis=1)


def tile_rows(z, row, j, count, number):
    return pl.ds((z * (count + 2 * SUB) + SUB + row) * number + j, SUB, stride=number)


def spread(tiles, count, source, start, row, size):
    depth, _, width_y = source.shape
    parts = tile_parts(width_y)

    def body(i, carry):
        r = i * SUB
        for z in range(depth):
            for j, (lo, hi) in enumerate(parts):
                if hi > lo:
                    value = source[z, pl.ds(pl.multiple_of(r + start, SUB), SUB), lo:hi]
                    if hi - lo < LANES:
                        value = jnp.pad(value, ((0, 0), (0, LANES - (hi - lo))))
                else:
                    value = jnp.zeros((SUB, LANES), F32)
                tiles[tile_rows(z, r + row, j, count, len(parts)), :] = value
        return carry

    lax.fori_loop(0, size // SUB, body, 0)


def clear(tiles, count, depth, number, row):
    for z in range(depth):
        for j in range(number):
            tiles[tile_rows(z, row, j, count, number), :] = jnp.zeros((SUB, LANES), F32)


def band(width_y):
    number = len(tile_parts(width_y))
    spot = np.arange(number * LANES)
    away = np.abs(spot[:, None] - spot[None, :])
    inside = (spot[:, None] < width_y) & (spot[None, :] < width_y)
    whole = np.zeros(away.shape, np.float32)
    for k in range(1, HALO + 1):
        whole[(away == k) & inside] = W[k]
    out = []
    for w in range(number - 1):
        part = whole[w * LANES : (w + 2) * LANES, w * LANES : (w + 2) * LANES].copy()
        if w:
            part[:LANES, :LANES] = 0.0
        high = part.astype(BF16)
        out.append([high, (part - high.astype(np.float32)).astype(BF16)])
    return np.array(out)


def halve(high, low, source, start, count):
    depth, _, width_y = source.shape
    extra = high.shape[1] - width_y

    def body(r):
        for z in range(depth):
            value = source[z, pl.ds(pl.multiple_of(r + start, SUB), ROWS), :]
            value = jnp.pad(value, ((0, 0), (0, extra)))
            top = value.astype(BF16)
            into = pl.ds(pl.multiple_of(r + z * count, ROWS), ROWS)
            high[into, :] = top
            low[into, :] = (value - top.astype(F32)).astype(BF16)

    row_loop(count, body)


def add_lanes(high, low, weights, lap):
    lines = high.shape[0]
    size = lines // 2

    def product(x, y):
        return jnp.dot(x, y, preferred_element_type=F32)

    def step(i, carry):
        rows = pl.ds(pl.multiple_of(i * size, ROWS), size)
        for w in range(weights.shape[0]):
            window = slice(w * LANES, (w + 2) * LANES)
            x, y = high[rows, window], low[rows, window]
            total = product(x, weights[w, 0]) + product(y, weights[w, 0])
            total = total + product(x, weights[w, 1])
            for q in range(2):
                into = pl.ds(pl.multiple_of(i * size + (w + q) * lines, ROWS), size)
                lap[into, :] = lap[into, :] + total[:, q * LANES : (q + 1) * LANES]
        return carry

    lax.fori_loop(0, 2, step, 0)


def add_rows(tiles, lap, depth, count, number):
    groups = count // SUB
    unroll = max(u for u in range(1, UNROLL + 1) if groups % u == 0)

    def one(r):
        def at(z, j, shift=0):
            return tiles[tile_rows(z, r + shift, j, count, number), :]

        centre = [[at(z, j) for j in range(number)] for z in range(depth)]
        for z in range(depth):
            for j in range(number):
                place = pl.ds(pl.multiple_of(r + (j * depth + z) * count, SUB), SUB)
                total = lap[place, :] + 3.0 * W[0] * centre[z][j]
                for k in range(1, HALO + 1):
                    pair = at(z, j, -k) + at(z, j, k)
                    if z - k >= 0:
                        pair = pair + centre[z - k][j]
                    if z + k < depth:
                        pair = pair + centre[z + k][j]
                    total = total + W[k] * pair
                lap[place, :] = total

    def step(i, carry):
        for u in range(unroll):
            one((i * unroll + u) * SUB)
        return carry

    lax.fori_loop(0, groups // unroll, step, 0)


def blank(lap):
    def body(i, carry):
        lap[pl.ds(pl.multiple_of(i * 8 * SUB, SUB), 8 * SUB), :] = jnp.zeros((8 * SUB, LANES), F32)
        return carry

    whole = lap.shape[0] // (8 * SUB)
    lax.fori_loop(0, whole, body, 0)
    rest = lap.shape[0] - whole * 8 * SUB
    lap[whole * 8 * SUB :, :] = jnp.zeros((rest, LANES), F32)


def inject(step, got, lap, planes, first, count, width_x):
    lane = lax.broadcasted_iota(jnp.int32, (1, LANES), 1)
    span = row_span(width_x)
    shift = LANES.bit_length() - 1

    def body(i, carry):
        for slot in range(CAP):
            source = got[i, 0, step * CAP + slot]
            code = got[i, 0, STEPS * CAP + slot].astype(jnp.int32)
            line = lax.shift_right_logical(code, jnp.int32(shift))
            row = (line & (span - 1)) - first
            plane = lax.shift_right_logical(line, jnp.int32(span.bit_length() - 1))
            inside = (row >= 0) & (row < count)
            place = pl.ds(jnp.where(inside, plane * count + row, planes * count), 1)
            lap[place, :] = lap[place, :] + jnp.where(lane == (code & (LANES - 1)), source, 0.0)
        return carry

    lax.fori_loop(0, got.shape[0], body, 0)


def lap_rows(lap, z, r, depth, count, width_y):
    pieces = []
    for j in range(-(-width_y // LANES)):
        place = pl.multiple_of((j * depth + z) * count + r, ROWS)
        pieces.append(lap[pl.ds(place, ROWS), :])
    return join(pieces, width_y)


def halo_sum(got_on, rows_on, got_off, rows_off, width_y, depth):
    near = decode(take(got_on, rows_on, width_y))
    far = decode(take(got_off, rows_off, width_y))
    out = []
    for j in range(depth):
        terms = [near[j]] if j < HALO else []
        if depth - 1 - j < HALO:
            terms.append(far[depth - 1 - j])
        out.append(functools.reduce(lambda a, b: a + b, terms) if terms else None)
    return out


def prepare(step, first, count, width_x, depth, width_y, got, tiles, lap):
    number = len(tile_parts(width_y))
    blank(lap)
    if first == 0:
        clear(tiles, count, depth, number, -SUB)
    if first + count == width_x:
        clear(tiles, count, depth, number, count)
    inject(step, got, lap, number * depth, first, count, width_x)


def first_kernel(first, width_x, pieces, now, prior, velocity, lanes, got, got_on, *refs):
    faces, refs = refs[: len(pieces)], refs[len(pieces) :]
    part, on_ref, off_ref, held, speed = refs[:5]
    tiles, lap, high_buf, low_buf, prior_buf, sems, band_sem = refs[-7:]
    depth, count, width_y = part.shape
    low, high = max(first - SUB, 0), min(first + count + SUB, width_x)
    now_copies = fetch(now, held, sems.at[0], low, high - low)
    keep_band = len(refs) > 12
    if keep_band:
        weights = pltpu.make_async_copy(lanes, refs[5], band_sem)
        weights.start()
    copies = fetch(prior, prior_buf, sems.at[1], first, count)
    copies += fetch(velocity, speed, sems.at[2], first, count)
    prepare(0, first, count, width_x, depth, width_y, got, tiles, lap)
    for copy, (row, size) in zip(now_copies, blocks_of(low, high - low)):
        copy.wait()
        spread(tiles, count, held, row - low, row - first, size)
    halve(high_buf, low_buf, held, first - low, count)
    if keep_band:
        weights.wait()
    add_lanes(high_buf, low_buf, refs[5] if keep_band else lanes, lap)
    add_rows(tiles, lap, depth, count, len(tile_parts(width_y)))
    for copy in copies:
        copy.wait()

    for got_off, (start, size) in zip(faces, pieces):
        row, end = max(first, start), min(first + count, start + size)

        def body(r):
            r = r + (row - first)
            rows = pl.ds(r, ROWS)
            here = pl.ds(pl.multiple_of(r + (first - low), SUB), ROWS)
            there = pl.ds(r + (first - start), ROWS)
            halo = halo_sum(got_on, pl.ds(r + first, ROWS), got_off, there, width_y, depth)
            u = []
            for j in range(depth):
                z = depth_at(j, depth)
                change = lap_rows(lap, z, r, depth, count, width_y)
                if halo[j] is not None:
                    change = change + halo[j]
                value = 2.0 * held[z, here, :] - prior_buf[z, rows, :]
                value = value + speed[z, rows, :] * change
                part[z, rows, :] = value
                u.append(value)
            put(off_ref, rows, encode(u[::-1][:HALO]))
            put(on_ref, rows, encode(u[:HALO]))

        row_loop(end - row, body)


def second_local(first, starts, parts, width_x, lanes, got, stencil):
    tiles, lap, high_buf, low_buf = stencil
    here = parts[starts.index(first)]
    depth, count, width_y = here.shape
    low, high = max(first - SUB, 0), min(first + count + SUB, width_x)
    prepare(1, first, count, width_x, depth, width_y, got, tiles, lap)
    for start, part in zip(starts, parts):
        row, end = max(low, start), min(high, start + part.shape[1])
        spread(tiles, count, part, row - start, row - first, end - row)
    halve(high_buf, low_buf, here, 0, count)
    add_lanes(high_buf, low_buf, lanes, lap)
    add_rows(tiles, lap, depth, count, len(tile_parts(width_y)))
    return here


def send_rows(pairs, first, row, sems, n):
    writes = []
    for k, (buf, target) in enumerate(pairs):
        write = pltpu.make_async_copy(
            buf.at[:, pl.ds(row, BLOCK)], target.at[:, pl.ds(first + row, BLOCK)], sems.at[k, n]
        )
        write.start()
        writes.append(write)
    return writes


def second_kernel(first, starts, *refs):
    parts, refs = refs[: len(starts)], refs[len(starts) :]
    held, speed, forward, lanes, got, got_on, got_off, out, image = refs[:9]
    stencil = refs[9:13]
    out_buf, image_buf, out_sems = refs[13:]
    lap = stencil[1]
    depth, width_x, width_y = out.shape
    count = out_buf.shape[1]
    back = first - max(first - SUB, 0)
    writes = []
    here = second_local(first, starts, parts, width_x, lanes, got, stencil)
    for n, i in enumerate(range(0, count, BLOCK)):

        def body(r):
            r = r + i
            rows = pl.ds(r, ROWS)
            whole = pl.ds(r + first, ROWS)
            before = pl.ds(pl.multiple_of(r + back, SUB), ROWS)
            halo = halo_sum(got_on, rows, got_off, rows, width_y, depth)
            for j in range(depth):
                z = depth_at(j, depth)
                change = lap_rows(lap, z, r, depth, count, width_y)
                if halo[j] is not None:
                    change = change + halo[j]
                mine = here[z, rows, :]
                value = 2.0 * mine - held[z, before, :] + speed[z, rows, :] * change
                out_buf[z, rows, :] = value
                image_buf[z, rows, :] = forward[0, z, whole, :] * mine + forward[1, z, whole, :] * value

        row_loop(BLOCK, body)
        writes += send_rows(((out_buf, out), (image_buf, image)), first, i, out_sems, n)
    for write in writes:
        write.wait()


def partial_kernel(first, starts, *refs):
    parts, refs = refs[: len(starts)], refs[len(starts) :]
    held, speed, forward, lanes, got, current, out, image = refs[:8]
    stencil, sems = refs[8:12], refs[12]
    lap = stencil[1]
    width_x = current.shape[1]
    depth, count, width_y = out.shape
    back = first - max(first - SUB, 0)
    writes = []
    for i, (start, part) in enumerate(zip(starts, parts)):
        write = pltpu.make_async_copy(part, current.at[:, pl.ds(start, part.shape[1])], sems.at[i])
        write.start()
        writes.append(write)
    here = second_local(first, starts, parts, width_x, lanes, got, stencil)

    def body(r):
        rows = pl.ds(r, ROWS)
        whole = pl.ds(r + first, ROWS)
        before = pl.ds(pl.multiple_of(r + back, SUB), ROWS)
        for z in range(depth):
            change = lap_rows(lap, z, r, depth, count, width_y)
            mine = here[z, rows, :]
            value = 2.0 * mine - held[z, before, :] + speed[z, rows, :] * change
            out[z, rows, :] = value
            image[z, rows, :] = forward[0, z, whole, :] * mine + forward[1, z, whole, :] * value

    row_loop(count, body)
    for write in writes:
        write.wait()


def last_kernel(first, partial, image_in, speed, forward, got_on, got_off, *refs):
    out, image, out_buf, image_buf, sems = refs[-5:]
    depth, count, width_y = out_buf.shape
    writes = []
    for n, i in enumerate(range(0, count, BLOCK)):

        def body(r):
            rows = pl.ds(r + i, ROWS)
            whole = pl.ds(r + (first + i), ROWS)
            halo = halo_sum(got_on, rows, got_off, rows, width_y, depth)
            for j in range(depth):
                z = depth_at(j, depth)
                extra = speed[z, rows, :] * halo[j] if halo[j] is not None else 0.0
                out_buf[z, rows, :] = partial[z, rows, :] + extra
                image_buf[z, rows, :] = image_in[z, rows, :] + forward[1, z, whole, :] * extra

        row_loop(BLOCK, body)
        writes += send_rows(((out_buf, out), (image_buf, image)), first, i, sems, n)
    for write in writes:
        write.wait()


def cut(width_x, share):
    return width_x * share[0] // (sum(share) * BLOCK) * BLOCK


def shard(now, prior, velocity, forward, traces, weights, target, cell):
    now, prior, velocity = (
        pltpu.with_memory_space_constraint(x, pltpu.HBM) for x in (now, prior, velocity)
    )
    slabs = lax.axis_size("slab")
    depth, width_x, width_y = now.shape
    lanes = pltpu.with_memory_space_constraint(jnp.asarray(band(width_y)), pltpu.HBM)
    rows = traces.shape[0]
    face_lanes = payload_lanes(width_y)
    split = cut(width_x, SHARE)
    early_chunks = ((0, split), (split, width_x - split))
    chunks = ((0, cut(width_x, LATER)), (cut(width_x, LATER), width_x - cut(width_x, LATER)))
    starts = tuple(first for first, _ in chunks)
    field = jax.ShapeDtypeStruct(now.shape, F32)
    number = len(tile_parts(width_y))
    dma = pltpu.SemaphoreType.DMA
    on_pairs = [(k, k ^ 1) for k in range(slabs) if k ^ 1 < slabs]
    off_pairs = [(i + 1, j + 1) for i, j in on_pairs if i + 1 < slabs and j + 1 < slabs]

    def plane(count):
        return jax.ShapeDtypeStruct((count, face_lanes), BF16)

    def rows_of(count):
        return jax.ShapeDtypeStruct((depth, count, width_y), F32)

    def buffer(count):
        return pltpu.VMEM((depth, count, width_y), F32)

    def stencil(count):
        tiles = pltpu.VMEM((number * depth * (count + 2 * SUB), LANES), F32)
        lap = pltpu.VMEM((number * depth * count + SUB, LANES), F32)
        half = pltpu.VMEM((depth * count, number * LANES), BF16)
        return (tiles, lap, half, half)

    def blocks(count):
        return -(-count // BLOCK)

    def call(kernel, ins, outs, scratch=(), out_spec=None, **kw):
        return pl.pallas_call(
            kernel,
            in_specs=ins,
            out_specs=out_spec or [VMEM] * len(outs),
            out_shape=outs,
            scratch_shapes=scratch,
            compiler_params=params(),
            **kw,
        )

    def swap(face, pairs):
        return lax.ppermute(face, "slab", pairs)

    got_off = []
    (face,) = call(
        functools.partial(pack_kernel, 0, False),
        [HBM],
        [plane(split)],
        (buffer(split), dma((blocks(split),))),
    )(now)
    got_off.append(swap(face, off_pairs))
    face, traces = lax.optimization_barrier((face, traces))
    (sent,) = call(
        functools.partial(route_kernel, slabs, now.shape),
        [VMEM] * 4,
        [jax.ShapeDtypeStruct((slabs, 1, LANES), F32)],
    )(traces, weights, target.reshape(1, rows), cell.reshape(1, rows))
    got = lax.all_to_all(sent, "slab", split_axis=0, concat_axis=0, tiled=True)
    sent, later = lax.optimization_barrier((sent, now))
    on_face, face = call(
        functools.partial(pack_kernel, split, True),
        [HBM],
        [plane(width_x), plane(width_x - split)],
        (buffer(width_x), dma((blocks(width_x),))),
    )(later)
    got_off.append(swap(face, off_pairs))
    got_on = swap(on_face, on_pairs)
    parts, held, speed, second_on, second_off = [], [], [], [], []
    for i, (first, count) in enumerate(chunks):
        pieces, faces = [], []
        for piece, face in zip(early_chunks, got_off):
            if piece[0] < first + count and first < sum(piece):
                pieces.append(piece)
                faces.append(face)
        near = min(first + count + SUB, width_x) - max(first - SUB, 0)
        keep = [] if i else [jax.ShapeDtypeStruct(lanes.shape, BF16)]
        part, on_face, face, rows_held, rows_speed, *kept = call(
            functools.partial(first_kernel, first, width_x, tuple(pieces)),
            [HBM] * 3 + [VMEM if i else HBM, SMEM] + [VMEM] * (1 + len(faces)),
            [rows_of(count), plane(count), plane(count), rows_of(near), rows_of(count)] + keep,
            (*stencil(count), buffer(count), dma((3, blocks(near))), dma),
        )(now, prior, velocity, lanes, got, got_on, *faces)
        lanes = kept[0] if kept else lanes
        second_off.append(swap(face, off_pairs))
        second_on.append(swap(on_face, on_pairs))
        parts.append(part)
        held.append(rows_held)
        speed.append(rows_speed)
    parts[-1], forward = lax.optimization_barrier((parts[-1], forward))
    (first, count), (last, size) = chunks
    current, partial, image_part = call(
        functools.partial(partial_kernel, last, starts),
        [VMEM] * (len(parts) + 4) + [SMEM],
        [field, rows_of(size), rows_of(size)],
        (*stencil(size), dma((len(parts),))),
        [HBM, VMEM, VMEM],
    )(*parts, held[1], speed[1], forward, lanes, got)
    second, image = call(
        functools.partial(second_kernel, first, starts),
        [VMEM] * (len(parts) + 4) + [SMEM, VMEM, VMEM],
        [field, field],
        (*stencil(count), buffer(count), buffer(count), dma((2, blocks(count)))),
        [HBM] * 2,
    )(*parts, held[0], speed[0], forward, lanes, got, second_on[0], second_off[0])
    second, image = call(
        functools.partial(last_kernel, last),
        [VMEM] * 6 + [HBM] * 2,
        [field, field],
        (buffer(size), buffer(size), dma((2, blocks(size)))),
        [HBM] * 2,
        input_output_aliases={6: 0, 7: 1},
    )(partial, image_part, speed[1], forward, second_on[1], second_off[1], second, image)
    return (image, second, current)


def solution(mesh):
    split = P(("groups", "slab"), None, None)
    return jax.shard_map(
        shard,
        mesh=mesh,
        in_specs=(
            split,
            split,
            split,
            P(None, ("groups", "slab"), None, None),
            P(("groups", "slab"), None),
            P(),
            P(("groups", "slab"), None),
            P(("groups", "slab")),
        ),
        out_specs=(split, split, split),
        check_vma=False,
    )
```

```python
import functools

import jax
import jax.numpy as jnp
import numpy as np
from jax import lax
from jax.experimental import pallas as pl
from jax.experimental.pallas import tpu as pltpu
from jax.sharding import PartitionSpec as P


CAP = 4
STEPS = 2
W = (-205.0 / 72.0, 8.0 / 5.0, -1.0 / 5.0, 8.0 / 315.0, -1.0 / 560.0)
HALO = 4
ROWS = 16
BLOCK = 32
SUB = 8
UNROLL = 4
SHARE = (3, 2)
LATER = (1, 1)
LANES = 128
F32 = jnp.float32
BF16 = jnp.bfloat16
VMEM = pl.BlockSpec(memory_space=pltpu.VMEM)
SMEM = pl.BlockSpec(memory_space=pltpu.SMEM)
HBM = pl.BlockSpec(memory_space=pltpu.HBM)


def params():
    return pltpu.CompilerParams(vmem_limit_bytes=20 << 20)


def payload_lanes(width):
    full = width // LANES * LANES
    rest = width - full
    if rest == 0:
        return HALO * full
    return HALO * full + (2 * LANES if rest * 2 <= LANES else HALO * LANES)


def depth_at(j, depth):
    odd = lax.rem(lax.axis_index("slab"), 2)
    return j + (1 - odd) * (depth - 1 - 2 * j)


def encode(u):
    t1 = u[0].astype(BF16).astype(F32)
    e1 = u[0] - t1
    t2 = (u[1] + (W[2] / W[3]) * e1).astype(BF16).astype(F32)
    t3 = u[2].astype(BF16).astype(F32)
    t0 = W[1] * e1 + W[2] * (u[1] - t2) + W[3] * (u[2] - t3) + W[4] * u[3]
    return (t0, t1, t2, t3)


def decode(t):
    t0, t1, t2, t3 = t
    return (
        t0 + W[1] * t1 + W[2] * t2 + W[3] * t3,
        W[2] * t1 + W[3] * t2 + W[4] * t3,
        W[3] * t1 + W[4] * t2,
        W[4] * t1,
    )


def put(ref, rows, t):
    width = t[0].shape[1]
    full = width // LANES * LANES
    rest = width - full
    for k in range(HALO):
        ref[rows, k * full : (k + 1) * full] = t[k][:, :full].astype(BF16)
    if rest == 0:
        return
    base = HALO * full
    if rest * 2 <= LANES:
        half = LANES // 2
        for k in range(0, HALO, 2):
            a = jnp.pad(t[k][:, full:], ((0, 0), (0, half - rest)))
            b = jnp.pad(t[k + 1][:, full:], ((0, 0), (0, half - rest)))
            ref[rows, base : base + LANES] = jnp.concatenate([a, b], axis=1).astype(BF16)
            base += LANES
    else:
        for k in range(HALO):
            tail = jnp.pad(t[k][:, full:], ((0, 0), (0, LANES - rest)))
            ref[rows, base : base + LANES] = tail.astype(BF16)
            base += LANES


def take(ref, rows, width):
    full = width // LANES * LANES
    rest = width - full
    main = [ref[rows, k * full : (k + 1) * full].astype(F32) for k in range(HALO)]
    if rest == 0:
        return main
    base = HALO * full
    tails = []
    if rest * 2 <= LANES:
        half = LANES // 2
        for _ in range(0, HALO, 2):
            both = ref[rows, base : base + LANES].astype(F32)
            tails.append(both[:, :rest])
            tails.append(pltpu.roll(both, half, 1)[:, :rest])
            base += LANES
    else:
        for _ in range(HALO):
            tails.append(ref[rows, base : base + LANES].astype(F32)[:, :rest])
            base += LANES
    return [jnp.concatenate([m, t], axis=1) for m, t in zip(main, tails)]


def row_loop(count, body):
    def step(i, carry):
        body(pl.multiple_of(i * ROWS, ROWS))
        return carry

    lax.fori_loop(0, count // ROWS, step, 0)


def row_span(width_x):
    return 1 << (width_x - 1).bit_length()


def blocks_of(first, count):
    return [(i, min(BLOCK, first + count - i)) for i in range(first, first + count, BLOCK)]


def fetch(source, buf, sems, first, count):
    copies = []
    for n, (row, size) in enumerate(blocks_of(first, count)):
        rows = pl.ds(row, size)
        copies.append(
            pltpu.make_async_copy(source.at[:, rows], buf.at[:, pl.ds(row - first, size)], sems.at[n])
        )
        copies[-1].start()
    return copies


def pack_rows(first, with_on, copies, buf, base, on_ref, off_ref):
    depth, count, _ = buf.shape
    for copy, (row, size) in zip(copies, blocks_of(0, count)):
        copy.wait()

        def body(r):
            r = r + row
            rows = pl.ds(r, ROWS)
            u = [buf[depth_at(j, depth), rows, :] for j in range(depth)]
            if base + row >= first and base + row < first + off_ref.shape[0]:
                put(off_ref, pl.ds(r + (base - first), ROWS), encode(u[::-1][:HALO]))
            if with_on:
                put(on_ref, rows, encode(u[:HALO]))

        row_loop(size, body)


def pack_kernel(first, now, off_ref, buf, sems):
    copies = fetch(now, buf, sems, first, buf.shape[1])
    pack_rows(first, False, copies, buf, first, None, off_ref)


def route_kernel(slabs, field, traces, weights, target, cell, out):
    depth, width_x, width_y = field
    rows = traces.shape[0]
    lane = lax.broadcasted_iota(jnp.int32, (rows, rows), 1)
    row = lax.broadcasted_iota(jnp.int32, (rows, rows), 0)
    eye = lane == row
    target_row = jnp.broadcast_to(target[...], (rows, rows))
    cell_row = jnp.broadcast_to(cell[...], (rows, rows))
    target_col = jnp.sum(jnp.where(eye, target_row, 0), axis=1, keepdims=True)
    cell_col = jnp.sum(jnp.where(eye, cell_row, 0), axis=1, keepdims=True)
    same = (target_row == target_col) & (lane < row)
    rank = jnp.sum(jnp.where(same, 1, 0), axis=1, keepdims=True)
    values = traces[...].astype(F32)
    columns = [
        jnp.sum(values * weights[s : s + 1, :].astype(F32), axis=1, keepdims=True)
        for s in range(STEPS)
    ]
    line = cell_col // width_y
    layer = line // width_x
    column = cell_col - line * width_y
    plane = (column // LANES) * depth + layer
    code = (plane * row_span(width_x) + line - layer * width_x) * LANES + column % LANES
    columns.append(code.astype(F32))
    spot = lax.broadcasted_iota(jnp.int32, (rows, LANES), 1)
    spread = jnp.zeros((rows, LANES), F32)
    for j, column in enumerate(columns):
        spread = jnp.where(spot == j * CAP + rank, column, spread)
    taker = lax.broadcasted_iota(jnp.int32, (slabs, rows), 0)
    chosen = (taker == jnp.broadcast_to(target[...], (slabs, rows))).astype(F32)
    picked = jnp.dot(
        chosen, spread, precision=lax.Precision.HIGHEST, preferred_element_type=F32
    )
    out[...] = picked.reshape(out.shape)


def route_pack_kernel(
    slabs, first, traces, weights, target, cell, now, out, on_ref, off_ref, buf, sems
):
    copies = fetch(now, buf, sems, 0, now.shape[1])
    route_kernel(slabs, now.shape, traces, weights, target, cell, out)
    pack_rows(first, True, copies, buf, 0, on_ref, off_ref)


def tile_parts(width_y):
    return [(lo, min(lo + LANES, width_y)) for lo in range(0, width_y + HALO, LANES)]


def join(pieces, width_y):
    last = width_y - (len(pieces) - 1) * LANES
    return jnp.concatenate([*pieces[:-1], pieces[-1][:, :last]], axis=1)


def tile_rows(z, row, j, count, number):
    return pl.ds((z * (count + 2 * SUB) + SUB + row) * number + j, SUB, stride=number)


def spread(tiles, count, source, start, row, size):
    depth, _, width_y = source.shape
    parts = tile_parts(width_y)

    def body(i, carry):
        r = i * SUB
        for z in range(depth):
            for j, (lo, hi) in enumerate(parts):
                if hi > lo:
                    value = source[z, pl.ds(pl.multiple_of(r + start, SUB), SUB), lo:hi]
                    if hi - lo < LANES:
                        value = jnp.pad(value, ((0, 0), (0, LANES - (hi - lo))))
                else:
                    value = jnp.zeros((SUB, LANES), F32)
                tiles[tile_rows(z, r + row, j, count, len(parts)), :] = value
        return carry

    lax.fori_loop(0, size // SUB, body, 0)


def clear(tiles, count, depth, number, row):
    for z in range(depth):
        for j in range(number):
            tiles[tile_rows(z, row, j, count, number), :] = jnp.zeros((SUB, LANES), F32)


def band(width_y):
    number = len(tile_parts(width_y))
    spot = np.arange(number * LANES)
    away = np.abs(spot[:, None] - spot[None, :])
    inside = (spot[:, None] < width_y) & (spot[None, :] < width_y)
    whole = np.zeros(away.shape, np.float32)
    for k in range(1, HALO + 1):
        whole[(away == k) & inside] = W[k]
    out = []
    for w in range(number - 1):
        part = whole[w * LANES : (w + 2) * LANES, w * LANES : (w + 2) * LANES].copy()
        if w:
            part[:LANES, :LANES] = 0.0
        high = part.astype(BF16)
        out.append([high, (part - high.astype(np.float32)).astype(BF16)])
    return np.array(out)


def halve(high, low, source, start, count):
    depth, _, width_y = source.shape
    extra = high.shape[1] - width_y

    def body(r):
        for z in range(depth):
            value = source[z, pl.ds(pl.multiple_of(r + start, SUB), ROWS), :]
            value = jnp.pad(value, ((0, 0), (0, extra)))
            top = value.astype(BF16)
            into = pl.ds(pl.multiple_of(r + z * count, ROWS), ROWS)
            high[into, :] = top
            low[into, :] = (value - top.astype(F32)).astype(BF16)

    row_loop(count, body)


def add_lanes(high, low, weights, lap):
    lines = high.shape[0]
    size = lines // 2

    def product(x, y):
        return jnp.dot(x, y, preferred_element_type=F32)

    def step(i, carry):
        rows = pl.ds(pl.multiple_of(i * size, ROWS), size)
        for w in range(weights.shape[0]):
            window = slice(w * LANES, (w + 2) * LANES)
            x, y = high[rows, window], low[rows, window]
            total = product(x, weights[w, 0]) + product(y, weights[w, 0])
            total = total + product(x, weights[w, 1])
            for q in range(2):
                into = pl.ds(pl.multiple_of(i * size + (w + q) * lines, ROWS), size)
                lap[into, :] = lap[into, :] + total[:, q * LANES : (q + 1) * LANES]
        return carry

    lax.fori_loop(0, 2, step, 0)


def add_rows(tiles, lap, depth, count, number):
    groups = count // SUB
    unroll = max(u for u in range(1, UNROLL + 1) if groups % u == 0)

    def one(r):
        def at(z, j, shift=0):
            return tiles[tile_rows(z, r + shift, j, count, number), :]

        centre = [[at(z, j) for j in range(number)] for z in range(depth)]
        for z in range(depth):
            for j in range(number):
                place = pl.ds(pl.multiple_of(r + (j * depth + z) * count, SUB), SUB)
                total = lap[place, :] + 3.0 * W[0] * centre[z][j]
                for k in range(1, HALO + 1):
                    pair = at(z, j, -k) + at(z, j, k)
                    if z - k >= 0:
                        pair = pair + centre[z - k][j]
                    if z + k < depth:
                        pair = pair + centre[z + k][j]
                    total = total + W[k] * pair
                lap[place, :] = total

    def step(i, carry):
        for u in range(unroll):
            one((i * unroll + u) * SUB)
        return carry

    lax.fori_loop(0, groups // unroll, step, 0)


def blank(lap):
    def body(i, carry):
        lap[pl.ds(pl.multiple_of(i * 8 * SUB, SUB), 8 * SUB), :] = jnp.zeros((8 * SUB, LANES), F32)
        return carry

    whole = lap.shape[0] // (8 * SUB)
    lax.fori_loop(0, whole, body, 0)
    rest = lap.shape[0] - whole * 8 * SUB
    lap[whole * 8 * SUB :, :] = jnp.zeros((rest, LANES), F32)


def inject(step, got, lap, planes, first, count, width_x):
    lane = lax.broadcasted_iota(jnp.int32, (1, LANES), 1)
    span = row_span(width_x)
    shift = LANES.bit_length() - 1

    def body(i, carry):
        for slot in range(CAP):
            source = got[i, 0, step * CAP + slot]
            code = got[i, 0, STEPS * CAP + slot].astype(jnp.int32)
            line = lax.shift_right_logical(code, jnp.int32(shift))
            row = (line & (span - 1)) - first
            plane = lax.shift_right_logical(line, jnp.int32(span.bit_length() - 1))
            inside = (row >= 0) & (row < count)
            place = pl.ds(jnp.where(inside, plane * count + row, planes * count), 1)
            lap[place, :] = lap[place, :] + jnp.where(lane == (code & (LANES - 1)), source, 0.0)
        return carry

    lax.fori_loop(0, got.shape[0], body, 0)


def lap_rows(lap, z, r, depth, count, width_y):
    pieces = []
    for j in range(-(-width_y // LANES)):
        place = pl.multiple_of((j * depth + z) * count + r, ROWS)
        pieces.append(lap[pl.ds(place, ROWS), :])
    return join(pieces, width_y)


def halo_sum(got_on, rows_on, got_off, rows_off, width_y, depth):
    near = decode(take(got_on, rows_on, width_y))
    far = decode(take(got_off, rows_off, width_y))
    out = []
    for j in range(depth):
        terms = [near[j]] if j < HALO else []
        if depth - 1 - j < HALO:
            terms.append(far[depth - 1 - j])
        out.append(functools.reduce(lambda a, b: a + b, terms) if terms else None)
    return out


def prepare(step, first, count, width_x, depth, width_y, got, tiles, lap):
    number = len(tile_parts(width_y))
    blank(lap)
    if first == 0:
        clear(tiles, count, depth, number, -SUB)
    if first + count == width_x:
        clear(tiles, count, depth, number, count)
    inject(step, got, lap, number * depth, first, count, width_x)


def first_kernel(first, width_x, pieces, now, prior, velocity, lanes, got, got_on, *refs):
    faces, refs = refs[: len(pieces)], refs[len(pieces) :]
    part, on_ref, off_ref, held, speed = refs[:5]
    tiles, lap, high_buf, low_buf, prior_buf, sems, band_sem = refs[-7:]
    depth, count, width_y = part.shape
    low, high = max(first - SUB, 0), min(first + count + SUB, width_x)
    now_copies = fetch(now, held, sems.at[0], low, high - low)
    keep_band = len(refs) > 12
    if keep_band:
        weights = pltpu.make_async_copy(lanes, refs[5], band_sem)
        weights.start()
    copies = fetch(prior, prior_buf, sems.at[1], first, count)
    copies += fetch(velocity, speed, sems.at[2], first, count)
    prepare(0, first, count, width_x, depth, width_y, got, tiles, lap)
    for copy, (row, size) in zip(now_copies, blocks_of(low, high - low)):
        copy.wait()
        spread(tiles, count, held, row - low, row - first, size)
    halve(high_buf, low_buf, held, first - low, count)
    if keep_band:
        weights.wait()
    add_lanes(high_buf, low_buf, refs[5] if keep_band else lanes, lap)
    add_rows(tiles, lap, depth, count, len(tile_parts(width_y)))
    for copy in copies:
        copy.wait()

    for got_off, (start, size) in zip(faces, pieces):
        row, end = max(first, start), min(first + count, start + size)

        def body(r):
            r = r + (row - first)
            rows = pl.ds(r, ROWS)
            here = pl.ds(pl.multiple_of(r + (first - low), SUB), ROWS)
            there = pl.ds(r + (first - start), ROWS)
            halo = halo_sum(got_on, pl.ds(r + first, ROWS), got_off, there, width_y, depth)
            u = []
            for j in range(depth):
                z = depth_at(j, depth)
                change = lap_rows(lap, z, r, depth, count, width_y)
                if halo[j] is not None:
                    change = change + halo[j]
                value = 2.0 * held[z, here, :] - prior_buf[z, rows, :]
                value = value + speed[z, rows, :] * change
                part[z, rows, :] = value
                u.append(value)
            put(off_ref, rows, encode(u[::-1][:HALO]))
            put(on_ref, rows, encode(u[:HALO]))

        row_loop(end - row, body)


def second_local(first, starts, parts, width_x, lanes, got, stencil):
    tiles, lap, high_buf, low_buf = stencil
    here = parts[starts.index(first)]
    depth, count, width_y = here.shape
    low, high = max(first - SUB, 0), min(first + count + SUB, width_x)
    prepare(1, first, count, width_x, depth, width_y, got, tiles, lap)
    for start, part in zip(starts, parts):
        row, end = max(low, start), min(high, start + part.shape[1])
        spread(tiles, count, part, row - start, row - first, end - row)
    halve(high_buf, low_buf, here, 0, count)
    add_lanes(high_buf, low_buf, lanes, lap)
    add_rows(tiles, lap, depth, count, len(tile_parts(width_y)))
    return here


def send_rows(pairs, first, row, sems, n):
    writes = []
    for k, (buf, target) in enumerate(pairs):
        write = pltpu.make_async_copy(
            buf.at[:, pl.ds(row, BLOCK)], target.at[:, pl.ds(first + row, BLOCK)], sems.at[k, n]
        )
        write.start()
        writes.append(write)
    return writes


def second_kernel(first, starts, *refs):
    parts, refs = refs[: len(starts)], refs[len(starts) :]
    held, speed, forward, lanes, got, got_on, got_off, out, image = refs[:9]
    stencil = refs[9:13]
    out_buf, image_buf, out_sems = refs[13:]
    lap = stencil[1]
    depth, width_x, width_y = out.shape
    count = out_buf.shape[1]
    back = first - max(first - SUB, 0)
    writes = []
    here = second_local(first, starts, parts, width_x, lanes, got, stencil)
    for n, i in enumerate(range(0, count, BLOCK)):

        def body(r):
            r = r + i
            rows = pl.ds(r, ROWS)
            whole = pl.ds(r + first, ROWS)
            before = pl.ds(pl.multiple_of(r + back, SUB), ROWS)
            halo = halo_sum(got_on, rows, got_off, rows, width_y, depth)
            for j in range(depth):
                z = depth_at(j, depth)
                change = lap_rows(lap, z, r, depth, count, width_y)
                if halo[j] is not None:
                    change = change + halo[j]
                mine = here[z, rows, :]
                value = 2.0 * mine - held[z, before, :] + speed[z, rows, :] * change
                out_buf[z, rows, :] = value
                image_buf[z, rows, :] = forward[0, z, whole, :] * mine + forward[1, z, whole, :] * value

        row_loop(BLOCK, body)
        writes += send_rows(((out_buf, out), (image_buf, image)), first, i, out_sems, n)
    for write in writes:
        write.wait()


def partial_kernel(first, starts, *refs):
    parts, refs = refs[: len(starts)], refs[len(starts) :]
    held, speed, forward, lanes, got, current, out, image = refs[:8]
    stencil, sems = refs[8:12], refs[12]
    lap = stencil[1]
    width_x = current.shape[1]
    depth, count, width_y = out.shape
    back = first - max(first - SUB, 0)
    writes = []
    for i, (start, part) in enumerate(zip(starts, parts)):
        write = pltpu.make_async_copy(part, current.at[:, pl.ds(start, part.shape[1])], sems.at[i])
        write.start()
        writes.append(write)
    here = second_local(first, starts, parts, width_x, lanes, got, stencil)

    def body(r):
        rows = pl.ds(r, ROWS)
        whole = pl.ds(r + first, ROWS)
        before = pl.ds(pl.multiple_of(r + back, SUB), ROWS)
        for z in range(depth):
            change = lap_rows(lap, z, r, depth, count, width_y)
            mine = here[z, rows, :]
            value = 2.0 * mine - held[z, before, :] + speed[z, rows, :] * change
            out[z, rows, :] = value
            image[z, rows, :] = forward[0, z, whole, :] * mine + forward[1, z, whole, :] * value

    row_loop(count, body)
    for write in writes:
        write.wait()


def last_kernel(first, partial, image_in, speed, forward, got_on, got_off, *refs):
    out, image, out_buf, image_buf, sems = refs[-5:]
    depth, count, width_y = out_buf.shape
    writes = []
    for n, i in enumerate(range(0, count, BLOCK)):

        def body(r):
            rows = pl.ds(r + i, ROWS)
            whole = pl.ds(r + (first + i), ROWS)
            halo = halo_sum(got_on, rows, got_off, rows, width_y, depth)
            for j in range(depth):
                z = depth_at(j, depth)
                extra = speed[z, rows, :] * halo[j] if halo[j] is not None else 0.0
                out_buf[z, rows, :] = partial[z, rows, :] + extra
                image_buf[z, rows, :] = image_in[z, rows, :] + forward[1, z, whole, :] * extra

        row_loop(BLOCK, body)
        writes += send_rows(((out_buf, out), (image_buf, image)), first, i, sems, n)
    for write in writes:
        write.wait()


def cut(width_x, share):
    return width_x * share[0] // (sum(share) * BLOCK) * BLOCK


def shard(now, prior, velocity, forward, traces, weights, target, cell):
    now, prior, velocity = (
        pltpu.with_memory_space_constraint(x, pltpu.HBM) for x in (now, prior, velocity)
    )
    slabs = lax.axis_size("slab")
    depth, width_x, width_y = now.shape
    lanes = pltpu.with_memory_space_constraint(jnp.asarray(band(width_y)), pltpu.HBM)
    rows = traces.shape[0]
    face_lanes = payload_lanes(width_y)
    split = cut(width_x, SHARE)
    early_chunks = ((0, split), (split, width_x - split))
    chunks = ((0, cut(width_x, LATER)), (cut(width_x, LATER), width_x - cut(width_x, LATER)))
    starts = tuple(first for first, _ in chunks)
    field = jax.ShapeDtypeStruct(now.shape, F32)
    number = len(tile_parts(width_y))
    dma = pltpu.SemaphoreType.DMA
    on_pairs = [(k, k ^ 1) for k in range(slabs) if k ^ 1 < slabs]
    off_pairs = [(i + 1, j + 1) for i, j in on_pairs if i + 1 < slabs and j + 1 < slabs]

    def plane(count):
        return jax.ShapeDtypeStruct((count, face_lanes), BF16)

    def rows_of(count):
        return jax.ShapeDtypeStruct((depth, count, width_y), F32)

    def buffer(count):
        return pltpu.VMEM((depth, count, width_y), F32)

    def stencil(count):
        tiles = pltpu.VMEM((number * depth * (count + 2 * SUB), LANES), F32)
        lap = pltpu.VMEM((number * depth * count + SUB, LANES), F32)
        half = pltpu.VMEM((depth * count, number * LANES), BF16)
        return (tiles, lap, half, half)

    def blocks(count):
        return -(-count // BLOCK)

    def call(kernel, ins, outs, scratch=(), out_spec=None, **kw):
        return pl.pallas_call(
            kernel,
            in_specs=ins,
            out_specs=out_spec or [VMEM] * len(outs),
            out_shape=outs,
            scratch_shapes=scratch,
            compiler_params=params(),
            **kw,
        )

    def swap(face, pairs):
        return lax.ppermute(face, "slab", pairs)

    got_off = []
    (face,) = call(
        functools.partial(pack_kernel, 0),
        [HBM],
        [plane(split)],
        (buffer(split), dma((blocks(split),))),
    )(now)
    got_off.append(swap(face, off_pairs))
    face, traces = lax.optimization_barrier((face, traces))
    sent, on_face, face = call(
        functools.partial(route_pack_kernel, slabs, split),
        [VMEM] * 4 + [HBM],
        [
            jax.ShapeDtypeStruct((slabs, 1, LANES), F32),
            plane(width_x),
            plane(width_x - split),
        ],
        (buffer(width_x), dma((blocks(width_x),))),
    )(traces, weights, target.reshape(1, rows), cell.reshape(1, rows), now)
    got = lax.all_to_all(sent, "slab", split_axis=0, concat_axis=0, tiled=True)
    got_off.append(swap(face, off_pairs))
    got_on = swap(on_face, on_pairs)
    parts, held, speed, second_on, second_off = [], [], [], [], []
    for i, (first, count) in enumerate(chunks):
        pieces, faces = [], []
        for piece, face in zip(early_chunks, got_off):
            if piece[0] < first + count and first < sum(piece):
                pieces.append(piece)
                faces.append(face)
        near = min(first + count + SUB, width_x) - max(first - SUB, 0)
        keep = [] if i else [jax.ShapeDtypeStruct(lanes.shape, BF16)]
        part, on_face, face, rows_held, rows_speed, *kept = call(
            functools.partial(first_kernel, first, width_x, tuple(pieces)),
            [HBM] * 3 + [VMEM if i else HBM, SMEM] + [VMEM] * (1 + len(faces)),
            [rows_of(count), plane(count), plane(count), rows_of(near), rows_of(count)] + keep,
            (*stencil(count), buffer(count), dma((3, blocks(near))), dma),
        )(now, prior, velocity, lanes, got, got_on, *faces)
        lanes = kept[0] if kept else lanes
        second_off.append(swap(face, off_pairs))
        second_on.append(swap(on_face, on_pairs))
        parts.append(part)
        held.append(rows_held)
        speed.append(rows_speed)
    parts[-1], forward = lax.optimization_barrier((parts[-1], forward))
    (first, count), (last, size) = chunks
    current, partial, image_part = call(
        functools.partial(partial_kernel, last, starts),
        [VMEM] * (len(parts) + 4) + [SMEM],
        [field, rows_of(size), rows_of(size)],
        (*stencil(size), dma((len(parts),))),
        [HBM, VMEM, VMEM],
    )(*parts, held[1], speed[1], forward, lanes, got)
    second, image = call(
        functools.partial(second_kernel, first, starts),
        [VMEM] * (len(parts) + 4) + [SMEM, VMEM, VMEM],
        [field, field],
        (*stencil(count), buffer(count), buffer(count), dma((2, blocks(count)))),
        [HBM] * 2,
    )(*parts, held[0], speed[0], forward, lanes, got, second_on[0], second_off[0])
    second, image = call(
        functools.partial(last_kernel, last),
        [VMEM] * 6 + [HBM] * 2,
        [field, field],
        (buffer(size), buffer(size), dma((2, blocks(size)))),
        [HBM] * 2,
        input_output_aliases={6: 0, 7: 1},
    )(partial, image_part, speed[1], forward, second_on[1], second_off[1], second, image)
    return (image, second, current)


def solution(mesh):
    split = P(("groups", "slab"), None, None)
    return jax.shard_map(
        shard,
        mesh=mesh,
        in_specs=(
            split,
            split,
            split,
            P(None, ("groups", "slab"), None, None),
            P(("groups", "slab"), None),
            P(),
            P(("groups", "slab"), None),
            P(("groups", "slab")),
        ),
        out_specs=(split, split, split),
        check_vma=False,
    )
```

```python
import functools

import jax
import jax.numpy as jnp
import numpy as np
from jax import lax
from jax.experimental import pallas as pl
from jax.experimental.pallas import tpu as pltpu
from jax.sharding import PartitionSpec as P


CAP = 4
STEPS = 2
W = (-205.0 / 72.0, 8.0 / 5.0, -1.0 / 5.0, 8.0 / 315.0, -1.0 / 560.0)
HALO = 4
ROWS = 16
BLOCK = 32
SUB = 8
UNROLL = 4
SHARE = (1, 1)
LATER = (1, 1)
LANES = 128
F32 = jnp.float32
BF16 = jnp.bfloat16
VMEM = pl.BlockSpec(memory_space=pltpu.VMEM)
SMEM = pl.BlockSpec(memory_space=pltpu.SMEM)
HBM = pl.BlockSpec(memory_space=pltpu.HBM)


def params():
    return pltpu.CompilerParams(vmem_limit_bytes=20 << 20)


def payload_lanes(width):
    full = width // LANES * LANES
    rest = width - full
    if rest == 0:
        return HALO * full
    return HALO * full + (2 * LANES if rest * 2 <= LANES else HALO * LANES)


def depth_at(j, depth):
    odd = lax.rem(lax.axis_index("slab"), 2)
    return j + (1 - odd) * (depth - 1 - 2 * j)


def encode(u):
    t1 = u[0].astype(BF16).astype(F32)
    e1 = u[0] - t1
    t2 = (u[1] + (W[2] / W[3]) * e1).astype(BF16).astype(F32)
    t3 = u[2].astype(BF16).astype(F32)
    t0 = W[1] * e1 + W[2] * (u[1] - t2) + W[3] * (u[2] - t3) + W[4] * u[3]
    return (t0, t1, t2, t3)


def decode(t):
    t0, t1, t2, t3 = t
    return (
        t0 + W[1] * t1 + W[2] * t2 + W[3] * t3,
        W[2] * t1 + W[3] * t2 + W[4] * t3,
        W[3] * t1 + W[4] * t2,
        W[4] * t1,
    )


def put(ref, rows, t):
    width = t[0].shape[1]
    full = width // LANES * LANES
    rest = width - full
    for k in range(HALO):
        ref[rows, k * full : (k + 1) * full] = t[k][:, :full].astype(BF16)
    if rest == 0:
        return
    base = HALO * full
    if rest * 2 <= LANES:
        half = LANES // 2
        for k in range(0, HALO, 2):
            a = jnp.pad(t[k][:, full:], ((0, 0), (0, half - rest)))
            b = jnp.pad(t[k + 1][:, full:], ((0, 0), (0, half - rest)))
            ref[rows, base : base + LANES] = jnp.concatenate([a, b], axis=1).astype(BF16)
            base += LANES
    else:
        for k in range(HALO):
            tail = jnp.pad(t[k][:, full:], ((0, 0), (0, LANES - rest)))
            ref[rows, base : base + LANES] = tail.astype(BF16)
            base += LANES


def take(ref, rows, width):
    full = width // LANES * LANES
    rest = width - full
    main = [ref[rows, k * full : (k + 1) * full].astype(F32) for k in range(HALO)]
    if rest == 0:
        return main
    base = HALO * full
    tails = []
    if rest * 2 <= LANES:
        half = LANES // 2
        for _ in range(0, HALO, 2):
            both = ref[rows, base : base + LANES].astype(F32)
            tails.append(both[:, :rest])
            tails.append(pltpu.roll(both, half, 1)[:, :rest])
            base += LANES
    else:
        for _ in range(HALO):
            tails.append(ref[rows, base : base + LANES].astype(F32)[:, :rest])
            base += LANES
    return [jnp.concatenate([m, t], axis=1) for m, t in zip(main, tails)]


def row_loop(count, body):
    def step(i, carry):
        body(pl.multiple_of(i * ROWS, ROWS))
        return carry

    lax.fori_loop(0, count // ROWS, step, 0)


def row_span(width_x):
    return 1 << (width_x - 1).bit_length()


def blocks_of(first, count):
    return [(i, min(BLOCK, first + count - i)) for i in range(first, first + count, BLOCK)]


def fetch(source, buf, sems, first, count):
    copies = []
    for n, (row, size) in enumerate(blocks_of(first, count)):
        rows = pl.ds(row, size)
        copies.append(
            pltpu.make_async_copy(source.at[:, rows], buf.at[:, pl.ds(row - first, size)], sems.at[n])
        )
        copies[-1].start()
    return copies


def pack_kernel(first, now, on_ref, off_ref, buf, sems):
    depth, count, _ = buf.shape
    copies = fetch(now, buf, sems, first, count)
    for copy, (row, size) in zip(copies, blocks_of(0, count)):
        copy.wait()

        def body(r):
            rows = pl.ds(r + row, ROWS)
            u = [buf[depth_at(j, depth), rows, :] for j in range(depth)]
            put(off_ref, rows, encode(u[::-1][:HALO]))
            put(on_ref, rows, encode(u[:HALO]))

        row_loop(size, body)


def route_kernel(slabs, field, traces, weights, target, cell, out):
    depth, width_x, width_y = field
    rows = traces.shape[0]
    lane = lax.broadcasted_iota(jnp.int32, (rows, rows), 1)
    row = lax.broadcasted_iota(jnp.int32, (rows, rows), 0)
    eye = lane == row
    target_row = jnp.broadcast_to(target[...], (rows, rows))
    cell_row = jnp.broadcast_to(cell[...], (rows, rows))
    target_col = jnp.sum(jnp.where(eye, target_row, 0), axis=1, keepdims=True)
    cell_col = jnp.sum(jnp.where(eye, cell_row, 0), axis=1, keepdims=True)
    same = (target_row == target_col) & (lane < row)
    rank = jnp.sum(jnp.where(same, 1, 0), axis=1, keepdims=True)
    values = traces[...].astype(F32)
    columns = [
        jnp.sum(values * weights[s : s + 1, :].astype(F32), axis=1, keepdims=True)
        for s in range(STEPS)
    ]
    line = cell_col // width_y
    layer = line // width_x
    column = cell_col - line * width_y
    plane = (column // LANES) * depth + layer
    code = (plane * row_span(width_x) + line - layer * width_x) * LANES + column % LANES
    columns.append(code.astype(F32))
    spot = lax.broadcasted_iota(jnp.int32, (rows, LANES), 1)
    spread = jnp.zeros((rows, LANES), F32)
    for j, column in enumerate(columns):
        spread = jnp.where(spot == j * CAP + rank, column, spread)
    taker = lax.broadcasted_iota(jnp.int32, (slabs, rows), 0)
    chosen = (taker == jnp.broadcast_to(target[...], (slabs, rows))).astype(F32)
    picked = jnp.dot(
        chosen, spread, precision=lax.Precision.HIGHEST, preferred_element_type=F32
    )
    out[...] = picked.reshape(out.shape)


def tile_parts(width_y):
    return [(lo, min(lo + LANES, width_y)) for lo in range(0, width_y + HALO, LANES)]


def join(pieces, width_y):
    last = width_y - (len(pieces) - 1) * LANES
    return jnp.concatenate([*pieces[:-1], pieces[-1][:, :last]], axis=1)


def tile_rows(z, row, j, count, number):
    return pl.ds((z * (count + 2 * SUB) + SUB + row) * number + j, SUB, stride=number)


def spread(tiles, count, source, start, row, size):
    depth, _, width_y = source.shape
    parts = tile_parts(width_y)

    def body(i, carry):
        r = i * SUB
        for z in range(depth):
            for j, (lo, hi) in enumerate(parts):
                if hi > lo:
                    value = source[z, pl.ds(pl.multiple_of(r + start, SUB), SUB), lo:hi]
                    if hi - lo < LANES:
                        value = jnp.pad(value, ((0, 0), (0, LANES - (hi - lo))))
                else:
                    value = jnp.zeros((SUB, LANES), F32)
                tiles[tile_rows(z, r + row, j, count, len(parts)), :] = value
        return carry

    lax.fori_loop(0, size // SUB, body, 0)


def clear(tiles, count, depth, number, row):
    for z in range(depth):
        for j in range(number):
            tiles[tile_rows(z, row, j, count, number), :] = jnp.zeros((SUB, LANES), F32)


def band():
    spot = np.arange(2 * LANES)
    away = np.abs(spot[:, None] - spot[None, :])
    whole = np.zeros(away.shape, np.float32)
    for k in range(1, HALO + 1):
        whole[away == k] = W[k]
    high = whole.astype(BF16)
    return np.stack([high, (whole - high.astype(np.float32)).astype(BF16)])


def halve(high, low, source, start, count):
    depth, _, width_y = source.shape
    extra = high.shape[1] - width_y

    def body(r):
        for z in range(depth):
            value = source[z, pl.ds(pl.multiple_of(r + start, SUB), ROWS), :]
            value = jnp.pad(value, ((0, 0), (0, extra)))
            top = value.astype(BF16)
            into = pl.ds(pl.multiple_of(r + z * count, ROWS), ROWS)
            high[into, :] = top
            low[into, :] = (value - top.astype(F32)).astype(BF16)

    row_loop(count, body)


def add_lanes(high, low, weights, lap):
    lines, lanes = high.shape
    number = lanes // LANES
    size = lines // 2
    first_half = lax.broadcasted_iota(jnp.int32, (size, LANES), 1) < LANES // 2

    def product(x, y):
        return jnp.dot(x, y, preferred_element_type=F32)

    def step(i, carry):
        rows = pl.ds(pl.multiple_of(i * size, ROWS), size)
        left = None
        for w in range(number - 1):
            window = slice(w * LANES, (w + 2) * LANES)
            x, y = high[rows, window], low[rows, window]
            total = product(x, weights[0]) + product(y, weights[0]) + product(x, weights[1])
            tile = total[:, :LANES]
            if left is not None:
                tile = jnp.where(first_half, left, tile)
            left = total[:, LANES:]
            into = pl.ds(pl.multiple_of(i * size + w * lines, ROWS), size)
            lap[into, :] = lap[into, :] + tile
        into = pl.ds(pl.multiple_of(i * size + (number - 1) * lines, ROWS), size)
        lap[into, :] = lap[into, :] + left
        return carry

    lax.fori_loop(0, 2, step, 0)


def add_rows(tiles, lap, depth, count, number):
    groups = count // SUB
    unroll = max(u for u in range(1, UNROLL + 1) if groups % u == 0)

    def one(r):
        def at(z, j, shift=0):
            return tiles[tile_rows(z, r + shift, j, count, number), :]

        centre = [[at(z, j) for j in range(number)] for z in range(depth)]
        for z in range(depth):
            for j in range(number):
                place = pl.ds(pl.multiple_of(r + (j * depth + z) * count, SUB), SUB)
                total = lap[place, :] + 3.0 * W[0] * centre[z][j]
                for k in range(1, HALO + 1):
                    pair = at(z, j, -k) + at(z, j, k)
                    if z - k >= 0:
                        pair = pair + centre[z - k][j]
                    if z + k < depth:
                        pair = pair + centre[z + k][j]
                    total = total + W[k] * pair
                lap[place, :] = total

    def step(i, carry):
        for u in range(unroll):
            one((i * unroll + u) * SUB)
        return carry

    lax.fori_loop(0, groups // unroll, step, 0)


def blank(lap):
    def body(i, carry):
        lap[pl.ds(pl.multiple_of(i * 8 * SUB, SUB), 8 * SUB), :] = jnp.zeros((8 * SUB, LANES), F32)
        return carry

    whole = lap.shape[0] // (8 * SUB)
    lax.fori_loop(0, whole, body, 0)
    rest = lap.shape[0] - whole * 8 * SUB
    lap[whole * 8 * SUB :, :] = jnp.zeros((rest, LANES), F32)


def inject(step, got, lap, planes, first, count, width_x):
    lane = lax.broadcasted_iota(jnp.int32, (1, LANES), 1)
    span = row_span(width_x)
    shift = LANES.bit_length() - 1

    def body(i, carry):
        for slot in range(CAP):
            source = got[i, 0, step * CAP + slot]
            code = got[i, 0, STEPS * CAP + slot].astype(jnp.int32)
            line = lax.shift_right_logical(code, jnp.int32(shift))
            row = (line & (span - 1)) - first
            plane = lax.shift_right_logical(line, jnp.int32(span.bit_length() - 1))
            inside = (row >= 0) & (row < count)
            place = pl.ds(jnp.where(inside, plane * count + row, planes * count), 1)
            lap[place, :] = lap[place, :] + jnp.where(lane == (code & (LANES - 1)), source, 0.0)
        return carry

    lax.fori_loop(0, got.shape[0], body, 0)


def lap_rows(lap, z, r, depth, count, width_y):
    pieces = []
    for j in range(-(-width_y // LANES)):
        place = pl.multiple_of((j * depth + z) * count + r, ROWS)
        pieces.append(lap[pl.ds(place, ROWS), :])
    return join(pieces, width_y)


def halo_sum(got_on, rows_on, got_off, rows_off, width_y, depth):
    near = decode(take(got_on, rows_on, width_y))
    far = decode(take(got_off, rows_off, width_y))
    out = []
    for j in range(depth):
        terms = [near[j]] if j < HALO else []
        if depth - 1 - j < HALO:
            terms.append(far[depth - 1 - j])
        out.append(functools.reduce(lambda a, b: a + b, terms) if terms else None)
    return out


def prepare(step, first, count, width_x, depth, width_y, got, tiles, lap):
    number = len(tile_parts(width_y))
    blank(lap)
    if first == 0:
        clear(tiles, count, depth, number, -SUB)
    if first + count == width_x:
        clear(tiles, count, depth, number, count)
    inject(step, got, lap, number * depth, first, count, width_x)


def first_kernel(first, width_x, pieces, now, prior, velocity, lanes, got, *refs):
    faces, refs = refs[: 2 * len(pieces)], refs[2 * len(pieces) :]
    part, on_ref, off_ref, held, speed = refs[:5]
    tiles, lap, high_buf, low_buf, prior_buf, sems = refs[5:]
    depth, count, width_y = part.shape
    low, high = max(first - SUB, 0), min(first + count + SUB, width_x)
    now_copies = fetch(now, held, sems.at[0], low, high - low)
    copies = fetch(prior, prior_buf, sems.at[1], first, count)
    copies += fetch(velocity, speed, sems.at[2], first, count)
    prepare(0, first, count, width_x, depth, width_y, got, tiles, lap)
    for copy, (row, size) in zip(now_copies, blocks_of(low, high - low)):
        copy.wait()
        spread(tiles, count, held, row - low, row - first, size)
    halve(high_buf, low_buf, held, first - low, count)
    add_lanes(high_buf, low_buf, lanes, lap)
    add_rows(tiles, lap, depth, count, len(tile_parts(width_y)))
    for copy in copies:
        copy.wait()

    for got_on, got_off, (start, size) in zip(faces[::2], faces[1::2], pieces):
        row, end = max(first, start), min(first + count, start + size)

        def body(r):
            r = r + (row - first)
            rows = pl.ds(r, ROWS)
            here = pl.ds(pl.multiple_of(r + (first - low), SUB), ROWS)
            there = pl.ds(r + (first - start), ROWS)
            halo = halo_sum(got_on, there, got_off, there, width_y, depth)
            u = []
            for j in range(depth):
                z = depth_at(j, depth)
                change = lap_rows(lap, z, r, depth, count, width_y)
                if halo[j] is not None:
                    change = change + halo[j]
                value = 2.0 * held[z, here, :] - prior_buf[z, rows, :]
                value = value + speed[z, rows, :] * change
                part[z, rows, :] = value
                u.append(value)
            put(off_ref, rows, encode(u[::-1][:HALO]))
            put(on_ref, rows, encode(u[:HALO]))

        row_loop(end - row, body)


def second_local(first, starts, parts, width_x, lanes, got, stencil):
    tiles, lap, high_buf, low_buf = stencil
    here = parts[starts.index(first)]
    depth, count, width_y = here.shape
    low, high = max(first - SUB, 0), min(first + count + SUB, width_x)
    prepare(1, first, count, width_x, depth, width_y, got, tiles, lap)
    for start, part in zip(starts, parts):
        row, end = max(low, start), min(high, start + part.shape[1])
        spread(tiles, count, part, row - start, row - first, end - row)
    halve(high_buf, low_buf, here, 0, count)
    add_lanes(high_buf, low_buf, lanes, lap)
    add_rows(tiles, lap, depth, count, len(tile_parts(width_y)))
    return here


def send_rows(pairs, first, row, sems, n):
    writes = []
    for k, (buf, target) in enumerate(pairs):
        write = pltpu.make_async_copy(
            buf.at[:, pl.ds(row, BLOCK)], target.at[:, pl.ds(first + row, BLOCK)], sems.at[k, n]
        )
        write.start()
        writes.append(write)
    return writes


def second_kernel(first, starts, *refs):
    parts, refs = refs[: len(starts)], refs[len(starts) :]
    held, speed, forward, lanes, got, got_on, got_off, out, image = refs[:9]
    stencil = refs[9:13]
    out_buf, image_buf, out_sems = refs[13:]
    lap = stencil[1]
    depth, width_x, width_y = out.shape
    count = out_buf.shape[1]
    back = first - max(first - SUB, 0)
    writes = []
    here = second_local(first, starts, parts, width_x, lanes, got, stencil)
    for n, i in enumerate(range(0, count, BLOCK)):

        def body(r):
            r = r + i
            rows = pl.ds(r, ROWS)
            whole = pl.ds(r + first, ROWS)
            before = pl.ds(pl.multiple_of(r + back, SUB), ROWS)
            halo = halo_sum(got_on, rows, got_off, rows, width_y, depth)
            for j in range(depth):
                z = depth_at(j, depth)
                change = lap_rows(lap, z, r, depth, count, width_y)
                if halo[j] is not None:
                    change = change + halo[j]
                mine = here[z, rows, :]
                value = 2.0 * mine - held[z, before, :] + speed[z, rows, :] * change
                out_buf[z, rows, :] = value
                image_buf[z, rows, :] = forward[0, z, whole, :] * mine + forward[1, z, whole, :] * value

        row_loop(BLOCK, body)
        writes += send_rows(((out_buf, out), (image_buf, image)), first, i, out_sems, n)
    for write in writes:
        write.wait()


def partial_kernel(first, starts, *refs):
    parts, refs = refs[: len(starts)], refs[len(starts) :]
    held, speed, forward, lanes, got, current, out, image = refs[:8]
    stencil, sems = refs[8:12], refs[12]
    lap = stencil[1]
    width_x = current.shape[1]
    depth, count, width_y = out.shape
    back = first - max(first - SUB, 0)
    writes = []
    for i, (start, part) in enumerate(zip(starts, parts)):
        write = pltpu.make_async_copy(part, current.at[:, pl.ds(start, part.shape[1])], sems.at[i])
        write.start()
        writes.append(write)
    here = second_local(first, starts, parts, width_x, lanes, got, stencil)

    def body(r):
        rows = pl.ds(r, ROWS)
        whole = pl.ds(r + first, ROWS)
        before = pl.ds(pl.multiple_of(r + back, SUB), ROWS)
        for z in range(depth):
            change = lap_rows(lap, z, r, depth, count, width_y)
            mine = here[z, rows, :]
            value = 2.0 * mine - held[z, before, :] + speed[z, rows, :] * change
            out[z, rows, :] = value
            image[z, rows, :] = forward[0, z, whole, :] * mine + forward[1, z, whole, :] * value

    row_loop(count, body)
    for write in writes:
        write.wait()


def last_kernel(first, partial, image_in, speed, forward, got_on, got_off, *refs):
    out, image, out_buf, image_buf, sems = refs[-5:]
    depth, count, width_y = out_buf.shape
    writes = []
    for n, i in enumerate(range(0, count, BLOCK)):

        def body(r):
            rows = pl.ds(r + i, ROWS)
            whole = pl.ds(r + (first + i), ROWS)
            halo = halo_sum(got_on, rows, got_off, rows, width_y, depth)
            for j in range(depth):
                z = depth_at(j, depth)
                extra = speed[z, rows, :] * halo[j] if halo[j] is not None else 0.0
                out_buf[z, rows, :] = partial[z, rows, :] + extra
                image_buf[z, rows, :] = image_in[z, rows, :] + forward[1, z, whole, :] * extra

        row_loop(BLOCK, body)
        writes += send_rows(((out_buf, out), (image_buf, image)), first, i, sems, n)
    for write in writes:
        write.wait()


def cut(width_x, share):
    return width_x * share[0] // (sum(share) * BLOCK) * BLOCK


def shard(now, prior, velocity, forward, traces, weights, target, cell):
    now, prior, velocity = (
        pltpu.with_memory_space_constraint(x, pltpu.HBM) for x in (now, prior, velocity)
    )
    slabs = lax.axis_size("slab")
    depth, width_x, width_y = now.shape
    lanes = jnp.asarray(band())
    rows = traces.shape[0]
    face_lanes = payload_lanes(width_y)
    split = cut(width_x, SHARE)
    early_chunks = ((0, split), (split, width_x - split))
    chunks = ((0, cut(width_x, LATER)), (cut(width_x, LATER), width_x - cut(width_x, LATER)))
    starts = tuple(first for first, _ in chunks)
    field = jax.ShapeDtypeStruct(now.shape, F32)
    number = len(tile_parts(width_y))
    dma = pltpu.SemaphoreType.DMA
    on_pairs = [(k, k ^ 1) for k in range(slabs) if k ^ 1 < slabs]
    off_pairs = [(i + 1, j + 1) for i, j in on_pairs if i + 1 < slabs and j + 1 < slabs]

    def plane(count):
        return jax.ShapeDtypeStruct((count, face_lanes), BF16)

    def rows_of(count):
        return jax.ShapeDtypeStruct((depth, count, width_y), F32)

    def buffer(count):
        return pltpu.VMEM((depth, count, width_y), F32)

    def stencil(count):
        tiles = pltpu.VMEM((number * depth * (count + 2 * SUB) + 4 * SUB, LANES), F32)
        lap = pltpu.VMEM((number * depth * count + SUB, LANES), F32)
        half = pltpu.VMEM((depth * count, number * LANES), BF16)
        return (tiles, lap, half, half)

    def blocks(count):
        return -(-count // BLOCK)

    def call(kernel, ins, outs, scratch=(), out_spec=None, **kw):
        return pl.pallas_call(
            kernel,
            in_specs=ins,
            out_specs=out_spec or [VMEM] * len(outs),
            out_shape=outs,
            scratch_shapes=scratch,
            compiler_params=params(),
            **kw,
        )

    def swap(face, pairs):
        return lax.ppermute(face, "slab", pairs)

    early = []

    def pack(field, first, count):
        return call(
            functools.partial(pack_kernel, first),
            [HBM],
            [plane(count), plane(count)],
            (buffer(count), dma((blocks(count),))),
        )(field)

    on_face, face = pack(now, *early_chunks[0])
    early.append((swap(on_face, on_pairs), swap(face, off_pairs)))
    face, traces = lax.optimization_barrier((face, traces))
    (sent,) = call(
        functools.partial(route_kernel, slabs, now.shape),
        [VMEM] * 4,
        [jax.ShapeDtypeStruct((slabs, 1, LANES), F32)],
    )(traces, weights, target.reshape(1, rows), cell.reshape(1, rows))
    got = lax.all_to_all(sent, "slab", split_axis=0, concat_axis=0, tiled=True)
    sent, later = lax.optimization_barrier((sent, now))
    on_face, face = pack(later, *early_chunks[1])
    early.append((swap(on_face, on_pairs), swap(face, off_pairs)))
    parts, held, speed, second_on, second_off = [], [], [], [], []
    for first, count in chunks:
        pieces, faces = [], []
        for piece, both in zip(early_chunks, early):
            if piece[0] < first + count and first < sum(piece):
                pieces.append(piece)
                faces.extend(both)
        near = min(first + count + SUB, width_x) - max(first - SUB, 0)
        part, on_face, face, rows_held, rows_speed = call(
            functools.partial(first_kernel, first, width_x, tuple(pieces)),
            [HBM] * 3 + [VMEM, SMEM] + [VMEM] * len(faces),
            [rows_of(count), plane(count), plane(count), rows_of(near), rows_of(count)],
            (*stencil(count), buffer(count), dma((3, blocks(near)))),
        )(now, prior, velocity, lanes, got, *faces)
        second_off.append(swap(face, off_pairs))
        second_on.append(swap(on_face, on_pairs))
        parts.append(part)
        held.append(rows_held)
        speed.append(rows_speed)
    parts[-1], forward = lax.optimization_barrier((parts[-1], forward))
    (first, count), (last, size) = chunks
    current, partial, image_part = call(
        functools.partial(partial_kernel, last, starts),
        [VMEM] * (len(parts) + 4) + [SMEM],
        [field, rows_of(size), rows_of(size)],
        (*stencil(size), dma((len(parts),))),
        [HBM, VMEM, VMEM],
    )(*parts, held[1], speed[1], forward, lanes, got)
    second, image = call(
        functools.partial(second_kernel, first, starts),
        [VMEM] * (len(parts) + 4) + [SMEM, VMEM, VMEM],
        [field, field],
        (*stencil(count), buffer(count), buffer(count), dma((2, blocks(count)))),
        [HBM] * 2,
    )(*parts, held[0], speed[0], forward, lanes, got, second_on[0], second_off[0])
    second, image = call(
        functools.partial(last_kernel, last),
        [VMEM] * 6 + [HBM] * 2,
        [field, field],
        (buffer(size), buffer(size), dma((2, blocks(size)))),
        [HBM] * 2,
        input_output_aliases={6: 0, 7: 1},
    )(partial, image_part, speed[1], forward, second_on[1], second_off[1], second, image)
    return (image, second, current)


def solution(mesh):
    split = P(("groups", "slab"), None, None)
    return jax.shard_map(
        shard,
        mesh=mesh,
        in_specs=(
            split,
            split,
            split,
            P(None, ("groups", "slab"), None, None),
            P(("groups", "slab"), None),
            P(),
            P(("groups", "slab"), None),
            P(("groups", "slab")),
        ),
        out_specs=(split, split, split),
        check_vma=False,
    )
```
